512 devices in a mesh: gz: 32 (over z, core), gy: 16 (over y, x).
Axes of the slice: x: 4, y: 4, z: 16, core: 2. Of those that a mesh axis runs over, the one named last changes fastest.
Arguments:
- excess_warmth: float32 [512, 128, 128], P('gz', 'gy'), may hold values from -0.2 to 0.3
- conversion_degree: float32 [512, 128, 128], P('gz', 'gy'), may hold values from 0 to 0.9
- substance_label: int32 [512, 128, 128], P('gz', 'gy'), may hold values from 0 to 2
Outputs:
- temperature_out: float32 [512, 128, 128], P('gz', 'gy')
- cure_out: float32 [512, 128, 128], P('gz', 'gy')
The draws below stay inside these ranges and needn't reach their ends.
Inputs may be any that keep to these rules, and one draw needn't show every extreme that they name: `substance_label`: material holds 0 for propellant, 1 for mandrel, 2 for case.
All inputs are finite; a program needn't handle non-finite values.
Results may differ from the reference program's by a relative error of at most 0.0003.
Values sent between devices are 32-bit elements; how exact they have to be, the bound alone decides.
No kernel may reach another device: no remote copies, remote signals or barrier semaphores. Data moves between devices by JAX's collectives and lax.ppermute only.
A program may use at most 64 MiB of HBM per device.

```python
import jax
import jax.numpy as jnp
from jax import lax

GRID_WIDTH_EAST = 128
STEPS = 2
GRID_WIDTH_UPWARD = 512
GRID_WIDTH_NORTH = 128


def with_ends(values, key, least, largest):
    shape = values.shape
    spot = [jax.random.randint(jax.random.fold_in(key, axis), (), 0, shape[axis]) for axis in range(len(shape))]
    values = values.at[tuple(spot)].set(least)
    longest = shape.index(max(shape))
    spot[longest] = (spot[longest] + 1) % shape[longest]
    return values.at[tuple(spot)].set(largest)


def level_of(rng, extent, cuts, least, high):
    level, own = 1.0, jax.random.fold_in(rng, 6)
    for position, blocks in cuts:
        steps = jnp.exp(jax.random.uniform(jax.random.fold_in(own, position), (blocks,), jnp.float32, least / len(cuts), high / len(cuts)))
        level = level * jnp.repeat(steps, extent[position] // blocks).reshape([-1 if axis == position else 1 for axis in range(len(extent))])
    return level


def setup_inputs(seed: int = 0) -> dict:
    key_list = jax.random.split(jax.random.key(seed), 4)
    return {
        "excess_warmth": jnp.clip(-0.2 + 0.5 * jax.random.uniform(key_list[0], (GRID_WIDTH_UPWARD, GRID_WIDTH_NORTH, GRID_WIDTH_EAST), jnp.float32) ** level_of(key_list[0], (GRID_WIDTH_UPWARD, GRID_WIDTH_NORTH, GRID_WIDTH_EAST), ((0, 32), (1, 16)), -0.2, 0.2), -0.2, 0.3),
        "conversion_degree": jnp.clip(0.9 * jax.random.uniform(key_list[1], (GRID_WIDTH_UPWARD, GRID_WIDTH_NORTH, GRID_WIDTH_EAST), jnp.float32) ** level_of(key_list[1], (GRID_WIDTH_UPWARD, GRID_WIDTH_NORTH, GRID_WIDTH_EAST), ((0, 32), (1, 16)), -0.2, 0.2), 0.0, 0.9),
        "substance_label": with_ends(jax.random.randint(key_list[2], (GRID_WIDTH_UPWARD, GRID_WIDTH_NORTH, GRID_WIDTH_EAST), 0, 3), jax.random.fold_in(key_list[2], 1), 0, 2).astype(jnp.int32),
    }


courant_number = 120.0
implicit_share = 0.5
mandrel_conduct = 40.0
case_conduct = 20.0
grain_conduct = 0.6
cured_conduct = 0.8
mandrel_capacity = 3.0
case_capacity = 2.0
kinetic_prefactor = 0.3
arrhenius_barrier = 8.0
exothermic_release = 0.4


def material_state(substance_label, conversion_degree):
    is_mandrel = (substance_label == 1).astype(conversion_degree.dtype)
    is_case = (substance_label == 2).astype(conversion_degree.dtype)
    is_grain = (substance_label == 0).astype(conversion_degree.dtype)
    conductivity_coefficient = is_mandrel * mandrel_conduct + is_case * case_conduct + is_grain * (grain_conduct + cured_conduct * conversion_degree)
    specific_warmth = 1.0 + is_mandrel * (mandrel_capacity - 1.0) + is_case * (case_capacity - 1.0)
    return conductivity_coefficient, specific_warmth


def hardened_share(substance_label, excess_warmth, conversion_degree):
    conversion_speed = kinetic_prefactor * jnp.exp(arrhenius_barrier * excess_warmth)
    advanced = 1.0 - (1.0 - conversion_degree) * jnp.exp(-conversion_speed)
    return jnp.where(substance_label == 0, advanced, conversion_degree)


def band_set(conductivity_coefficient, specific_warmth, k_prev, k_next):
    upper_boundary = 0.5 * (conductivity_coefficient + k_next)
    lower_boundary = 0.5 * (conductivity_coefficient + k_prev)
    weight = implicit_share * courant_number / specific_warmth
    lower_band = -weight * lower_boundary
    upper_band = -weight * upper_boundary
    middle = 1.0 + weight * (upper_boundary + lower_boundary)
    return lower_band, middle, upper_band, lower_boundary, upper_boundary


def conducted_stream(excess_warmth, specific_warmth, warmth_lower_neighbour, warmth_upper_neighbour, lower_boundary, upper_boundary):
    return courant_number * (upper_boundary * (warmth_upper_neighbour - excess_warmth) - lower_boundary * (excess_warmth - warmth_lower_neighbour)) / specific_warmth


def neighbour_values(values, implicit_direction):
    widths = []
    for dim_index in range(values.ndim):
        widths.append((1, 1) if dim_index == implicit_direction else (0, 0))
    padded_field = jnp.pad(values, widths)
    length = values.shape[implicit_direction]
    return lax.slice_in_dim(padded_field, 0, length, axis=implicit_direction), lax.slice_in_dim(padded_field, 2, length + 2, axis=implicit_direction)


def thomas(lower_band, middle, upper_band, right_side, implicit_direction):
    lows = jnp.moveaxis(lower_band, implicit_direction, 0)
    mids = jnp.moveaxis(middle, implicit_direction, 0)
    ups = jnp.moveaxis(upper_band, implicit_direction, 0)
    rights = jnp.moveaxis(right_side, implicit_direction, 0)
    zero_row = jnp.zeros(mids.shape[1:], mids.dtype)

    def forward(state_pair, row_values):
        prev_ratio, prev_value = state_pair
        low_here, mid_here, up_here, right_here = row_values
        divisor = mid_here - low_here * prev_ratio
        new_ratio = up_here / divisor
        new_value = (right_here - low_here * prev_value) / divisor
        return (new_ratio, new_value), (new_ratio, new_value)

    ignored, (ratios, partial_value) = lax.scan(forward, (zero_row, zero_row), (lows, mids, ups, rights))

    def backward(next_value, row_values):
        ratio_here, value_here = row_values
        inverted_lines = value_here - ratio_here * next_value
        return inverted_lines, inverted_lines

    ignored_last, solved_all = lax.scan(backward, zero_row, (ratios, partial_value), reverse=True)
    return jnp.moveaxis(solved_all, 0, implicit_direction)


def reference(excess_warmth, conversion_degree, substance_label):
    for step_index in range(STEPS):
        conductivity_coefficient, specific_warmth = material_state(substance_label, conversion_degree)
        progressed_conversion = hardened_share(substance_label, excess_warmth, conversion_degree)
        grid_portions = []
        for implicit_direction in (2, 1, 0):
            warmth_lower_neighbour, warmth_upper_neighbour = neighbour_values(excess_warmth, implicit_direction)
            k_prev, k_next = neighbour_values(conductivity_coefficient, implicit_direction)
            lower_band, middle, upper_band, lower_boundary, upper_boundary = band_set(conductivity_coefficient, specific_warmth, k_prev, k_next)
            diagonal_entry = conducted_stream(excess_warmth, specific_warmth, warmth_lower_neighbour, warmth_upper_neighbour, lower_boundary, upper_boundary)
            grid_portions.append((diagonal_entry, lower_band, middle, upper_band))
        forward_estimate = excess_warmth + grid_portions[0][0] + grid_portions[1][0] + grid_portions[2][0] + exothermic_release * (progressed_conversion - conversion_degree)
        for line_index in range(3):
            diagonal_entry, lower_band, middle, upper_band = grid_portions[line_index]
            forward_estimate = thomas(lower_band, middle, upper_band, forward_estimate - implicit_share * diagonal_entry, 2 - line_index)
        excess_warmth = forward_estimate
        conversion_degree = progressed_conversion
    return excess_warmth, conversion_degree
```

```python
import functools

import jax
import jax.numpy as jnp
from jax import lax
from jax.experimental import pallas as pl
from jax.experimental.pallas import tpu as pltpu
from jax.sharding import PartitionSpec as P

ZC = 16
YC = 8
XC = 128
ROWS = ZC * YC

VM = pl.BlockSpec(memory_space=pltpu.VMEM)
SM = pl.BlockSpec(memory_space=pltpu.SMEM)


def f32(*shape):
    return jax.ShapeDtypeStruct(shape, jnp.float32)


def conduct_of(label, cure):
    return jnp.where(label == 1, 40.0, jnp.where(label == 2, 20.0, 0.6 + 0.8 * cure))


def store_of(label):
    return jnp.where(label == 1, 3.0 / 60.0, jnp.where(label == 2, 2.0 / 60.0, 1.0 / 60.0))


def cure_of(label, warmth, cure):
    speed = 0.3 * jnp.exp(8.0 * warmth)
    return jnp.where(label == 0, 1.0 - (1.0 - cure) * jnp.exp(-speed), cure)


def y_rows(y):
    return pl.ds(y, ZC, stride=YC)


def z_rows(z):
    return pl.ds(z * YC, YC)


def edges_kernel(t_ref, c_ref, m_ref, zlo_ref, zhi_ref, ylo_ref, yhi_ref):
    def put(out, rows):
        t, c, m = t_ref[rows, :], c_ref[rows, :], m_ref[rows, :]
        out[0] = t
        out[1] = conduct_of(m, c)
        out[2] = conduct_of(m, cure_of(m, t, c))

    put(zlo_ref, z_rows(0))
    put(zhi_ref, z_rows(ZC - 1))
    put(ylo_ref, y_rows(0))
    put(yhi_ref, y_rows(YC - 1))


def eliminate(count, store, faces, right, entry, keep):
    ground, edge, side = store(0), entry, right(0)
    back_ground = back_side = None
    for i in range(count - 1):
        face = faces(i)
        inv = 1.0 / (ground + edge + face)
        edge_inv, face_inv, side_inv = edge * inv, face * inv, side * inv
        keep(i, side_inv, edge_inv, face_inv)
        more_ground, more_side = edge_inv * ground, edge_inv * side
        back_ground = more_ground if i == 0 else back_ground + more_ground
        back_side = more_side if i == 0 else back_side + more_side
        ground = store(i + 1) + face_inv * ground
        side = right(i + 1) + face_inv * side
        edge = edge_inv * face
    return back_ground, edge, ground, side, back_side


def front_kernel(
    place_ref,
    t_ref,
    c_ref,
    m_ref,
    ztlo_ref,
    zthi_ref,
    ytlo_ref,
    ythi_ref,
    zklo_ref,
    zkhi_ref,
    yklo_ref,
    ykhi_ref,
    pay_ref,
    sub_ref,
    fluxz_ref,
    cure_ref,
    k_ref,
    g_ref,
    fy_ref,
    r_ref,
    *,
    groups,
):
    t, c, m = t_ref[...], c_ref[...], m_ref[...]
    k_ref[...] = conduct_of(m, c)
    g_ref[...] = store_of(m)
    cure_ref[...] = cure_of(m, t, c)

    ks = [yklo_ref[...]] + [k_ref[y_rows(y), :] for y in range(YC)] + [ykhi_ref[...]]
    ts = [ytlo_ref[...]] + [t_ref[y_rows(y), :] for y in range(YC)] + [ythi_ref[...]]
    face_y = [0.5 * (ks[i] + ks[i + 1]) for i in range(YC + 1)]
    flow_y = [face_y[i] * (ts[i + 1] - ts[i]) for i in range(YC + 1)]
    for y in range(YC):
        fy_ref[y_rows(y), :] = flow_y[y + 1] - flow_y[y]

    lane = lax.broadcasted_iota(jnp.int32, (YC, XC), 1)
    first_lane, last_lane = lane == 0, lane == XC - 1
    k_prev, t_prev = zklo_ref[...], ztlo_ref[...]
    flow_prev = 0.5 * (k_prev + k_ref[z_rows(0), :]) * (t_ref[z_rows(0), :] - t_prev)
    batch = 4
    for z0 in range(0, ZC, batch):
        gs, ls, rs, sides, stores = [], [], [], [], []
        for z in range(z0, z0 + batch):
            kz, tz, g = k_ref[z_rows(z), :], t_ref[z_rows(z), :], g_ref[z_rows(z), :]
            k_next = k_ref[z_rows(z + 1), :] if z + 1 < ZC else zkhi_ref[...]
            t_next = t_ref[z_rows(z + 1), :] if z + 1 < ZC else zthi_ref[...]
            flow_next = 0.5 * (kz + k_next) * (t_next - tz)
            flux_z = flow_next - flow_prev
            flow_prev = flow_next
            fluxz_ref[z_rows(z), :] = flux_z
            k_left = jnp.where(first_lane, 0.0, pltpu.roll(kz, 1, 1))
            t_left = jnp.where(first_lane, 0.0, pltpu.roll(tz, 1, 1))
            face_left = 0.5 * (kz + k_left)
            flow_left = face_left * (tz - t_left)
            face_right = jnp.where(last_lane, 0.5 * kz, pltpu.roll(face_left, XC - 1, 1))
            flow_right = jnp.where(last_lane, -face_right * tz, pltpu.roll(flow_left, XC - 1, 1))
            delta = cure_ref[z_rows(z), :] - c_ref[z_rows(z), :]
            sides.append(
                g * (tz + 0.4 * delta)
                + (flow_right - flow_left)
                + 2.0 * (fy_ref[z_rows(z), :] + flux_z)
            )
            gs.append(
                g
                + jnp.where(first_lane, face_left, 0.0)
                + jnp.where(last_lane, face_right, 0.0)
            )
            ls.append(jnp.where(first_lane, 0.0, face_left))
            rs.append(jnp.where(last_lane, 0.0, face_right))
            stores.append(g)
        stride = 1
        while stride < XC:
            for b in range(batch):
                ground, left, right, side = gs[b], ls[b], rs[b], sides[b]
                inv = 1.0 / (ground + left + right)
                ground_inv, side_inv = ground * inv, side * inv
                gs[b] = (
                    ground
                    + left * pltpu.roll(ground_inv, stride, 1)
                    + right * pltpu.roll(ground_inv, XC - stride, 1)
                )
                sides[b] = (
                    side
                    + left * pltpu.roll(side_inv, stride, 1)
                    + right * pltpu.roll(side_inv, XC - stride, 1)
                )
                ls[b] = left * pltpu.roll(left * inv, stride, 1)
                rs[b] = right * pltpu.roll(right * inv, XC - stride, 1)
            stride *= 2
        for b in range(batch):
            rows = z_rows(z0 + b)
            r_ref[rows, :] = stores[b] * (sides[b] / gs[b]) - fy_ref[rows, :]

    def keep(i, side_inv, edge_inv, face_inv):
        sub_ref[0, i] = side_inv
        sub_ref[1, i] = edge_inv
        sub_ref[2, i] = face_inv

    back_ground, edge, ground, side, back_side = eliminate(
        YC,
        lambda i: g_ref[y_rows(i), :],
        lambda i: face_y[i + 1],
        lambda i: r_ref[y_rows(i), :],
        face_y[0],
        keep,
    )
    ground = ground + jnp.where(place_ref[0] == groups - 1, face_y[YC], 0.0)
    for d in range(groups):
        pay_ref[d, 0:16] = back_ground
        pay_ref[d, 16:32] = edge
        pay_ref[d, 32:48] = ground
        pay_ref[d, 48:64] = side
        pay_ref[d, 64:80] = back_side


def chain(count, read, put):
    def ground_of(j):
        return read(j, 2) + read(j + 1, 0) if j + 1 < count else read(j, 2)

    def side_of(j):
        return read(j, 3) + read(j + 1, 4) if j + 1 < count else read(j, 3)

    half = count // 2
    gain, part = [None] * count, [None] * count
    ground_l, side_l = ground_of(0) + read(0, 1), side_of(0)
    ground_r, side_r = ground_of(count - 1), side_of(count - 1)
    for i in range(half - 1):
        edge = read(i + 1, 1)
        inv = 1.0 / (ground_l + edge)
        gain[i], part[i] = edge * inv, side_l * inv
        ground_l = ground_of(i + 1) + gain[i] * ground_l
        side_l = side_of(i + 1) + gain[i] * side_l
        j = count - 1 - i
        edge = read(j, 1)
        inv = 1.0 / (ground_r + edge)
        gain[j], part[j] = edge * inv, side_r * inv
        ground_r = ground_of(j - 1) + gain[j] * ground_r
        side_r = side_of(j - 1) + gain[j] * side_r
    edge = read(half, 1)
    inv = 1.0 / (ground_l * ground_r + edge * (ground_l + ground_r))
    low = (side_l * (ground_r + edge) + edge * side_r) * inv
    high = (side_r * (ground_l + edge) + edge * side_l) * inv
    put(half - 1, low)
    put(half, high)
    for i in range(half - 2, -1, -1):
        low = part[i] + gain[i] * low
        put(i, low)
        j = count - 1 - i
        high = part[j] + gain[j] * high
        put(j, high)


def middle_kernel(
    place_ref,
    all_ref,
    sub_ref,
    fluxz_ref,
    c_ref,
    m_ref,
    zklo_ref,
    zkhi_ref,
    pay_ref,
    subz_ref,
    entry_ref,
    s_ref,
    v_ref,
    *,
    groups_y,
    groups_z,
    copies,
):
    zero = jnp.zeros((ZC, XC), jnp.float32)
    s_ref[0] = zero

    def put(j, value):
        s_ref[j + 1] = value

    chain(groups_y, lambda j, q: all_ref[j, 16 * q : 16 * q + 16, :], put)
    me = place_ref[0]
    before, value = s_ref[me], s_ref[me + 1]
    v_ref[y_rows(YC - 1), :] = value
    for i in range(YC - 2, -1, -1):
        value = (sub_ref[0, i] + sub_ref[1, i] * before) + sub_ref[2, i] * value
        v_ref[y_rows(i), :] = value

    ks = [zklo_ref[...]]
    for z in range(ZC):
        ks.append(conduct_of(m_ref[z_rows(z), :], c_ref[z_rows(z), :]))
    ks.append(zkhi_ref[...])
    faces = [0.5 * (ks[i] + ks[i + 1]) for i in range(ZC + 1)]
    entry_ref[...] = faces[ZC]

    def keep(i, side_inv, edge_inv, face_inv):
        subz_ref[0, i] = side_inv
        subz_ref[1, i] = edge_inv
        subz_ref[2, i] = face_inv

    def right(i):
        return store_of(m_ref[z_rows(i), :]) * v_ref[z_rows(i), :] - fluxz_ref[z_rows(i), :]

    back_ground, edge, ground, side, back_side = eliminate(
        ZC,
        lambda i: store_of(m_ref[z_rows(i), :]),
        lambda i: faces[i + 1],
        right,
        faces[0],
        keep,
    )
    ground = ground + jnp.where(place_ref[1] == groups_z - 1, faces[ZC], 0.0)
    for d in range(copies):
        pay_ref[d, 0:8] = back_ground
        pay_ref[d, 8:16] = edge
        pay_ref[d, 16:24] = ground
        pay_ref[d, 24:32] = side
        pay_ref[d, 32:40] = back_side


def back_kernel(
    place_ref,
    all_ref,
    subz_ref,
    entry_ref,
    t_ref,
    ylo_ref,
    yhi_ref,
    zlo_ref,
    zhi_ref,
    s_ref,
    *,
    groups_z,
    more,
):
    s_ref[0] = jnp.zeros((YC, XC), jnp.float32)

    def put(j, value):
        s_ref[j + 1] = value

    chain(groups_z, lambda j, q: all_ref[j % 2, j // 2, 8 * q : 8 * q + 8, :], put)
    me = place_ref[1]
    before, own = s_ref[me], s_ref[me + 1]
    value = own
    t_ref[z_rows(ZC - 1), :] = value
    for i in range(ZC - 2, -1, -1):
        value = (subz_ref[0, i] + subz_ref[1, i] * before) + subz_ref[2, i] * value
        t_ref[z_rows(i), :] = value
    if more:
        ylo_ref[...] = t_ref[y_rows(0), :]
        yhi_ref[...] = t_ref[y_rows(YC - 1), :]
        zlo_ref[...] = before
        then = jnp.minimum(me + 1, groups_z - 1)
        core, chip = lax.rem(then, 2), lax.div(then, 2)
        after = s_ref[then + 1]
        back_ground = all_ref[core, chip, 0:8, :]
        edge = all_ref[core, chip, 8:16, :]
        back_side = all_ref[core, chip, 32:40, :]
        drop = (back_ground * own + edge * (own - after) - back_side) / entry_ref[...]
        zhi_ref[...] = jnp.where(me == groups_z - 1, 0.0, own - drop)


def body(warmth, cure, label):
    groups_z, groups_y = lax.axis_size("gz"), lax.axis_size("gy")
    chips = groups_z // 2
    place = jnp.stack([lax.axis_index("gy"), lax.axis_index("gz")]).astype(jnp.int32)
    up = {a: [(i, i + 1) for i in range(n - 1)] for a, n in (("gz", groups_z), ("gy", groups_y))}
    down = {a: [(j, i) for i, j in up[a]] for a in up}
    pairs = [[2 * i, 2 * i + 1] for i in range(chips)]
    same_core = [[2 * i + core for i in range(chips)] for core in range(2)]

    t = warmth.reshape(ROWS, XC)
    c = cure.reshape(ROWS, XC)
    m = label.reshape(ROWS, XC)

    zlo, zhi, ylo, yhi = pl.pallas_call(
        edges_kernel,
        out_shape=(f32(3, YC, XC), f32(3, YC, XC), f32(3, ZC, XC), f32(3, ZC, XC)),
        in_specs=[VM] * 3,
        out_specs=(VM,) * 4,
        name="edges",
    )(t, c, m)
    from_below = lax.ppermute(zhi, "gz", up["gz"])
    from_above = lax.ppermute(zlo, "gz", down["gz"])
    from_south = lax.ppermute(yhi, "gy", up["gy"])
    from_north = lax.ppermute(ylo, "gy", down["gy"])
    zt = (from_below[0], from_above[0])
    yt = (from_south[0], from_north[0])

    for step in range(2):
        zk = (from_below[1 + step], from_above[1 + step])
        yk = (from_south[1 + step], from_north[1 + step])
        pay, sub, fluxz, next_c = pl.pallas_call(
            functools.partial(front_kernel, groups=groups_y),
            out_shape=(
                f32(groups_y, 5 * ZC, XC),
                f32(3, YC - 1, ZC, XC),
                f32(ROWS, XC),
                f32(ROWS, XC),
            ),
            in_specs=[SM] + [VM] * 11,
            out_specs=(VM,) * 4,
            scratch_shapes=[pltpu.VMEM((ROWS, XC), jnp.float32)] * 4,
            name="front",
        )(place, t, c, m, *zt, *yt, *zk, *yk)
        everyone = lax.all_to_all(pay, "gy", 0, 0, tiled=True)
        payz, subz, entry = pl.pallas_call(
            functools.partial(
                middle_kernel, groups_y=groups_y, groups_z=groups_z, copies=chips
            ),
            out_shape=(f32(chips, 5 * YC, XC), f32(3, ZC - 1, YC, XC), f32(YC, XC)),
            in_specs=[SM] + [VM] * 7,
            out_specs=(VM,) * 3,
            scratch_shapes=[
                pltpu.VMEM((groups_y + 1, ZC, XC), jnp.float32),
                pltpu.VMEM((ROWS, XC), jnp.float32),
            ],
            name="middle",
        )(place, everyone, sub, fluxz, c, m, *zk)
        column = lax.all_to_all(payz, "gz", 0, 0, tiled=True, axis_index_groups=same_core)
        column = lax.all_gather(column, "gz", axis_index_groups=pairs)
        t, ylo, yhi, zlo, zhi = pl.pallas_call(
            functools.partial(back_kernel, groups_z=groups_z, more=step == 0),
            out_shape=(f32(ROWS, XC), f32(ZC, XC), f32(ZC, XC), f32(YC, XC), f32(YC, XC)),
            in_specs=[SM] + [VM] * 3,
            out_specs=(VM,) * 5,
            scratch_shapes=[pltpu.VMEM((groups_z + 1, YC, XC), jnp.float32)],
            name="back",
        )(place, column, subz, entry)
        c = next_c
        if step == 0:
            zt = (zlo, zhi)
            yt = (lax.ppermute(yhi, "gy", up["gy"]), lax.ppermute(ylo, "gy", down["gy"]))
    return t.reshape(warmth.shape), c.reshape(cure.shape)


def solution(mesh):
    return jax.shard_map(
        body,
        mesh=mesh,
        in_specs=(P("gz", "gy", None),) * 3,
        out_specs=(P("gz", "gy", None),) * 2,
        check_vma=False,
    )
```

```python
import functools

import jax
import jax.numpy as jnp
from jax import lax
from jax.experimental import pallas as pl
from jax.experimental.pallas import tpu as pltpu
from jax.sharding import PartitionSpec as P

ZC = 16
YC = 8
XC = 128
ROWS = ZC * YC


def f32(*shape):
    return jax.ShapeDtypeStruct(shape, jnp.float32)


def conduct_of(label, cure):
    return jnp.where(label == 1, 40.0, jnp.where(label == 2, 20.0, 0.6 + 0.8 * cure))


def store_of(label):
    return jnp.where(label == 1, 3.0 / 60.0, jnp.where(label == 2, 2.0 / 60.0, 1.0 / 60.0))


def cure_of(label, warmth, cure):
    speed = 0.3 * jnp.exp(8.0 * warmth)
    return jnp.where(label == 0, 1.0 - (1.0 - cure) * jnp.exp(-speed), cure)


def y_rows(y):
    return pl.ds(y, ZC, stride=YC)


def z_rows(z):
    return pl.ds(z * YC, YC)


def edges_kernel(t_ref, c_ref, m_ref, zlo_ref, zhi_ref, ylo_ref, yhi_ref):
    def put(out, rows):
        t, c, m = t_ref[rows, :], c_ref[rows, :], m_ref[rows, :]
        out[0] = t
        out[1] = conduct_of(m, c)
        out[2] = conduct_of(m, cure_of(m, t, c))

    put(zlo_ref, z_rows(0))
    put(zhi_ref, z_rows(ZC - 1))
    put(ylo_ref, y_rows(0))
    put(yhi_ref, y_rows(YC - 1))


def eliminate(count, store, faces, right, entry, keep):
    ground, edge, side = store(0), entry, right(0)
    back_ground = back_side = None
    for i in range(count - 1):
        face = faces(i)
        inv = 1.0 / (ground + edge + face)
        edge_inv, face_inv, side_inv = edge * inv, face * inv, side * inv
        keep(i, side_inv, edge_inv, face_inv)
        more_ground, more_side = edge_inv * ground, edge_inv * side
        back_ground = more_ground if i == 0 else back_ground + more_ground
        back_side = more_side if i == 0 else back_side + more_side
        ground = store(i + 1) + face_inv * ground
        side = right(i + 1) + face_inv * side
        edge = edge_inv * face
    return back_ground, edge, ground, side, back_side


def front(groups, t_ref, c_ref, m_ref, zt, yt, zk, yk, outs, scratch):
    pay_ref, sub_ref, fluxz_ref, cure_ref, entry_ref = outs
    k_ref, g_ref, fy_ref, r_ref = scratch
    t, c, m = t_ref[...], c_ref[...], m_ref[...]
    k_ref[...] = conduct_of(m, c)
    g_ref[...] = store_of(m)
    cure_ref[...] = cure_of(m, t, c)

    ks = [yk[0]] + [k_ref[y_rows(y), :] for y in range(YC)] + [yk[1]]
    ts = [yt[0]] + [t_ref[y_rows(y), :] for y in range(YC)] + [yt[1]]
    face_y = [0.5 * (ks[i] + ks[i + 1]) for i in range(YC + 1)]
    flow_y = [face_y[i] * (ts[i + 1] - ts[i]) for i in range(YC + 1)]
    for y in range(YC):
        fy_ref[y_rows(y), :] = flow_y[y + 1] - flow_y[y]
    if entry_ref is not None:
        entry_ref[...] = face_y[YC]

    lane = lax.broadcasted_iota(jnp.int32, (YC, XC), 1)
    first_lane, last_lane = lane == 0, lane == XC - 1
    k_prev, t_prev = zk[0], zt[0]
    flow_prev = 0.5 * (k_prev + k_ref[z_rows(0), :]) * (t_ref[z_rows(0), :] - t_prev)
    batch = 4
    for z0 in range(0, ZC, batch):
        gs, ls, rs, sides, stores = [], [], [], [], []
        for z in range(z0, z0 + batch):
            kz, tz, g = k_ref[z_rows(z), :], t_ref[z_rows(z), :], g_ref[z_rows(z), :]
            k_next = k_ref[z_rows(z + 1), :] if z + 1 < ZC else zk[1]
            t_next = t_ref[z_rows(z + 1), :] if z + 1 < ZC else zt[1]
            flow_next = 0.5 * (kz + k_next) * (t_next - tz)
            flux_z = flow_next - flow_prev
            flow_prev = flow_next
            fluxz_ref[z_rows(z), :] = flux_z
            k_left = jnp.where(first_lane, 0.0, pltpu.roll(kz, 1, 1))
            t_left = jnp.where(first_lane, 0.0, pltpu.roll(tz, 1, 1))
            face_left = 0.5 * (kz + k_left)
            flow_left = face_left * (tz - t_left)
            face_right = jnp.where(last_lane, 0.5 * kz, pltpu.roll(face_left, XC - 1, 1))
            flow_right = jnp.where(last_lane, -face_right * tz, pltpu.roll(flow_left, XC - 1, 1))
            delta = cure_ref[z_rows(z), :] - c_ref[z_rows(z), :]
            sides.append(
                g * (tz + 0.4 * delta)
                + (flow_right - flow_left)
                + 2.0 * (fy_ref[z_rows(z), :] + flux_z)
            )
            gs.append(
                g
                + jnp.where(first_lane, face_left, 0.0)
                + jnp.where(last_lane, face_right, 0.0)
            )
            ls.append(jnp.where(first_lane, 0.0, face_left))
            rs.append(jnp.where(last_lane, 0.0, face_right))
            stores.append(g)
        stride = 1
        while stride < XC:
            for b in range(batch):
                ground, left, right, side = gs[b], ls[b], rs[b], sides[b]
                inv = 1.0 / (ground + left + right)
                ground_inv, side_inv = ground * inv, side * inv
                gs[b] = (
                    ground
                    + left * pltpu.roll(ground_inv, stride, 1)
                    + right * pltpu.roll(ground_inv, XC - stride, 1)
                )
                sides[b] = (
                    side
                    + left * pltpu.roll(side_inv, stride, 1)
                    + right * pltpu.roll(side_inv, XC - stride, 1)
                )
                if 2 * stride < XC:
                    ls[b] = left * pltpu.roll(left * inv, stride, 1)
                    rs[b] = right * pltpu.roll(right * inv, XC - stride, 1)
            stride *= 2
        for b in range(batch):
            rows = z_rows(z0 + b)
            r_ref[rows, :] = stores[b] * (sides[b] / gs[b]) - fy_ref[rows, :]

    def keep(i, side_inv, edge_inv, face_inv):
        sub_ref[0, i] = side_inv
        sub_ref[1, i] = edge_inv
        sub_ref[2, i] = face_inv

    back_ground, edge, ground, side, back_side = eliminate(
        YC,
        lambda i: g_ref[y_rows(i), :],
        lambda i: face_y[i + 1],
        lambda i: r_ref[y_rows(i), :],
        face_y[0],
        keep,
    )
    ground = ground + jnp.where(lax.axis_index("gy") == groups - 1, face_y[YC], 0.0)
    for d in range(groups):
        pay_ref[d, 0:16] = back_ground
        pay_ref[d, 16:32] = edge
        pay_ref[d, 32:48] = ground
        pay_ref[d, 48:64] = side
        pay_ref[d, 64:80] = back_side


def front_kernel(
    t_ref,
    c_ref,
    m_ref,
    below_ref,
    above_ref,
    south_ref,
    north_ref,
    pay_ref,
    sub_ref,
    fluxz_ref,
    cure_ref,
    entry_ref,
    toward_south_ref,
    toward_north_ref,
    k_ref,
    g_ref,
    fy_ref,
    r_ref,
    *,
    groups,
):
    front(
        groups,
        t_ref,
        c_ref,
        m_ref,
        (below_ref[0], above_ref[0]),
        (south_ref[0], north_ref[0]),
        (below_ref[1], above_ref[1]),
        (south_ref[1], north_ref[1]),
        (pay_ref, sub_ref, fluxz_ref, cure_ref, entry_ref),
        (k_ref, g_ref, fy_ref, r_ref),
    )
    for out, y in ((toward_south_ref, 0), (toward_north_ref, YC - 1)):
        k = k_ref[y_rows(y), :]
        out[0:16] = fluxz_ref[y_rows(y), :]
        out[16:32] = g_ref[y_rows(y), :]
        fy_ref[8:24, :] = k
        fy_ref[7:8, :] = below_ref[1, y : y + 1, :]
        fy_ref[24:25, :] = above_ref[1, y : y + 1, :]
        out[32:48] = 0.5 * (fy_ref[7:23, :] + k)
        out[48:49] = 0.5 * (fy_ref[23:24, :] + fy_ref[24:25, :])


def chain(count, read, put):
    def ground_of(j):
        return read(j, 2) + read(j + 1, 0) if j + 1 < count else read(j, 2)

    def side_of(j):
        return read(j, 3) + read(j + 1, 4) if j + 1 < count else read(j, 3)

    half = count // 2
    gain, part = [None] * count, [None] * count
    ground_l, side_l = ground_of(0) + read(0, 1), side_of(0)
    ground_r, side_r = ground_of(count - 1), side_of(count - 1)
    for i in range(half - 1):
        edge = read(i + 1, 1)
        inv = 1.0 / (ground_l + edge)
        gain[i], part[i] = edge * inv, side_l * inv
        ground_l = ground_of(i + 1) + gain[i] * ground_l
        side_l = side_of(i + 1) + gain[i] * side_l
        j = count - 1 - i
        edge = read(j, 1)
        inv = 1.0 / (ground_r + edge)
        gain[j], part[j] = edge * inv, side_r * inv
        ground_r = ground_of(j - 1) + gain[j] * ground_r
        side_r = side_of(j - 1) + gain[j] * side_r
    edge = read(half, 1)
    inv = 1.0 / (ground_l * ground_r + edge * (ground_l + ground_r))
    low = (side_l * (ground_r + edge) + edge * side_r) * inv
    high = (side_r * (ground_l + edge) + edge * side_l) * inv
    put(half - 1, low)
    put(half, high)
    for i in range(half - 2, -1, -1):
        low = part[i] + gain[i] * low
        put(i, low)
        j = count - 1 - i
        high = part[j] + gain[j] * high
        put(j, high)


def first_of_next(own, after, back_ground, edge, back_side, entry):
    return own - (back_ground * own + edge * (own - after) - back_side) / entry


def middle_kernel(*refs, groups_y, groups_z, copies, now, wide):
    all_ref, sub_ref, fluxz_ref, c_ref, m_ref, below_ref, above_ref = refs[:7]
    refs = refs[7:]
    if wide:
        y_entry_ref, of_south_ref, of_north_ref = refs[:3]
        refs = refs[3:]
    pay_ref, subz_ref, entry_ref = refs[:3]
    refs = refs[3:]
    if wide:
        sub_wide_ref, refs = refs[0], refs[1:]
    s_ref, v_ref, p_ref = refs[:3]
    s_ref[0] = jnp.zeros((ZC, XC), jnp.float32)

    def put(j, value):
        s_ref[j + 1] = value

    chain(groups_y, lambda j, q: all_ref[j, 16 * q : 16 * q + 16, :], put)
    me = lax.axis_index("gy")
    before, own = s_ref[me], s_ref[me + 1]
    value = own
    v_ref[y_rows(YC - 1), :] = value
    for i in range(YC - 2, -1, -1):
        value = (sub_ref[0, i] + sub_ref[1, i] * before) + sub_ref[2, i] * value
        v_ref[y_rows(i), :] = value

    ks = [below_ref[now]]
    for z in range(ZC):
        ks.append(conduct_of(m_ref[z_rows(z), :], c_ref[z_rows(z), :]))
    ks.append(above_ref[now])
    faces = [0.5 * (ks[i] + ks[i + 1]) for i in range(ZC + 1)]
    entry_ref[...] = faces[ZC]

    def keep(i, side_inv, edge_inv, face_inv):
        subz_ref[0, i] = side_inv
        subz_ref[1, i] = edge_inv
        subz_ref[2, i] = face_inv

    def right(i):
        return store_of(m_ref[z_rows(i), :]) * v_ref[z_rows(i), :] - fluxz_ref[z_rows(i), :]

    at_end = lax.axis_index("gz") == groups_z - 1
    numbers = eliminate(
        ZC,
        lambda i: store_of(m_ref[z_rows(i), :]),
        lambda i: faces[i + 1],
        right,
        faces[0],
        keep,
    )
    for q, number in enumerate(numbers):
        if q == 2:
            number = number + jnp.where(at_end, faces[ZC], 0.0)
        p_ref[8 * q : 8 * q + 8] = number

    if wide:
        h_ref = refs[3]
        p_ref[48:56] = jnp.zeros((8, XC), jnp.float32)
        then = jnp.minimum(me + 1, groups_y - 1)
        after = s_ref[then + 1]
        north = first_of_next(
            own,
            after,
            all_ref[then, 0:16, :],
            all_ref[then, 16:32, :],
            all_ref[then, 64:80, :],
            y_entry_ref[...],
        )
        for side, value, of_ref in ((0, before, of_south_ref), (1, north, of_north_ref)):
            capacity = of_ref[16:32]
            rows = pl.ds(side, ZC, stride=2)
            h_ref[0, rows, :] = jnp.where(capacity > 0.0, capacity, 1.0)
            h_ref[1, rows, :] = capacity * value - of_ref[0:16]
            h_ref[2, rows, :] = of_ref[32:48]
            h_ref[2, 32 + side : 33 + side, :] = of_ref[48:49]

        def keep_wide(i, side_inv, edge_inv, face_inv):
            sub_wide_ref[0, i] = side_inv
            sub_wide_ref[1, i] = edge_inv
            sub_wide_ref[2, i] = face_inv

        numbers = eliminate(
            ZC,
            lambda i: h_ref[0, 2 * i : 2 * i + 2, :],
            lambda i: h_ref[2, 2 * i + 2 : 2 * i + 4, :],
            lambda i: h_ref[1, 2 * i : 2 * i + 2, :],
            h_ref[2, 0:2, :],
            keep_wide,
        )
        for q, number in enumerate(numbers):
            if q == 2:
                number = number + jnp.where(at_end, h_ref[2, 32:34, :], 0.0)
            p_ref[40 + 2 * q : 42 + 2 * q] = number
    for d in range(copies):
        pay_ref[d] = p_ref[...]


def back(groups_z, all_ref, subz_ref, t_ref, s_ref):
    s_ref[0] = jnp.zeros((YC, XC), jnp.float32)

    def put(j, value):
        s_ref[j + 1] = value

    chain(groups_z, lambda j, q: all_ref[j % 2, j // 2, 8 * q : 8 * q + 8, :], put)
    me = lax.axis_index("gz")
    before, own = s_ref[me], s_ref[me + 1]
    value = own
    t_ref[z_rows(ZC - 1), :] = value
    for i in range(ZC - 2, -1, -1):
        value = (subz_ref[0, i] + subz_ref[1, i] * before) + subz_ref[2, i] * value
        t_ref[z_rows(i), :] = value
    return before, own


def back_kernel(all_ref, subz_ref, t_ref, s_ref, *, groups_z):
    back(groups_z, all_ref, subz_ref, t_ref, s_ref)


def turn_kernel(
    all_ref,
    subz_ref,
    sub_wide_ref,
    z_entry_ref,
    c_ref,
    m_ref,
    below_ref,
    above_ref,
    south_ref,
    north_ref,
    pay_ref,
    sub_ref,
    fluxz_ref,
    cure_ref,
    s_ref,
    w_ref,
    t_ref,
    e_ref,
    k_ref,
    g_ref,
    fy_ref,
    r_ref,
    *,
    groups_y,
    groups_z,
):
    before, own = back(groups_z, all_ref, subz_ref, t_ref, s_ref)
    me = lax.axis_index("gz")
    then = jnp.minimum(me + 1, groups_z - 1)
    core, chip = lax.rem(then, 2), lax.div(then, 2)
    above = first_of_next(
        own,
        s_ref[then + 1],
        all_ref[core, chip, 0:8, :],
        all_ref[core, chip, 8:16, :],
        all_ref[core, chip, 32:40, :],
        z_entry_ref[...],
    )
    above = jnp.where(me == groups_z - 1, 0.0, above)

    w_ref[0] = jnp.zeros((2, XC), jnp.float32)

    def put(j, value):
        w_ref[j + 1] = value

    chain(groups_z, lambda j, q: all_ref[j % 2, j // 2, 40 + 2 * q : 42 + 2 * q, :], put)
    before_wide, value = w_ref[me], w_ref[me + 1]
    e_ref[2 * ZC - 2 : 2 * ZC] = value
    for i in range(ZC - 2, -1, -1):
        value = (sub_wide_ref[0, i] + sub_wide_ref[1, i] * before_wide) + sub_wide_ref[2, i] * value
        e_ref[2 * i : 2 * i + 2] = value
    row = lax.axis_index("gy")
    south = jnp.where(row == 0, 0.0, e_ref[pl.ds(0, ZC, stride=2), :])
    north = jnp.where(row == groups_y - 1, 0.0, e_ref[pl.ds(1, ZC, stride=2), :])
    front(
        groups_y,
        t_ref,
        c_ref,
        m_ref,
        (before, above),
        (south, north),
        (below_ref[2], above_ref[2]),
        (south_ref[2], north_ref[2]),
        (pay_ref, sub_ref, fluxz_ref, cure_ref, None),
        (k_ref, g_ref, fy_ref, r_ref),
    )


def call(kernel, outs, scratch=(), **static):
    return pl.pallas_call(
        functools.partial(kernel, **static),
        out_shape=outs,
        scratch_shapes=[pltpu.VMEM(shape, jnp.float32) for shape in scratch],
        compiler_params=pltpu.CompilerParams(vmem_limit_bytes=12 * 1024 * 1024),
        name=kernel.__name__,
    )


def body(warmth, cure, label):
    groups_z, groups_y = lax.axis_size("gz"), lax.axis_size("gy")
    chips = groups_z // 2
    up = {a: [(i, i + 1) for i in range(n - 1)] for a, n in (("gz", groups_z), ("gy", groups_y))}
    down = {a: [(j, i) for i, j in up[a]] for a in up}
    pairs = [[2 * i, 2 * i + 1] for i in range(chips)]
    same_core = [[2 * i + core for i in range(chips)] for core in range(2)]
    cells = (ROWS, XC)

    t = warmth.reshape(cells)
    c = cure.reshape(cells)
    m = label.reshape(cells)

    zlo, zhi, ylo, yhi = call(
        edges_kernel, (f32(3, YC, XC), f32(3, YC, XC), f32(3, ZC, XC), f32(3, ZC, XC))
    )(t, c, m)
    z_halo = (lax.ppermute(zhi, "gz", up["gz"]), lax.ppermute(zlo, "gz", down["gz"]))
    y_halo = (lax.ppermute(yhi, "gy", up["gy"]), lax.ppermute(ylo, "gy", down["gy"]))

    def gather_y(pay):
        return lax.all_to_all(pay, "gy", 0, 0, tiled=True)

    def gather_z(pay):
        column = lax.all_to_all(pay, "gz", 0, 0, tiled=True, axis_index_groups=same_core)
        return lax.all_gather(column, "gz", axis_index_groups=pairs)

    sizes = dict(groups_y=groups_y, groups_z=groups_z)
    pay_y, sub_y, block = f32(groups_y, 5 * ZC, XC), f32(3, YC - 1, ZC, XC), f32(*cells)
    sub_z, z_entry = f32(3, ZC - 1, YC, XC), f32(YC, XC)
    line = (groups_y + 1, ZC, XC)
    message = f32(3 * ZC + 1, XC)

    pay, sub, fluxz, c1, y_entry, toward_south, toward_north = call(
        front_kernel,
        (pay_y, sub_y, block, block, f32(ZC, XC), message, message),
        [cells] * 4,
        groups=groups_y,
    )(t, c, m, *z_halo, *y_halo)
    of_south = lax.ppermute(toward_north, "gy", up["gy"])
    of_north = lax.ppermute(toward_south, "gy", down["gy"])
    pay, subz, entry, sub_wide = call(
        middle_kernel,
        (f32(chips, 56, XC), sub_z, z_entry, f32(3, ZC - 1, 2, XC)),
        [line, cells, (56, XC), (3, 2 * ZC + 2, XC)],
        copies=chips,
        now=1,
        wide=True,
        **sizes,
    )(gather_y(pay), sub, fluxz, c, m, *z_halo, y_entry, of_south, of_north)
    pay, sub, fluxz, c2 = call(
        turn_kernel,
        (pay_y, sub_y, block, block),
        [(groups_z + 1, YC, XC), (groups_z + 1, 2, XC), cells, (2 * ZC, XC)] + [cells] * 4,
        **sizes,
    )(gather_z(pay), subz, sub_wide, entry, c1, m, *z_halo, *y_halo)
    pay, subz, entry = call(
        middle_kernel,
        (f32(chips, 40, XC), sub_z, z_entry),
        [line, cells, (40, XC)],
        copies=chips,
        now=2,
        wide=False,
        **sizes,
    )(gather_y(pay), sub, fluxz, c1, m, *z_halo)
    t2 = call(back_kernel, block, [(groups_z + 1, YC, XC)], groups_z=groups_z)(gather_z(pay), subz)
    return t2.reshape(warmth.shape), c2.reshape(cure.shape)


def solution(mesh):
    return jax.shard_map(
        body,
        mesh=mesh,
        in_specs=(P("gz", "gy", None),) * 3,
        out_specs=(P("gz", "gy", None),) * 2,
        check_vma=False,
    )
```

```python
import functools

import jax
import jax.numpy as jnp
from jax import lax
from jax.experimental import pallas as pl
from jax.experimental.pallas import tpu as pltpu
from jax.sharding import PartitionSpec as P

ZC = 16
YC = 8
XC = 128
ROWS = ZC * YC


def f32(*shape):
    return jax.ShapeDtypeStruct(shape, jnp.float32)


def conduct_of(label, cure):
    return jnp.where(label == 1, 40.0, jnp.where(label == 2, 20.0, 0.6 + 0.8 * cure))


def store_of(label):
    return jnp.where(label == 1, 3.0 / 60.0, jnp.where(label == 2, 2.0 / 60.0, 1.0 / 60.0))


def cure_of(label, warmth, cure):
    speed = 0.3 * jnp.exp(8.0 * warmth)
    return jnp.where(label == 0, 1.0 - (1.0 - cure) * jnp.exp(-speed), cure)


def y_rows(y):
    return pl.ds(y, ZC, stride=YC)


def z_rows(z):
    return pl.ds(z * YC, YC)


def edges_kernel(
    t_in, c_in, m_in, zlo_ref, zhi_ref, ylo_ref, yhi_ref, t_ref, c_ref, m_ref, sem
):
    copies = [
        pltpu.make_async_copy(src, dst, sem.at[i])
        for i, (src, dst) in enumerate(((t_in, t_ref), (c_in, c_ref), (m_in, m_ref)))
    ]
    for copy in copies:
        copy.start()
    for copy in copies:
        copy.wait()

    def put(out, rows):
        t, c, m = t_ref[rows, :], c_ref[rows, :], m_ref[rows, :]
        out[0] = t
        out[1] = conduct_of(m, c)
        out[2] = conduct_of(m, cure_of(m, t, c))

    put(zlo_ref, z_rows(0))
    put(zhi_ref, z_rows(ZC - 1))
    put(ylo_ref, y_rows(0))
    put(yhi_ref, y_rows(YC - 1))


def spread(one_ref, out_ref, sem, count):
    copies = [pltpu.make_async_copy(one_ref, out_ref.at[d], sem.at[d]) for d in range(count)]
    for copy in copies:
        copy.start()
    for copy in copies:
        copy.wait()


def eliminate(count, store, faces, right, entry, keep):
    ground, edge, side = store(0), entry, right(0)
    back_ground = back_side = None
    for i in range(count - 1):
        face = faces(i)
        inv = 1.0 / (ground + edge + face)
        edge_inv, face_inv, side_inv = edge * inv, face * inv, side * inv
        keep(i, side_inv, edge_inv, face_inv)
        more_ground, more_side = edge_inv * ground, edge_inv * side
        back_ground = more_ground if i == 0 else back_ground + more_ground
        back_side = more_side if i == 0 else back_side + more_side
        ground = store(i + 1) + face_inv * ground
        side = right(i + 1) + face_inv * side
        edge = edge_inv * face
    return back_ground, edge, ground, side, back_side


def front(groups, t_ref, c_ref, m_ref, zt, yt, zk, yk, outs, scratch):
    pay_ref, sub_ref, fluxz_ref, cure_ref, entry_ref = outs
    k_ref, g_ref, fy_ref, r_ref, p_ref, sem = scratch
    t, c, m = t_ref[...], c_ref[...], m_ref[...]
    k_ref[...] = conduct_of(m, c)
    g_ref[...] = store_of(m)
    cure_ref[...] = cure_of(m, t, c)

    ks = [yk[0]] + [k_ref[y_rows(y), :] for y in range(YC)] + [yk[1]]
    ts = [yt[0]] + [t_ref[y_rows(y), :] for y in range(YC)] + [yt[1]]
    face_y = [0.5 * (ks[i] + ks[i + 1]) for i in range(YC + 1)]
    flow_y = [face_y[i] * (ts[i + 1] - ts[i]) for i in range(YC + 1)]
    for y in range(YC):
        fy_ref[y_rows(y), :] = flow_y[y + 1] - flow_y[y]
    if entry_ref is not None:
        entry_ref[...] = face_y[YC]

    lane = lax.broadcasted_iota(jnp.int32, (YC, XC), 1)
    first_lane, last_lane = lane == 0, lane == XC - 1
    k_prev, t_prev = zk[0], zt[0]
    flow_prev = 0.5 * (k_prev + k_ref[z_rows(0), :]) * (t_ref[z_rows(0), :] - t_prev)
    batch = 4
    for z0 in range(0, ZC, batch):
        gs, ls, rs, sides, stores = [], [], [], [], []
        for z in range(z0, z0 + batch):
            kz, tz, g = k_ref[z_rows(z), :], t_ref[z_rows(z), :], g_ref[z_rows(z), :]
            k_next = k_ref[z_rows(z + 1), :] if z + 1 < ZC else zk[1]
            t_next = t_ref[z_rows(z + 1), :] if z + 1 < ZC else zt[1]
            flow_next = 0.5 * (kz + k_next) * (t_next - tz)
            flux_z = flow_next - flow_prev
            flow_prev = flow_next
            fluxz_ref[z_rows(z), :] = flux_z
            k_left = jnp.where(first_lane, 0.0, pltpu.roll(kz, 1, 1))
            t_left = jnp.where(first_lane, 0.0, pltpu.roll(tz, 1, 1))
            face_left = 0.5 * (kz + k_left)
            flow_left = face_left * (tz - t_left)
            face_right = jnp.where(last_lane, 0.5 * kz, pltpu.roll(face_left, XC - 1, 1))
            flow_right = jnp.where(last_lane, -face_right * tz, pltpu.roll(flow_left, XC - 1, 1))
            delta = cure_ref[z_rows(z), :] - c_ref[z_rows(z), :]
            sides.append(
                g * (tz + 0.4 * delta)
                + (flow_right - flow_left)
                + 2.0 * (fy_ref[z_rows(z), :] + flux_z)
            )
            gs.append(
                g
                + jnp.where(first_lane, face_left, 0.0)
                + jnp.where(last_lane, face_right, 0.0)
            )
            ls.append(jnp.where(first_lane, 0.0, face_left))
            rs.append(jnp.where(last_lane, 0.0, face_right))
            stores.append(g)
        stride = 1
        while stride < XC:
            for b in range(batch):
                ground, left, right, side = gs[b], ls[b], rs[b], sides[b]
                inv = 1.0 / (ground + left + right)
                ground_inv, side_inv = ground * inv, side * inv
                gs[b] = (
                    ground
                    + left * pltpu.roll(ground_inv, stride, 1)
                    + right * pltpu.roll(ground_inv, XC - stride, 1)
                )
                sides[b] = (
                    side
                    + left * pltpu.roll(side_inv, stride, 1)
                    + right * pltpu.roll(side_inv, XC - stride, 1)
                )
                if 2 * stride < XC:
                    ls[b] = left * pltpu.roll(left * inv, stride, 1)
                    rs[b] = right * pltpu.roll(right * inv, XC - stride, 1)
            stride *= 2
        for b in range(batch):
            rows = z_rows(z0 + b)
            r_ref[rows, :] = stores[b] * (sides[b] / gs[b]) - fy_ref[rows, :]

    def keep(i, side_inv, edge_inv, face_inv):
        sub_ref[0, i] = side_inv
        sub_ref[1, i] = edge_inv
        sub_ref[2, i] = face_inv

    back_ground, edge, ground, side, back_side = eliminate(
        YC,
        lambda i: g_ref[y_rows(i), :],
        lambda i: face_y[i + 1],
        lambda i: r_ref[y_rows(i), :],
        face_y[0],
        keep,
    )
    ground = ground + jnp.where(lax.axis_index("gy") == groups - 1, face_y[YC], 0.0)
    for q, number in enumerate((back_ground, edge, ground, side, back_side)):
        p_ref[ZC * q : ZC * q + ZC] = number
    spread(p_ref, pay_ref, sem, groups)


def front_kernel(
    t_ref,
    c_ref,
    m_ref,
    below_ref,
    above_ref,
    south_ref,
    north_ref,
    pay_ref,
    sub_ref,
    fluxz_ref,
    cure_ref,
    entry_ref,
    toward_south_ref,
    toward_north_ref,
    k_ref,
    g_ref,
    fy_ref,
    r_ref,
    p_ref,
    sem,
    *,
    groups,
):
    front(
        groups,
        t_ref,
        c_ref,
        m_ref,
        (below_ref[0], above_ref[0]),
        (south_ref[0], north_ref[0]),
        (below_ref[1], above_ref[1]),
        (south_ref[1], north_ref[1]),
        (pay_ref, sub_ref, fluxz_ref, cure_ref, entry_ref),
        (k_ref, g_ref, fy_ref, r_ref, p_ref, sem),
    )
    for out, y in ((toward_south_ref, 0), (toward_north_ref, YC - 1)):
        k = k_ref[y_rows(y), :]
        out[0:16] = fluxz_ref[y_rows(y), :]
        out[16:32] = g_ref[y_rows(y), :]
        fy_ref[8:24, :] = k
        fy_ref[7:8, :] = below_ref[1, y : y + 1, :]
        fy_ref[24:25, :] = above_ref[1, y : y + 1, :]
        out[32:48] = 0.5 * (fy_ref[7:23, :] + k)
        out[48:49] = 0.5 * (fy_ref[23:24, :] + fy_ref[24:25, :])


def chain(count, read, put):
    def ground_of(j):
        return read(j, 2) + read(j + 1, 0) if j + 1 < count else read(j, 2)

    def side_of(j):
        return read(j, 3) + read(j + 1, 4) if j + 1 < count else read(j, 3)

    half = count // 2
    gain, part = [None] * count, [None] * count
    ground_l, side_l = ground_of(0) + read(0, 1), side_of(0)
    ground_r, side_r = ground_of(count - 1), side_of(count - 1)
    for i in range(half - 1):
        edge = read(i + 1, 1)
        inv = 1.0 / (ground_l + edge)
        gain[i], part[i] = edge * inv, side_l * inv
        ground_l = ground_of(i + 1) + gain[i] * ground_l
        side_l = side_of(i + 1) + gain[i] * side_l
        j = count - 1 - i
        edge = read(j, 1)
        inv = 1.0 / (ground_r + edge)
        gain[j], part[j] = edge * inv, side_r * inv
        ground_r = ground_of(j - 1) + gain[j] * ground_r
        side_r = side_of(j - 1) + gain[j] * side_r
    edge = read(half, 1)
    inv = 1.0 / (ground_l * ground_r + edge * (ground_l + ground_r))
    low = (side_l * (ground_r + edge) + edge * side_r) * inv
    high = (side_r * (ground_l + edge) + edge * side_l) * inv
    put(half - 1, low)
    put(half, high)
    for i in range(half - 2, -1, -1):
        low = part[i] + gain[i] * low
        put(i, low)
        j = count - 1 - i
        high = part[j] + gain[j] * high
        put(j, high)


def first_of_next(own, after, back_ground, edge, back_side, entry):
    return own - (back_ground * own + edge * (own - after) - back_side) / entry


def middle_kernel(*refs, groups_y, groups_z, now, wide):
    all_ref, sub_ref, fluxz_ref, c_ref, m_ref, below_ref, above_ref = refs[:7]
    refs = refs[7:]
    if wide:
        y_entry_ref, of_south_ref, of_north_ref = refs[:3]
        refs = refs[3:]
    p_ref, subz_ref, entry_ref = refs[:3]
    refs = refs[3:]
    if wide:
        sub_wide_ref, refs = refs[0], refs[1:]
    s_ref, v_ref = refs[:2]
    s_ref[0] = jnp.zeros((ZC, XC), jnp.float32)

    def put(j, value):
        s_ref[j + 1] = value

    chain(groups_y, lambda j, q: all_ref[j, 16 * q : 16 * q + 16, :], put)
    me = lax.axis_index("gy")
    before, own = s_ref[me], s_ref[me + 1]
    value = own
    v_ref[y_rows(YC - 1), :] = value
    for i in range(YC - 2, -1, -1):
        value = (sub_ref[0, i] + sub_ref[1, i] * before) + sub_ref[2, i] * value
        v_ref[y_rows(i), :] = value

    ks = [below_ref[now]]
    for z in range(ZC):
        ks.append(conduct_of(m_ref[z_rows(z), :], c_ref[z_rows(z), :]))
    ks.append(above_ref[now])
    faces = [0.5 * (ks[i] + ks[i + 1]) for i in range(ZC + 1)]
    entry_ref[...] = faces[ZC]

    def keep(i, side_inv, edge_inv, face_inv):
        subz_ref[0, i] = side_inv
        subz_ref[1, i] = edge_inv
        subz_ref[2, i] = face_inv

    def right(i):
        return store_of(m_ref[z_rows(i), :]) * v_ref[z_rows(i), :] - fluxz_ref[z_rows(i), :]

    at_end = lax.axis_index("gz") == groups_z - 1
    numbers = eliminate(
        ZC,
        lambda i: store_of(m_ref[z_rows(i), :]),
        lambda i: faces[i + 1],
        right,
        faces[0],
        keep,
    )
    for q, number in enumerate(numbers):
        if q == 2:
            number = number + jnp.where(at_end, faces[ZC], 0.0)
        p_ref[8 * q : 8 * q + 8] = number

    if wide:
        h_ref = refs[2]
        p_ref[48:56] = jnp.zeros((8, XC), jnp.float32)
        then = jnp.minimum(me + 1, groups_y - 1)
        after = s_ref[then + 1]
        north = first_of_next(
            own,
            after,
            all_ref[then, 0:16, :],
            all_ref[then, 16:32, :],
            all_ref[then, 64:80, :],
            y_entry_ref[...],
        )
        for side, value, of_ref in ((0, before, of_south_ref), (1, north, of_north_ref)):
            capacity = of_ref[16:32]
            rows = pl.ds(side, ZC, stride=2)
            h_ref[0, rows, :] = jnp.where(capacity > 0.0, capacity, 1.0)
            h_ref[1, rows, :] = capacity * value - of_ref[0:16]
            h_ref[2, rows, :] = of_ref[32:48]
            h_ref[2, 32 + side : 33 + side, :] = of_ref[48:49]

        def keep_wide(i, side_inv, edge_inv, face_inv):
            sub_wide_ref[0, i] = side_inv
            sub_wide_ref[1, i] = edge_inv
            sub_wide_ref[2, i] = face_inv

        numbers = eliminate(
            ZC,
            lambda i: h_ref[0, 2 * i : 2 * i + 2, :],
            lambda i: h_ref[2, 2 * i + 2 : 2 * i + 4, :],
            lambda i: h_ref[1, 2 * i : 2 * i + 2, :],
            h_ref[2, 0:2, :],
            keep_wide,
        )
        for q, number in enumerate(numbers):
            if q == 2:
                number = number + jnp.where(at_end, h_ref[2, 32:34, :], 0.0)
            p_ref[40 + 2 * q : 42 + 2 * q] = number


def pair_numbers(pair_ref, rows):
    return [[pair_ref[core, rows(q), :] for q in range(5)] for core in range(2)]


def between(low, high):
    ground, side = low[2] + high[0], low[3] + high[4]
    return ground, side, 1.0 / (ground + low[1] + high[1])


def main_rows(q):
    return pl.ds(YC * q, YC)


def wide_rows(q):
    return pl.ds(5 * YC + 2 * q, 2)


def merge_kernel(pair_ref, pay_ref, p_ref, sem, *, copies, wide):
    def merged(rows):
        low, high = pair_numbers(pair_ref, rows)
        ground, side, inv = between(low, high)
        low_inv, high_inv = low[1] * inv, high[1] * inv
        return (
            low[0] + low_inv * ground,
            low_inv * high[1],
            high[2] + high_inv * ground,
            high[3] + high_inv * side,
            low[4] + low_inv * side,
        )

    half = YC // 2
    width = half + wide
    core = lax.rem(lax.axis_index("gz"), 2)
    if p_ref.shape[0] > 5 * width:
        p_ref[p_ref.shape[0] - 8 :] = jnp.zeros((8, XC), jnp.float32)
    for q, number in enumerate(merged(main_rows)):
        p_ref[width * q : width * q + half] = jnp.where(core == 0, number[:half], number[half:])
    if wide:
        for q, number in enumerate(merged(wide_rows)):
            row = width * q + half
            p_ref[row : row + 1] = jnp.where(core == 0, number[:1], number[1:])
    spread(p_ref, pay_ref, sem, copies)


def chain_kernel(all_ref, out_ref, s_ref, *, chips, width):
    s_ref[0] = jnp.zeros((width, XC), jnp.float32)

    def put(j, value):
        s_ref[j + 1] = value

    chain(chips, lambda j, q: all_ref[j, width * q : width * q + width, :], put)
    me = lax.div(lax.axis_index("gz"), 2)
    then = jnp.minimum(me + 1, chips - 1)
    own, after = s_ref[me + 1], s_ref[then + 1]
    numbers = [all_ref[then, width * q : width * q + width, :] for q in range(5)]
    out_ref[8:16] = jnp.zeros((8, XC), jnp.float32)
    out_ref[0:width] = s_ref[me]
    out_ref[width : 2 * width] = own
    out_ref[2 * width : 3 * width] = numbers[0] * own + numbers[1] * (own - after) - numbers[4]


def ends_of(pair_ref, rows, before, last):
    low, high = pair_numbers(pair_ref, rows)
    ground, side, inv = between(low, high)
    node = (side + low[1] * before + high[1] * last) * inv
    upper = lax.rem(lax.axis_index("gz"), 2) == 1
    return jnp.where(upper, node, before), jnp.where(upper, last, node), node, high


def back(pair_ref, res_ref, subz_ref, t_ref, u_ref, width):
    half = YC // 2
    for q in range(3):
        for core in range(2):
            u_ref[q, half * core : half * core + half] = res_ref[
                core, width * q : width * q + half, :
            ]
    last = u_ref[1]
    before, own, node, high = ends_of(pair_ref, main_rows, u_ref[0], last)
    value = own
    t_ref[z_rows(ZC - 1), :] = value
    for i in range(ZC - 2, -1, -1):
        value = (subz_ref[0, i] + subz_ref[1, i] * before) + subz_ref[2, i] * value
        t_ref[z_rows(i), :] = value
    return before, own, node, last, high


def back_kernel(pair_ref, res_ref, subz_ref, t_ref, u_ref):
    back(pair_ref, res_ref, subz_ref, t_ref, u_ref, YC // 2)


def turn_kernel(
    pair_ref,
    res_ref,
    subz_ref,
    sub_wide_ref,
    z_entry_ref,
    c_ref,
    m_ref,
    below_ref,
    above_ref,
    south_ref,
    north_ref,
    pay_ref,
    sub_ref,
    fluxz_ref,
    cure_ref,
    u_ref,
    w_ref,
    t_ref,
    e_ref,
    k_ref,
    g_ref,
    fy_ref,
    r_ref,
    p_ref,
    sem,
    *,
    groups_y,
    groups_z,
):
    half = YC // 2
    width = half + 1
    before, own, node, last, high = back(pair_ref, res_ref, subz_ref, t_ref, u_ref, width)
    me = lax.axis_index("gz")
    inside = high[0] * node + high[1] * (node - last) - high[4]
    current = jnp.where(lax.rem(me, 2) == 1, u_ref[2], inside)
    above = jnp.where(me == groups_z - 1, 0.0, own - current / z_entry_ref[...])

    for q in range(2):
        for core in range(2):
            row = width * q + half
            w_ref[q, core : core + 1] = res_ref[core, row : row + 1, :]
    before_wide, value, _, _ = ends_of(pair_ref, wide_rows, w_ref[0], w_ref[1])
    e_ref[2 * ZC - 2 : 2 * ZC] = value
    for i in range(ZC - 2, -1, -1):
        value = (sub_wide_ref[0, i] + sub_wide_ref[1, i] * before_wide) + sub_wide_ref[2, i] * value
        e_ref[2 * i : 2 * i + 2] = value
    row = lax.axis_index("gy")
    south = jnp.where(row == 0, 0.0, e_ref[pl.ds(0, ZC, stride=2), :])
    north = jnp.where(row == groups_y - 1, 0.0, e_ref[pl.ds(1, ZC, stride=2), :])
    front(
        groups_y,
        t_ref,
        c_ref,
        m_ref,
        (before, above),
        (south, north),
        (below_ref[2], above_ref[2]),
        (south_ref[2], north_ref[2]),
        (pay_ref, sub_ref, fluxz_ref, cure_ref, None),
        (k_ref, g_ref, fy_ref, r_ref, p_ref, sem),
    )


def call(kernel, outs, scratch=(), spread_to=0, **static):
    out_specs = [pl.BlockSpec(memory_space=pltpu.VMEM)] * len(outs)
    shapes = [pltpu.VMEM(shape, jnp.float32) for shape in scratch]
    if spread_to:
        out_specs[0] = pl.BlockSpec(memory_space=pl.ANY)
        shapes.append(pltpu.SemaphoreType.DMA((spread_to,)))
    return pl.pallas_call(
        functools.partial(kernel, **static),
        out_shape=tuple(outs),
        out_specs=tuple(out_specs),
        scratch_shapes=shapes,
        compiler_params=pltpu.CompilerParams(vmem_limit_bytes=12 * 1024 * 1024),
        name=kernel.__name__,
    )


def body(warmth, cure, label):
    groups_z, groups_y = lax.axis_size("gz"), lax.axis_size("gy")
    chips = groups_z // 2
    up = {a: [(i, i + 1) for i in range(n - 1)] for a, n in (("gz", groups_z), ("gy", groups_y))}
    down = {a: [(j, i) for i, j in up[a]] for a in up}
    pairs = [[2 * i, 2 * i + 1] for i in range(chips)]
    same_core = [[2 * i + core for i in range(chips)] for core in range(2)]
    cells = (ROWS, XC)
    block = f32(*cells)

    t = warmth.reshape(cells)
    c = cure.reshape(cells)
    m = label.reshape(cells)

    zlo, zhi, ylo, yhi = pl.pallas_call(
        edges_kernel,
        out_shape=(f32(3, YC, XC), f32(3, YC, XC), f32(3, ZC, XC), f32(3, ZC, XC)),
        in_specs=[pl.BlockSpec(memory_space=pltpu.HBM)] * 3,
        scratch_shapes=[
            pltpu.VMEM(cells, jnp.float32),
            pltpu.VMEM(cells, jnp.float32),
            pltpu.VMEM(cells, jnp.int32),
            pltpu.SemaphoreType.DMA((3,)),
        ],
        compiler_params=pltpu.CompilerParams(vmem_limit_bytes=12 * 1024 * 1024),
        name="edges_kernel",
    )(t, c, m)
    z_halo = (lax.ppermute(zhi, "gz", up["gz"]), lax.ppermute(zlo, "gz", down["gz"]))
    y_halo = (lax.ppermute(yhi, "gy", up["gy"]), lax.ppermute(ylo, "gy", down["gy"]))

    def gather_y(pay):
        return lax.all_to_all(pay, "gy", 0, 0, tiled=True)

    def share(numbers):
        return lax.all_gather(numbers, "gz", axis_index_groups=pairs)

    def chain_z(pair, wide):
        width = YC // 2 + wide
        rows = -(-5 * width // 8) * 8
        (pay,) = call(
            merge_kernel,
            [f32(chips, rows, XC)],
            [(rows, XC)],
            spread_to=chips,
            copies=chips,
            wide=wide,
        )(pair)
        column = lax.all_to_all(pay, "gz", 0, 0, tiled=True, axis_index_groups=same_core)
        (found,) = call(
            chain_kernel, [f32(16, XC)], [(chips + 1, width, XC)], chips=chips, width=width
        )(column)
        return share(found)

    sizes = dict(groups_y=groups_y, groups_z=groups_z)
    pay_y, sub_y = f32(groups_y, 5 * ZC, XC), f32(3, YC - 1, ZC, XC)
    sub_z, z_entry = f32(3, ZC - 1, YC, XC), f32(YC, XC)
    line = (groups_y + 1, ZC, XC)
    message = f32(3 * ZC + 1, XC)
    front_scratch = [cells] * 4 + [(5 * ZC, XC)]

    pay, sub, fluxz, c1, y_entry, toward_south, toward_north = call(
        front_kernel,
        [pay_y, sub_y, block, block, f32(ZC, XC), message, message],
        front_scratch,
        spread_to=groups_y,
        groups=groups_y,
    )(t, c, m, *z_halo, *y_halo)
    of_south = lax.ppermute(toward_north, "gy", up["gy"])
    of_north = lax.ppermute(toward_south, "gy", down["gy"])
    numbers, subz, entry, sub_wide = call(
        middle_kernel,
        [f32(56, XC), sub_z, z_entry, f32(3, ZC - 1, 2, XC)],
        [line, cells, (3, 2 * ZC + 2, XC)],
        now=1,
        wide=True,
        **sizes,
    )(gather_y(pay), sub, fluxz, c, m, *z_halo, y_entry, of_south, of_north)
    pair = share(numbers)
    pay, sub, fluxz, c2 = call(
        turn_kernel,
        [pay_y, sub_y, block, block],
        [(3, YC, XC), (2, 2, XC), cells, (2 * ZC, XC)] + front_scratch,
        spread_to=groups_y,
        **sizes,
    )(pair, chain_z(pair, True), subz, sub_wide, entry, c1, m, *z_halo, *y_halo)
    numbers, subz, entry = call(
        middle_kernel,
        [f32(40, XC), sub_z, z_entry],
        [line, cells],
        now=2,
        wide=False,
        **sizes,
    )(gather_y(pay), sub, fluxz, c1, m, *z_halo)
    pair = share(numbers)
    (t2,) = call(back_kernel, [block], [(3, YC, XC)])(pair, chain_z(pair, False), subz)
    return t2.reshape(warmth.shape), c2.reshape(cure.shape)


def solution(mesh):
    return jax.shard_map(
        body,
        mesh=mesh,
        in_specs=(P("gz", "gy", None),) * 3,
        out_specs=(P("gz", "gy", None),) * 2,
        check_vma=False,
    )
```

```python
import functools

import jax
import jax.numpy as jnp
from jax import lax
from jax.experimental import pallas as pl
from jax.experimental.pallas import tpu as pltpu
from jax.sharding import PartitionSpec as P

ZC = 16
YC = 8
XC = 128
ROWS = ZC * YC


def f32(*shape):
    return jax.ShapeDtypeStruct(shape, jnp.float32)


def conduct_of(label, cure):
    return jnp.where(label == 1, 40.0, jnp.where(label == 2, 20.0, 0.6 + 0.8 * cure))


def store_of(label):
    return jnp.where(label == 1, 3.0 / 60.0, jnp.where(label == 2, 2.0 / 60.0, 1.0 / 60.0))


def cure_of(label, warmth, cure):
    speed = 0.3 * jnp.exp(8.0 * warmth)
    return jnp.where(label == 0, 1.0 - (1.0 - cure) * jnp.exp(-speed), cure)


def y_rows(y):
    return pl.ds(y, ZC, stride=YC)


def z_rows(z):
    return pl.ds(z * YC, YC)


def edges_kernel(
    t_in, c_in, m_in, zlo_ref, zhi_ref, ylo_ref, yhi_ref, t_ref, c_ref, m_ref, sem
):
    copies = [
        pltpu.make_async_copy(src, dst, sem.at[i])
        for i, (src, dst) in enumerate(((t_in, t_ref), (c_in, c_ref), (m_in, m_ref)))
    ]
    for copy in copies:
        copy.start()
    for copy in copies:
        copy.wait()

    def put(out, rows):
        t, c, m = t_ref[rows, :], c_ref[rows, :], m_ref[rows, :]
        out[0] = t
        out[1] = conduct_of(m, c)
        out[2] = conduct_of(m, cure_of(m, t, c))

    put(zlo_ref, z_rows(0))
    put(zhi_ref, z_rows(ZC - 1))
    put(ylo_ref, y_rows(0))
    put(yhi_ref, y_rows(YC - 1))


def spread(one_ref, out_ref, sem, count):
    copies = [pltpu.make_async_copy(one_ref, out_ref.at[d], sem.at[d]) for d in range(count)]
    for copy in copies:
        copy.start()
    for copy in copies:
        copy.wait()


def reduce_coefficients(count, store, faces, entry, co_ref):
    ground, edge = store(0), entry
    back_ground = None
    for i in range(count - 1):
        face = faces(i)
        inv = 1.0 / (ground + edge + face)
        edge_inv, face_inv = edge * inv, face * inv
        co_ref[0, i] = inv
        co_ref[1, i] = edge_inv
        co_ref[2, i] = face_inv
        more = edge_inv * ground
        back_ground = more if i == 0 else back_ground + more
        ground = store(i + 1) + face_inv * ground
        edge = edge_inv * face
    return back_ground, edge, ground


def reduce_sides(count, right, co_ref, side_ref):
    side = right(0)
    back_side = None
    for i in range(count - 1):
        side_ref[i] = side * co_ref[0, i]
        more = co_ref[1, i] * side
        back_side = more if i == 0 else back_side + more
        side = right(i + 1) + co_ref[2, i] * side
    return side, back_side


def substitute(count, before, own, co_ref, side_ref, put):
    value = own
    put(count - 1, value)
    for i in range(count - 2, -1, -1):
        value = (side_ref[i] + co_ref[1, i] * before) + co_ref[2, i] * value
        put(i, value)


def edge_lanes():
    lane = lax.broadcasted_iota(jnp.int32, (YC, XC), 1)
    return lane == 0, lane == XC - 1


ROUNDS = 7


def x_coefficients(c_ref, m_ref, x_ref):
    first_lane, last_lane = edge_lanes()
    batch = 4
    for z0 in range(0, ZC, batch):
        gs, ls, rs, stores = [], [], [], []
        for z in range(z0, z0 + batch):
            rows = z_rows(z)
            m = m_ref[rows, :]
            k, g = conduct_of(m, c_ref[rows, :]), store_of(m)
            face_left = 0.5 * (k + jnp.where(first_lane, 0.0, pltpu.roll(k, 1, 1)))
            face_right = jnp.where(last_lane, 0.5 * k, pltpu.roll(face_left, XC - 1, 1))
            x_ref[2 * ROUNDS + 1, rows, :] = face_left
            gs.append(
                g
                + jnp.where(first_lane, face_left, 0.0)
                + jnp.where(last_lane, face_right, 0.0)
            )
            ls.append(jnp.where(first_lane, 0.0, face_left))
            rs.append(jnp.where(last_lane, 0.0, face_right))
            stores.append(g)
        for level in range(ROUNDS):
            low, high = 1 << level, XC - (1 << level)
            for b in range(batch):
                rows = z_rows(z0 + b)
                ground, left, right = gs[b], ls[b], rs[b]
                inv = 1.0 / (ground + left + right)
                to_left = left * pltpu.roll(inv, low, 1)
                to_right = right * pltpu.roll(inv, high, 1)
                x_ref[2 * level, rows, :] = to_left
                x_ref[2 * level + 1, rows, :] = to_right
                gs[b] = (
                    ground
                    + to_left * pltpu.roll(ground, low, 1)
                    + to_right * pltpu.roll(ground, high, 1)
                )
                if level + 1 < ROUNDS:
                    ls[b] = to_left * pltpu.roll(left, low, 1)
                    rs[b] = to_right * pltpu.roll(right, high, 1)
        for b in range(batch):
            x_ref[2 * ROUNDS, z_rows(z0 + b), :] = stores[b] / gs[b]


def x_kernel(c_ref, m_ref, x_ref):
    x_coefficients(c_ref, m_ref, x_ref)


def z_coefficients(groups_z, c_ref, m_ref, below, above, co_ref, num_ref):
    ks = [below]
    for z in range(ZC):
        ks.append(conduct_of(m_ref[z_rows(z), :], c_ref[z_rows(z), :]))
    ks.append(above)
    faces = [0.5 * (ks[i] + ks[i + 1]) for i in range(ZC + 1)]
    numbers = reduce_coefficients(
        ZC,
        lambda i: store_of(m_ref[z_rows(i), :]),
        lambda i: faces[i + 1],
        faces[0],
        co_ref,
    )
    num_ref[0] = numbers[0]
    num_ref[1] = numbers[1]
    at_end = lax.axis_index("gz") == groups_z - 1
    num_ref[2] = numbers[2] + jnp.where(at_end, faces[ZC], 0.0)
    return faces[ZC]


def ahead_kernel(
    c_ref,
    next_c_ref,
    m_ref,
    below_ref,
    above_ref,
    x_ref,
    co1_ref,
    num1_ref,
    co2_ref,
    num2_ref,
    entry_ref,
    *,
    groups_z,
):
    x_coefficients(next_c_ref, m_ref, x_ref)
    entry_ref[...] = z_coefficients(
        groups_z, c_ref, m_ref, below_ref[1], above_ref[1], co1_ref, num1_ref
    )
    z_coefficients(groups_z, next_c_ref, m_ref, below_ref[2], above_ref[2], co2_ref, num2_ref)


def flow_rhs(t_ref, c_ref, m_ref, x_ref, zt, yt, zk, yk, outs, scratch):
    fluxz_ref, cure_ref = outs
    k_ref, g_ref, fy_ref, r_ref = scratch
    t, c, m = t_ref[...], c_ref[...], m_ref[...]
    k_ref[...] = conduct_of(m, c)
    g_ref[...] = store_of(m)
    cure_ref[...] = cure_of(m, t, c)

    ks = [yk[0]] + [k_ref[y_rows(y), :] for y in range(YC)] + [yk[1]]
    ts = [yt[0]] + [t_ref[y_rows(y), :] for y in range(YC)] + [yt[1]]
    face_y = [0.5 * (ks[i] + ks[i + 1]) for i in range(YC + 1)]
    flow_y = [face_y[i] * (ts[i + 1] - ts[i]) for i in range(YC + 1)]
    for y in range(YC):
        fy_ref[y_rows(y), :] = flow_y[y + 1] - flow_y[y]

    first_lane, last_lane = edge_lanes()
    k_prev, t_prev = zk[0], zt[0]
    flow_prev = 0.5 * (k_prev + k_ref[z_rows(0), :]) * (t_ref[z_rows(0), :] - t_prev)
    batch = 4
    for z0 in range(0, ZC, batch):
        sides = []
        for z in range(z0, z0 + batch):
            rows = z_rows(z)
            kz, tz = k_ref[rows, :], t_ref[rows, :]
            k_next = k_ref[z_rows(z + 1), :] if z + 1 < ZC else zk[1]
            t_next = t_ref[z_rows(z + 1), :] if z + 1 < ZC else zt[1]
            flow_next = 0.5 * (kz + k_next) * (t_next - tz)
            flux_z = flow_next - flow_prev
            flow_prev = flow_next
            fluxz_ref[rows, :] = flux_z
            t_left = jnp.where(first_lane, 0.0, pltpu.roll(tz, 1, 1))
            flow_left = x_ref[2 * ROUNDS + 1, rows, :] * (tz - t_left)
            flow_right = jnp.where(last_lane, -0.5 * kz * tz, pltpu.roll(flow_left, XC - 1, 1))
            delta = cure_ref[rows, :] - c_ref[rows, :]
            sides.append(
                g_ref[rows, :] * (tz + 0.4 * delta)
                + (flow_right - flow_left)
                + 2.0 * (fy_ref[rows, :] + flux_z)
            )
        for level in range(ROUNDS):
            low, high = 1 << level, XC - (1 << level)
            for b in range(batch):
                rows = z_rows(z0 + b)
                side = sides[b]
                sides[b] = (
                    side
                    + x_ref[2 * level, rows, :] * pltpu.roll(side, low, 1)
                    + x_ref[2 * level + 1, rows, :] * pltpu.roll(side, high, 1)
                )
        for b in range(batch):
            rows = z_rows(z0 + b)
            r_ref[rows, :] = x_ref[2 * ROUNDS, rows, :] * sides[b] - fy_ref[rows, :]
    return face_y


def front_kernel(
    t_ref,
    c_ref,
    m_ref,
    x_ref,
    below_ref,
    above_ref,
    south_ref,
    north_ref,
    pay_ref,
    co1_ref,
    side_ref,
    co2_ref,
    fluxz_ref,
    cure_ref,
    entry_ref,
    toward_south_ref,
    toward_north_ref,
    k_ref,
    g_ref,
    fy_ref,
    r_ref,
    p_ref,
    sem,
    *,
    groups,
):
    face_y = flow_rhs(
        t_ref,
        c_ref,
        m_ref,
        x_ref,
        (below_ref[0], above_ref[0]),
        (south_ref[0], north_ref[0]),
        (below_ref[1], above_ref[1]),
        (south_ref[1], north_ref[1]),
        (fluxz_ref, cure_ref),
        (k_ref, g_ref, fy_ref, r_ref),
    )
    entry_ref[...] = face_y[YC]
    at_end = lax.axis_index("gy") == groups - 1
    back_ground, edge, ground = reduce_coefficients(
        YC, lambda i: g_ref[y_rows(i), :], lambda i: face_y[i + 1], face_y[0], co1_ref
    )
    ground = ground + jnp.where(at_end, face_y[YC], 0.0)
    side, back_side = reduce_sides(YC, lambda i: r_ref[y_rows(i), :], co1_ref, side_ref)
    for out, y in ((toward_south_ref, 0), (toward_north_ref, YC - 1)):
        k = k_ref[y_rows(y), :]
        out[0:16] = fluxz_ref[y_rows(y), :]
        out[16:32] = g_ref[y_rows(y), :]
        fy_ref[8:24, :] = k
        fy_ref[7:8, :] = below_ref[1, y : y + 1, :]
        fy_ref[24:25, :] = above_ref[1, y : y + 1, :]
        out[32:48] = 0.5 * (fy_ref[7:23, :] + k)
        out[48:49] = 0.5 * (fy_ref[23:24, :] + fy_ref[24:25, :])
    k_ref[...] = conduct_of(m_ref[...], cure_ref[...])
    ks = [south_ref[2]] + [k_ref[y_rows(y), :] for y in range(YC)] + [north_ref[2]]
    faces = [0.5 * (ks[i] + ks[i + 1]) for i in range(YC + 1)]
    back_ground2, edge2, ground2 = reduce_coefficients(
        YC, lambda i: g_ref[y_rows(i), :], lambda i: faces[i + 1], faces[0], co2_ref
    )
    ground2 = ground2 + jnp.where(at_end, faces[YC], 0.0)
    numbers = (back_ground, edge, ground, side, back_side, back_ground2, edge2, ground2)
    for q, number in enumerate(numbers):
        p_ref[ZC * q : ZC * q + ZC] = number
    spread(p_ref, pay_ref, sem, groups)


def chain(count, read, put):
    def ground_of(j):
        return read(j, 2) + read(j + 1, 0) if j + 1 < count else read(j, 2)

    def side_of(j):
        return read(j, 3) + read(j + 1, 4) if j + 1 < count else read(j, 3)

    half = count // 2
    gain, part = [None] * count, [None] * count
    ground_l, side_l = ground_of(0) + read(0, 1), side_of(0)
    ground_r, side_r = ground_of(count - 1), side_of(count - 1)
    for i in range(half - 1):
        edge = read(i + 1, 1)
        inv = 1.0 / (ground_l + edge)
        gain[i], part[i] = edge * inv, side_l * inv
        ground_l = ground_of(i + 1) + gain[i] * ground_l
        side_l = side_of(i + 1) + gain[i] * side_l
        j = count - 1 - i
        edge = read(j, 1)
        inv = 1.0 / (ground_r + edge)
        gain[j], part[j] = edge * inv, side_r * inv
        ground_r = ground_of(j - 1) + gain[j] * ground_r
        side_r = side_of(j - 1) + gain[j] * side_r
    edge = read(half, 1)
    inv = 1.0 / (ground_l * ground_r + edge * (ground_l + ground_r))
    low = (side_l * (ground_r + edge) + edge * side_r) * inv
    high = (side_r * (ground_l + edge) + edge * side_l) * inv
    put(half - 1, low)
    put(half, high)
    for i in range(half - 2, -1, -1):
        low = part[i] + gain[i] * low
        put(i, low)
        j = count - 1 - i
        high = part[j] + gain[j] * high
        put(j, high)


def first_of_next(own, after, back_ground, edge, back_side, entry):
    return own - (back_ground * own + edge * (own - after) - back_side) / entry


def y_solution(groups_y, read, co_ref, side_ref, s_ref, v_ref):
    s_ref[0] = jnp.zeros((ZC, XC), jnp.float32)

    def put(j, value):
        s_ref[j + 1] = value

    chain(groups_y, read, put)
    me = lax.axis_index("gy")

    def place(i, value):
        v_ref[y_rows(i), :] = value

    before, own = s_ref[me], s_ref[me + 1]
    substitute(YC, before, own, co_ref, side_ref, place)
    return before, own


def main_rows(q):
    return pl.ds(YC * q, YC)


def later_rows(q):
    return pl.ds(YC * (5 + q), YC)


def wide_rows(q):
    return pl.ds(8 * YC + 2 * q, 2)


SHARED = 8 * YC + 16


def middle_kernel(
    all_ref,
    co_y_ref,
    side_y_ref,
    fluxz_ref,
    m_ref,
    co_z_ref,
    num1_ref,
    num2_ref,
    y_entry_ref,
    of_south_ref,
    of_north_ref,
    p_ref,
    side_z_ref,
    co_wide_ref,
    side_wide_ref,
    s_ref,
    v_ref,
    h_ref,
    *,
    groups_y,
    groups_z,
):
    def read(j, q):
        return all_ref[j, ZC * q : ZC * q + ZC, :]

    before, own = y_solution(groups_y, read, co_y_ref, side_y_ref, s_ref, v_ref)

    def right(i):
        return store_of(m_ref[z_rows(i), :]) * v_ref[z_rows(i), :] - fluxz_ref[z_rows(i), :]

    for q in range(3):
        p_ref[main_rows(q), :] = num1_ref[q]
        p_ref[later_rows(q), :] = num2_ref[q]
    sides = reduce_sides(ZC, right, co_z_ref, side_z_ref)
    p_ref[main_rows(3), :] = sides[0]
    p_ref[main_rows(4), :] = sides[1]

    me = lax.axis_index("gy")
    then = jnp.minimum(me + 1, groups_y - 1)
    north = first_of_next(
        own,
        s_ref[then + 1],
        all_ref[then, 0:16, :],
        all_ref[then, 16:32, :],
        all_ref[then, 64:80, :],
        y_entry_ref[...],
    )
    for side, value, of_ref in ((0, before, of_south_ref), (1, north, of_north_ref)):
        capacity = of_ref[16:32]
        rows = pl.ds(side, ZC, stride=2)
        h_ref[0, rows, :] = jnp.where(capacity > 0.0, capacity, 1.0)
        h_ref[1, rows, :] = capacity * value - of_ref[0:16]
        h_ref[2, rows, :] = of_ref[32:48]
        h_ref[2, 32 + side : 33 + side, :] = of_ref[48:49]
    numbers = reduce_coefficients(
        ZC,
        lambda i: h_ref[0, 2 * i : 2 * i + 2, :],
        lambda i: h_ref[2, 2 * i + 2 : 2 * i + 4, :],
        h_ref[2, 0:2, :],
        co_wide_ref,
    )
    sides = reduce_sides(
        ZC, lambda i: h_ref[1, 2 * i : 2 * i + 2, :], co_wide_ref, side_wide_ref
    )
    at_end = lax.axis_index("gz") == groups_z - 1
    p_ref[8 * YC + 8 :, :] = jnp.zeros((8, XC), jnp.float32)
    p_ref[wide_rows(0), :] = numbers[0]
    p_ref[wide_rows(1), :] = numbers[1]
    p_ref[wide_rows(2), :] = numbers[2] + jnp.where(at_end, h_ref[2, 32:34, :], 0.0)
    p_ref[wide_rows(3), :] = sides[0]
    p_ref[wide_rows(4), :] = sides[1]


def later_middle_kernel(
    all_ref,
    more_ref,
    co_y_ref,
    side_y_ref,
    fluxz_ref,
    m_ref,
    co_z_ref,
    p_ref,
    side_z_ref,
    s_ref,
    v_ref,
    *,
    groups_y,
):
    def read(j, q):
        if q < 3:
            return all_ref[j, ZC * (5 + q) : ZC * (6 + q), :]
        return more_ref[j, ZC * (q - 3) : ZC * (q - 2), :]

    y_solution(groups_y, read, co_y_ref, side_y_ref, s_ref, v_ref)

    def right(i):
        return store_of(m_ref[z_rows(i), :]) * v_ref[z_rows(i), :] - fluxz_ref[z_rows(i), :]

    sides = reduce_sides(ZC, right, co_z_ref, side_z_ref)
    p_ref[0:YC] = sides[0]
    p_ref[YC : 2 * YC] = sides[1]


HALF = YC // 2
WIDTH = HALF + 1


def node_between(low, high):
    ground = low[2] + high[0]
    return ground, 1.0 / (ground + low[1] + high[1])


def merged_coefficients(low, high):
    ground, inv = node_between(low, high)
    low_inv, high_inv = low[1] * inv, high[1] * inv
    return low[0] + low_inv * ground, low_inv * high[1], high[2] + high_inv * ground


def merged_sides(low, high):
    _, inv = node_between(low, high)
    side = low[3] + high[4]
    return high[3] + high[1] * inv * side, low[4] + low[1] * inv * side


def first_numbers(pair_ref, rows):
    return [[pair_ref[core, rows(q), :] for q in range(5)] for core in range(2)]


def later_numbers(pair_ref, more_ref):
    return [
        [pair_ref[core, later_rows(q), :] for q in range(3)]
        + [more_ref[core, main_rows(q), :] for q in range(2)]
        for core in range(2)
    ]


def my_half(number):
    half = number.shape[0] // 2
    core = lax.rem(lax.axis_index("gz"), 2)
    return jnp.where(core == 0, number[:half], number[half:])


def merge_kernel(pair_ref, pay_ref, p_ref, sem, *, copies):
    p_ref[32:40] = jnp.zeros((8, XC), jnp.float32)
    low, high = first_numbers(pair_ref, main_rows)
    for q, number in enumerate(merged_coefficients(low, high) + merged_sides(low, high)):
        p_ref[WIDTH * q : WIDTH * q + HALF] = my_half(number)
    low, high = first_numbers(pair_ref, wide_rows)
    for q, number in enumerate(merged_coefficients(low, high) + merged_sides(low, high)):
        p_ref[WIDTH * q + HALF : WIDTH * q + WIDTH] = my_half(number)
    low, high = ([pair_ref[core, later_rows(q), :] for q in range(3)] for core in range(2))
    for q, number in enumerate(merged_coefficients(low, high)):
        row = 5 * WIDTH + HALF * q
        p_ref[row : row + HALF] = my_half(number)
    spread(p_ref, pay_ref, sem, copies)


def later_merge_kernel(pair_ref, more_ref, pay_ref, p_ref, sem, *, copies):
    low, high = later_numbers(pair_ref, more_ref)
    for q, number in enumerate(merged_sides(low, high)):
        p_ref[HALF * q : HALF * q + HALF] = my_half(number)
    spread(p_ref, pay_ref, sem, copies)


def chain_kernel(all_ref, out_ref, s_ref, *, chips):
    s_ref[0] = jnp.zeros((WIDTH, XC), jnp.float32)

    def put(j, value):
        s_ref[j + 1] = value

    chain(chips, lambda j, q: all_ref[j, WIDTH * q : WIDTH * q + WIDTH, :], put)
    me = lax.div(lax.axis_index("gz"), 2)
    then = jnp.minimum(me + 1, chips - 1)
    own, after = s_ref[me + 1], s_ref[then + 1]
    numbers = [all_ref[then, WIDTH * q : WIDTH * q + WIDTH, :] for q in (0, 1, 4)]
    out_ref[8:16] = jnp.zeros((8, XC), jnp.float32)
    out_ref[0:WIDTH] = s_ref[me]
    out_ref[WIDTH : 2 * WIDTH] = own
    out_ref[2 * WIDTH : 3 * WIDTH] = numbers[0] * own + numbers[1] * (own - after) - numbers[2]


def later_chain_kernel(all_ref, more_ref, out_ref, s_ref, *, chips):
    s_ref[0] = jnp.zeros((HALF, XC), jnp.float32)

    def put(j, value):
        s_ref[j + 1] = value

    def read(j, q):
        if q < 3:
            return all_ref[j, 5 * WIDTH + HALF * q : 5 * WIDTH + HALF * (q + 1), :]
        return more_ref[j, HALF * (q - 3) : HALF * (q - 2), :]

    chain(chips, read, put)
    me = lax.div(lax.axis_index("gz"), 2)
    out_ref[0:HALF] = s_ref[me]
    out_ref[HALF : 2 * HALF] = s_ref[me + 1]


def ends_of(low, high, before, last):
    _, inv = node_between(low, high)
    node = (low[3] + high[4] + low[1] * before + high[1] * last) * inv
    upper = lax.rem(lax.axis_index("gz"), 2) == 1
    return jnp.where(upper, node, before), jnp.where(upper, last, node), node


def joined(res_ref, u_ref, width, count):
    for q in range(count):
        for core in range(2):
            rows = pl.ds(HALF * core, HALF)
            u_ref[q, rows, :] = res_ref[core, width * q : width * q + HALF, :]


def back_kernel(pair_ref, more_ref, res_ref, co_z_ref, side_z_ref, t_ref, u_ref):
    joined(res_ref, u_ref, HALF, 2)
    low, high = later_numbers(pair_ref, more_ref)
    before, own, _ = ends_of(low, high, u_ref[0], u_ref[1])

    def place(i, value):
        t_ref[z_rows(i), :] = value

    substitute(ZC, before, own, co_z_ref, side_z_ref, place)


def turn_kernel(
    pair_ref,
    res_ref,
    co_z_ref,
    side_z_ref,
    co_wide_ref,
    side_wide_ref,
    z_entry_ref,
    c_ref,
    m_ref,
    x_ref,
    co_y_ref,
    below_ref,
    above_ref,
    south_ref,
    north_ref,
    pay_ref,
    side_y_ref,
    fluxz_ref,
    cure_ref,
    u_ref,
    w_ref,
    t_ref,
    e_ref,
    k_ref,
    g_ref,
    fy_ref,
    r_ref,
    p_ref,
    sem,
    *,
    groups_y,
    groups_z,
):
    joined(res_ref, u_ref, WIDTH, 3)
    low, high = first_numbers(pair_ref, main_rows)
    last = u_ref[1]
    before, own, node = ends_of(low, high, u_ref[0], last)

    def place(i, value):
        t_ref[z_rows(i), :] = value

    substitute(ZC, before, own, co_z_ref, side_z_ref, place)
    me = lax.axis_index("gz")
    inside = high[0] * node + high[1] * (node - last) - high[4]
    current = jnp.where(lax.rem(me, 2) == 1, u_ref[2], inside)
    above = jnp.where(me == groups_z - 1, 0.0, own - current / z_entry_ref[...])

    for q in range(2):
        for core in range(2):
            row = WIDTH * q + HALF
            w_ref[q, core : core + 1] = res_ref[core, row : row + 1, :]
    low, high = first_numbers(pair_ref, wide_rows)
    before_wide, own_wide, _ = ends_of(low, high, w_ref[0], w_ref[1])

    def place_wide(i, value):
        e_ref[2 * i : 2 * i + 2] = value

    substitute(ZC, before_wide, own_wide, co_wide_ref, side_wide_ref, place_wide)
    row = lax.axis_index("gy")
    south = jnp.where(row == 0, 0.0, e_ref[pl.ds(0, ZC, stride=2), :])
    north = jnp.where(row == groups_y - 1, 0.0, e_ref[pl.ds(1, ZC, stride=2), :])
    flow_rhs(
        t_ref,
        c_ref,
        m_ref,
        x_ref,
        (before, above),
        (south, north),
        (below_ref[2], above_ref[2]),
        (south_ref[2], north_ref[2]),
        (fluxz_ref, cure_ref),
        (k_ref, g_ref, fy_ref, r_ref),
    )
    side, back_side = reduce_sides(YC, lambda i: r_ref[y_rows(i), :], co_y_ref, side_y_ref)
    p_ref[0:ZC] = side
    p_ref[ZC : 2 * ZC] = back_side
    spread(p_ref, pay_ref, sem, groups_y)


def call(kernel, outs, scratch=(), spread_to=0, **static):
    out_specs = [pl.BlockSpec(memory_space=pltpu.VMEM)] * len(outs)
    shapes = [pltpu.VMEM(shape, jnp.float32) for shape in scratch]
    if spread_to:
        out_specs[0] = pl.BlockSpec(memory_space=pl.ANY)
        shapes.append(pltpu.SemaphoreType.DMA((spread_to,)))
    return pl.pallas_call(
        functools.partial(kernel, **static),
        out_shape=tuple(outs),
        out_specs=tuple(out_specs),
        scratch_shapes=shapes,
        compiler_params=pltpu.CompilerParams(vmem_limit_bytes=12 * 1024 * 1024),
        name=kernel.__name__,
    )


def body(warmth, cure, label):
    groups_z, groups_y = lax.axis_size("gz"), lax.axis_size("gy")
    chips = groups_z // 2
    up = {a: [(i, i + 1) for i in range(n - 1)] for a, n in (("gz", groups_z), ("gy", groups_y))}
    down = {a: [(j, i) for i, j in up[a]] for a in up}
    pairs = [[2 * i, 2 * i + 1] for i in range(chips)]
    same_core = [[2 * i + core for i in range(chips)] for core in range(2)]
    cells = (ROWS, XC)
    block = f32(*cells)

    zlo, zhi, ylo, yhi, t, c, m = pl.pallas_call(
        edges_kernel,
        out_shape=(
            f32(3, YC, XC),
            f32(3, YC, XC),
            f32(3, ZC, XC),
            f32(3, ZC, XC),
            block,
            block,
            jax.ShapeDtypeStruct(cells, jnp.int32),
        ),
        in_specs=[pl.BlockSpec(memory_space=pltpu.HBM)] * 3,
        scratch_shapes=[pltpu.SemaphoreType.DMA((3,))],
        compiler_params=pltpu.CompilerParams(vmem_limit_bytes=12 * 1024 * 1024),
        name="edges_kernel",
    )(*(pltpu.with_memory_space_constraint(a.reshape(cells), pltpu.HBM) for a in (warmth, cure, label)))
    z_halo = (lax.ppermute(zhi, "gz", up["gz"]), lax.ppermute(zlo, "gz", down["gz"]))
    y_halo = (lax.ppermute(yhi, "gy", up["gy"]), lax.ppermute(ylo, "gy", down["gy"]))

    def gather_y(pay):
        return lax.all_to_all(pay, "gy", 0, 0, tiled=True)

    def gather_z(pay):
        return lax.all_to_all(pay, "gz", 0, 0, tiled=True, axis_index_groups=same_core)

    def share(numbers):
        return lax.all_gather(numbers, "gz", axis_index_groups=pairs)

    sizes = dict(groups_y=groups_y, groups_z=groups_z)
    co_y, side_y = f32(3, YC - 1, ZC, XC), f32(YC - 1, ZC, XC)
    co_z, side_z, num_z = f32(3, ZC - 1, YC, XC), f32(ZC - 1, YC, XC), f32(3, YC, XC)
    x_shape = f32(2 * ROUNDS + 2, ROWS, XC)
    line = (groups_y + 1, ZC, XC)
    message = f32(3 * ZC + 1, XC)

    (x1,) = call(x_kernel, [x_shape])(c, m)
    pay, co_y1, side, co_y2, fluxz, c1, y_entry, toward_south, toward_north = call(
        front_kernel,
        [f32(groups_y, 8 * ZC, XC), co_y, side_y, co_y, block, block, f32(ZC, XC), message, message],
        [cells] * 4 + [(8 * ZC, XC)],
        spread_to=groups_y,
        groups=groups_y,
    )(t, c, m, x1, *z_halo, *y_halo)
    of_south = lax.ppermute(toward_north, "gy", up["gy"])
    of_north = lax.ppermute(toward_south, "gy", down["gy"])
    x2, co_z1, num_z1, co_z2, num_z2, z_entry = call(
        ahead_kernel,
        [x_shape, co_z, num_z, co_z, num_z, f32(YC, XC)],
        groups_z=groups_z,
    )(c, c1, m, *z_halo)
    everyone = gather_y(pay)
    numbers, side, co_wide, side_wide = call(
        middle_kernel,
        [f32(SHARED, XC), side_z, f32(3, ZC - 1, 2, XC), f32(ZC - 1, 2, XC)],
        [line, cells, (3, 2 * ZC + 2, XC)],
        **sizes,
    )(everyone, co_y1, side, fluxz, m, co_z1, num_z1, num_z2, y_entry, of_south, of_north)
    pair = share(numbers)
    (pay,) = call(
        merge_kernel, [f32(chips, 40, XC)], [(40, XC)], spread_to=chips, copies=chips
    )(pair)
    column = gather_z(pay)
    (found,) = call(chain_kernel, [f32(16, XC)], [(chips + 1, WIDTH, XC)], chips=chips)(column)
    pay, side, fluxz, c2 = call(
        turn_kernel,
        [f32(groups_y, 2 * ZC, XC), side_y, block, block],
        [(3, YC, XC), (2, 2, XC), cells, (2 * ZC, XC)] + [cells] * 4 + [(2 * ZC, XC)],
        spread_to=groups_y,
        **sizes,
    )(
        pair,
        share(found),
        co_z1,
        side,
        co_wide,
        side_wide,
        z_entry,
        c1,
        m,
        x2,
        co_y2,
        *z_halo,
        *y_halo,
    )
    numbers, side = call(
        later_middle_kernel, [f32(2 * YC, XC), side_z], [line, cells], groups_y=groups_y
    )(everyone, gather_y(pay), co_y2, side, fluxz, m, co_z2)
    more = share(numbers)
    (pay,) = call(
        later_merge_kernel, [f32(chips, YC, XC)], [(YC, XC)], spread_to=chips, copies=chips
    )(pair, more)
    (found,) = call(
        later_chain_kernel, [f32(YC, XC)], [(chips + 1, HALF, XC)], chips=chips
    )(column, gather_z(pay))
    (t2,) = call(back_kernel, [block], [(2, YC, XC)])(pair, more, share(found), co_z2, side)
    return t2.reshape(warmth.shape), c2.reshape(cure.shape)


def solution(mesh):
    return jax.shard_map(
        body,
        mesh=mesh,
        in_specs=(P("gz", "gy", None),) * 3,
        out_specs=(P("gz", "gy", None),) * 2,
        check_vma=False,
    )
```

```python
import functools

import jax
import jax.numpy as jnp
from jax import lax
from jax.experimental import pallas as pl
from jax.experimental.pallas import tpu as pltpu
from jax.sharding import PartitionSpec as P

ZC = 16
YC = 8
XC = 128
ROWS = ZC * YC


def f32(*shape):
    return jax.ShapeDtypeStruct(shape, jnp.float32)


def conduct_of(label, cure):
    return jnp.where(label == 1, 40.0, jnp.where(label == 2, 20.0, 0.6 + 0.8 * cure))


def store_of(label):
    return jnp.where(label == 1, 3.0 / 60.0, jnp.where(label == 2, 2.0 / 60.0, 1.0 / 60.0))


def store_by(k):
    return jnp.where(k > 30.0, 3.0 / 60.0, jnp.where(k > 10.0, 2.0 / 60.0, 1.0 / 60.0))


def cure_of(label, warmth, cure):
    speed = 0.3 * jnp.exp(8.0 * warmth)
    return jnp.where(label == 0, 1.0 - (1.0 - cure) * jnp.exp(-speed), cure)


def y_rows(y):
    return pl.ds(y, ZC, stride=YC)


def z_rows(z):
    return pl.ds(z * YC, YC)


def edges_kernel(
    t_in, c_in, m_in, zlo_ref, zhi_ref, ylo_ref, yhi_ref, t_ref, c_ref, m_ref, sem
):
    copies = [
        pltpu.make_async_copy(src, dst, sem.at[i])
        for i, (src, dst) in enumerate(((t_in, t_ref), (c_in, c_ref), (m_in, m_ref)))
    ]
    for copy in copies:
        copy.start()
    for copy in copies:
        copy.wait()

    def put(out, rows):
        t, c, m = t_ref[rows, :], c_ref[rows, :], m_ref[rows, :]
        out[0] = t
        out[1] = conduct_of(m, c)
        out[2] = conduct_of(m, cure_of(m, t, c))

    put(zlo_ref, z_rows(0))
    put(zhi_ref, z_rows(ZC - 1))
    put(ylo_ref, y_rows(0))
    put(yhi_ref, y_rows(YC - 1))


def spread(one_ref, out_ref, sem, count):
    copies = [pltpu.make_async_copy(one_ref, out_ref.at[d], sem.at[d]) for d in range(count)]
    for copy in copies:
        copy.start()
    for copy in copies:
        copy.wait()


def reduce_coefficients(count, store, faces, entry, co_ref):
    ground, edge = store(0), entry
    back_ground = None
    for i in range(count - 1):
        face = faces(i)
        inv = 1.0 / (ground + edge + face)
        edge_inv, face_inv = edge * inv, face * inv
        co_ref[0, i] = inv
        co_ref[1, i] = edge_inv
        co_ref[2, i] = face_inv
        more = edge_inv * ground
        back_ground = more if i == 0 else back_ground + more
        ground = store(i + 1) + face_inv * ground
        edge = edge_inv * face
    return back_ground, edge, ground


def reduce_sides(count, right, co_ref, side_ref):
    side = right(0)
    back_side = None
    for i in range(count - 1):
        side_ref[i] = side * co_ref[0, i]
        more = co_ref[1, i] * side
        back_side = more if i == 0 else back_side + more
        side = right(i + 1) + co_ref[2, i] * side
    return side, back_side


def substitute(count, before, own, co_ref, side_ref, put):
    value = own
    put(count - 1, value)
    for i in range(count - 2, -1, -1):
        value = (side_ref[i] + co_ref[1, i] * before) + co_ref[2, i] * value
        put(i, value)


def edge_lanes():
    lane = lax.broadcasted_iota(jnp.int32, (YC, XC), 1)
    return lane == 0, lane == XC - 1


ROUNDS = 7


def x_coefficients(c_ref, m_ref, x_ref):
    first_lane, last_lane = edge_lanes()
    batch = 4
    for z0 in range(0, ZC, batch):
        gs, ls, rs, stores = [], [], [], []
        for z in range(z0, z0 + batch):
            rows = z_rows(z)
            m = m_ref[rows, :]
            k, g = conduct_of(m, c_ref[rows, :]), store_of(m)
            face_left = 0.5 * (k + jnp.where(first_lane, 0.0, pltpu.roll(k, 1, 1)))
            face_right = jnp.where(last_lane, 0.5 * k, pltpu.roll(face_left, XC - 1, 1))
            x_ref[2 * ROUNDS + 1, rows, :] = face_left
            gs.append(
                g
                + jnp.where(first_lane, face_left, 0.0)
                + jnp.where(last_lane, face_right, 0.0)
            )
            ls.append(jnp.where(first_lane, 0.0, face_left))
            rs.append(jnp.where(last_lane, 0.0, face_right))
            stores.append(g)
        for level in range(ROUNDS):
            low, high = 1 << level, XC - (1 << level)
            for b in range(batch):
                rows = z_rows(z0 + b)
                ground, left, right = gs[b], ls[b], rs[b]
                inv = 1.0 / (ground + left + right)
                to_left = left * pltpu.roll(inv, low, 1)
                to_right = right * pltpu.roll(inv, high, 1)
                x_ref[2 * level, rows, :] = to_left
                x_ref[2 * level + 1, rows, :] = to_right
                gs[b] = (
                    ground
                    + to_left * pltpu.roll(ground, low, 1)
                    + to_right * pltpu.roll(ground, high, 1)
                )
                if level + 1 < ROUNDS:
                    ls[b] = to_left * pltpu.roll(left, low, 1)
                    rs[b] = to_right * pltpu.roll(right, high, 1)
        for b in range(batch):
            x_ref[2 * ROUNDS, z_rows(z0 + b), :] = stores[b] / gs[b]


def x_kernel(c_ref, m_ref, x_ref):
    x_coefficients(c_ref, m_ref, x_ref)


def z_coefficients(groups_z, c_ref, m_ref, below, above, co_ref, num_ref):
    ks = [below]
    for z in range(ZC):
        ks.append(conduct_of(m_ref[z_rows(z), :], c_ref[z_rows(z), :]))
    ks.append(above)
    faces = [0.5 * (ks[i] + ks[i + 1]) for i in range(ZC + 1)]
    numbers = reduce_coefficients(
        ZC,
        lambda i: store_of(m_ref[z_rows(i), :]),
        lambda i: faces[i + 1],
        faces[0],
        co_ref,
    )
    num_ref[0] = numbers[0]
    num_ref[1] = numbers[1]
    at_end = lax.axis_index("gz") == groups_z - 1
    num_ref[2] = numbers[2] + jnp.where(at_end, faces[ZC], 0.0)
    return faces[ZC]


def ahead_kernel(
    c_ref,
    next_c_ref,
    m_ref,
    below_ref,
    above_ref,
    x_ref,
    co1_ref,
    num1_ref,
    co2_ref,
    num2_ref,
    entry_ref,
    *,
    groups_z,
):
    x_coefficients(next_c_ref, m_ref, x_ref)
    entry_ref[...] = z_coefficients(
        groups_z, c_ref, m_ref, below_ref[1], above_ref[1], co1_ref, num1_ref
    )
    z_coefficients(groups_z, next_c_ref, m_ref, below_ref[2], above_ref[2], co2_ref, num2_ref)


def flow_rhs(t_ref, c_ref, m_ref, x_ref, zt, yt, zk, yk, outs, scratch):
    fluxz_ref, cure_ref = outs
    k_ref, g_ref, fy_ref, r_ref = scratch
    t, c, m = t_ref[...], c_ref[...], m_ref[...]
    k_ref[...] = conduct_of(m, c)
    g_ref[...] = store_of(m)
    cure_ref[...] = cure_of(m, t, c)

    ks = [yk[0]] + [k_ref[y_rows(y), :] for y in range(YC)] + [yk[1]]
    ts = [yt[0]] + [t_ref[y_rows(y), :] for y in range(YC)] + [yt[1]]
    face_y = [0.5 * (ks[i] + ks[i + 1]) for i in range(YC + 1)]
    flow_y = [face_y[i] * (ts[i + 1] - ts[i]) for i in range(YC + 1)]
    for y in range(YC):
        fy_ref[y_rows(y), :] = flow_y[y + 1] - flow_y[y]

    first_lane, last_lane = edge_lanes()
    k_prev, t_prev = zk[0], zt[0]
    flow_prev = 0.5 * (k_prev + k_ref[z_rows(0), :]) * (t_ref[z_rows(0), :] - t_prev)
    batch = 4
    for z0 in range(0, ZC, batch):
        sides = []
        for z in range(z0, z0 + batch):
            rows = z_rows(z)
            kz, tz = k_ref[rows, :], t_ref[rows, :]
            k_next = k_ref[z_rows(z + 1), :] if z + 1 < ZC else zk[1]
            t_next = t_ref[z_rows(z + 1), :] if z + 1 < ZC else zt[1]
            flow_next = 0.5 * (kz + k_next) * (t_next - tz)
            flux_z = flow_next - flow_prev
            flow_prev = flow_next
            fluxz_ref[rows, :] = flux_z
            t_left = jnp.where(first_lane, 0.0, pltpu.roll(tz, 1, 1))
            flow_left = x_ref[2 * ROUNDS + 1, rows, :] * (tz - t_left)
            flow_right = jnp.where(last_lane, -0.5 * kz * tz, pltpu.roll(flow_left, XC - 1, 1))
            delta = cure_ref[rows, :] - c_ref[rows, :]
            sides.append(
                g_ref[rows, :] * (tz + 0.4 * delta)
                + (flow_right - flow_left)
                + 2.0 * (fy_ref[rows, :] + flux_z)
            )
        for level in range(ROUNDS):
            low, high = 1 << level, XC - (1 << level)
            for b in range(batch):
                rows = z_rows(z0 + b)
                side = sides[b]
                sides[b] = (
                    side
                    + x_ref[2 * level, rows, :] * pltpu.roll(side, low, 1)
                    + x_ref[2 * level + 1, rows, :] * pltpu.roll(side, high, 1)
                )
        for b in range(batch):
            rows = z_rows(z0 + b)
            r_ref[rows, :] = x_ref[2 * ROUNDS, rows, :] * sides[b] - fy_ref[rows, :]
    return face_y


def front_kernel(
    t_ref,
    c_ref,
    m_ref,
    x_ref,
    below_ref,
    above_ref,
    south_ref,
    north_ref,
    pay_ref,
    co1_ref,
    side_ref,
    co2_ref,
    fluxz_ref,
    cure_ref,
    entry_ref,
    k_ref,
    g_ref,
    fy_ref,
    r_ref,
    p_ref,
    sem,
    *,
    groups,
):
    face_y = flow_rhs(
        t_ref,
        c_ref,
        m_ref,
        x_ref,
        (below_ref[0], above_ref[0]),
        (south_ref[0], north_ref[0]),
        (below_ref[1], above_ref[1]),
        (south_ref[1], north_ref[1]),
        (fluxz_ref, cure_ref),
        (k_ref, g_ref, fy_ref, r_ref),
    )
    entry_ref[...] = face_y[YC]
    at_end = lax.axis_index("gy") == groups - 1
    back_ground, edge, ground = reduce_coefficients(
        YC, lambda i: g_ref[y_rows(i), :], lambda i: face_y[i + 1], face_y[0], co1_ref
    )
    ground = ground + jnp.where(at_end, face_y[YC], 0.0)
    side, back_side = reduce_sides(YC, lambda i: r_ref[y_rows(i), :], co1_ref, side_ref)
    for y, row in ((0, 8 * ZC), (YC - 1, 8 * ZC + 4)):
        for i, corner in enumerate((below_ref[0], above_ref[0], below_ref[1], above_ref[1])):
            p_ref[row + i : row + i + 1] = corner[y : y + 1]
    k_ref[...] = conduct_of(m_ref[...], cure_ref[...])
    ks = [south_ref[2]] + [k_ref[y_rows(y), :] for y in range(YC)] + [north_ref[2]]
    faces = [0.5 * (ks[i] + ks[i + 1]) for i in range(YC + 1)]
    back_ground2, edge2, ground2 = reduce_coefficients(
        YC, lambda i: g_ref[y_rows(i), :], lambda i: faces[i + 1], faces[0], co2_ref
    )
    ground2 = ground2 + jnp.where(at_end, faces[YC], 0.0)
    numbers = (back_ground, edge, ground, side, back_side, back_ground2, edge2, ground2)
    for q, number in enumerate(numbers):
        p_ref[ZC * q : ZC * q + ZC] = number
    spread(p_ref, pay_ref, sem, groups)


def chain(count, read, put):
    def ground_of(j):
        return read(j, 2) + read(j + 1, 0) if j + 1 < count else read(j, 2)

    def side_of(j):
        return read(j, 3) + read(j + 1, 4) if j + 1 < count else read(j, 3)

    half = count // 2
    gain, part = [None] * count, [None] * count
    ground_l, side_l = ground_of(0) + read(0, 1), side_of(0)
    ground_r, side_r = ground_of(count - 1), side_of(count - 1)
    for i in range(half - 1):
        edge = read(i + 1, 1)
        inv = 1.0 / (ground_l + edge)
        gain[i], part[i] = edge * inv, side_l * inv
        ground_l = ground_of(i + 1) + gain[i] * ground_l
        side_l = side_of(i + 1) + gain[i] * side_l
        j = count - 1 - i
        edge = read(j, 1)
        inv = 1.0 / (ground_r + edge)
        gain[j], part[j] = edge * inv, side_r * inv
        ground_r = ground_of(j - 1) + gain[j] * ground_r
        side_r = side_of(j - 1) + gain[j] * side_r
    edge = read(half, 1)
    inv = 1.0 / (ground_l * ground_r + edge * (ground_l + ground_r))
    low = (side_l * (ground_r + edge) + edge * side_r) * inv
    high = (side_r * (ground_l + edge) + edge * side_l) * inv
    put(half - 1, low)
    put(half, high)
    for i in range(half - 2, -1, -1):
        low = part[i] + gain[i] * low
        put(i, low)
        j = count - 1 - i
        high = part[j] + gain[j] * high
        put(j, high)


def first_of_next(own, after, back_ground, edge, back_side, entry):
    return own - (back_ground * own + edge * (own - after) - back_side) / entry


def y_solution(groups_y, read, co_ref, side_ref, s_ref, v_ref):
    s_ref[0] = jnp.zeros((ZC, XC), jnp.float32)

    def put(j, value):
        s_ref[j + 1] = value

    chain(groups_y, read, put)
    me = lax.axis_index("gy")

    def place(i, value):
        v_ref[y_rows(i), :] = value

    before, own = s_ref[me], s_ref[me + 1]
    substitute(YC, before, own, co_ref, side_ref, place)
    return before, own


def main_rows(q):
    return pl.ds(YC * q, YC)


def later_rows(q):
    return pl.ds(YC * (5 + q), YC)


def wide_rows(q):
    return pl.ds(8 * YC + 2 * q, 2)


SHARED = 8 * YC + 16


def middle_kernel(
    all_ref,
    co_y_ref,
    side_y_ref,
    fluxz_ref,
    m_ref,
    co_z_ref,
    num1_ref,
    num2_ref,
    y_entry_ref,
    south_ref,
    north_ref,
    p_ref,
    side_z_ref,
    co_wide_ref,
    side_wide_ref,
    s_ref,
    v_ref,
    h_ref,
    *,
    groups_y,
    groups_z,
):
    def read(j, q):
        return all_ref[j, ZC * q : ZC * q + ZC, :]

    before, own = y_solution(groups_y, read, co_y_ref, side_y_ref, s_ref, v_ref)

    def right(i):
        return store_of(m_ref[z_rows(i), :]) * v_ref[z_rows(i), :] - fluxz_ref[z_rows(i), :]

    for q in range(3):
        p_ref[main_rows(q), :] = num1_ref[q]
        p_ref[later_rows(q), :] = num2_ref[q]
    sides = reduce_sides(ZC, right, co_z_ref, side_z_ref)
    p_ref[main_rows(3), :] = sides[0]
    p_ref[main_rows(4), :] = sides[1]

    me = lax.axis_index("gy")
    then = jnp.minimum(me + 1, groups_y - 1)
    north = first_of_next(
        own,
        s_ref[then + 1],
        all_ref[then, 0:16, :],
        all_ref[then, 16:32, :],
        all_ref[then, 64:80, :],
        y_entry_ref[...],
    )
    last = jnp.maximum(me - 1, 0)
    beside = (
        (0, before, south_ref, all_ref[last, 8 * ZC + 4 : 8 * ZC + 8, :]),
        (1, north, north_ref, all_ref[then, 8 * ZC : 8 * ZC + 4, :]),
    )
    for side, value, halo_ref, corners in beside:
        rows = pl.ds(2 + side, ZC, stride=2)
        for q in range(2):
            h_ref[q, rows, :] = halo_ref[q]
            h_ref[q, side : side + 1, :] = corners[2 * q : 2 * q + 1]
            h_ref[q, 34 + side : 35 + side, :] = corners[2 * q + 1 : 2 * q + 2]
        h_ref[2, rows, :] = value
    faces = 0.5 * (h_ref[1, 0:34, :] + h_ref[1, 2:36, :])
    h_ref[3, 0:34, :] = faces
    h_ref[4, 0:34, :] = faces * (h_ref[0, 2:36, :] - h_ref[0, 0:34, :])
    capacity = store_by(h_ref[1, 2:34, :])
    h_ref[5, 0:32, :] = capacity
    h_ref[6, 0:32, :] = capacity * h_ref[2, 2:34, :] - (h_ref[4, 2:34, :] - h_ref[4, 0:32, :])
    numbers = reduce_coefficients(
        ZC,
        lambda i: h_ref[5, 2 * i : 2 * i + 2, :],
        lambda i: h_ref[3, 2 * i + 2 : 2 * i + 4, :],
        h_ref[3, 0:2, :],
        co_wide_ref,
    )
    sides = reduce_sides(
        ZC, lambda i: h_ref[6, 2 * i : 2 * i + 2, :], co_wide_ref, side_wide_ref
    )
    at_end = lax.axis_index("gz") == groups_z - 1
    p_ref[8 * YC + 8 :, :] = jnp.zeros((8, XC), jnp.float32)
    p_ref[wide_rows(0), :] = numbers[0]
    p_ref[wide_rows(1), :] = numbers[1]
    p_ref[wide_rows(2), :] = numbers[2] + jnp.where(at_end, h_ref[3, 32:34, :], 0.0)
    p_ref[wide_rows(3), :] = sides[0]
    p_ref[wide_rows(4), :] = sides[1]


def later_middle_kernel(
    all_ref,
    more_ref,
    co_y_ref,
    side_y_ref,
    fluxz_ref,
    m_ref,
    co_z_ref,
    p_ref,
    side_z_ref,
    s_ref,
    v_ref,
    *,
    groups_y,
):
    def read(j, q):
        if q < 3:
            return all_ref[j, ZC * (5 + q) : ZC * (6 + q), :]
        return more_ref[j, ZC * (q - 3) : ZC * (q - 2), :]

    y_solution(groups_y, read, co_y_ref, side_y_ref, s_ref, v_ref)

    def right(i):
        return store_of(m_ref[z_rows(i), :]) * v_ref[z_rows(i), :] - fluxz_ref[z_rows(i), :]

    sides = reduce_sides(ZC, right, co_z_ref, side_z_ref)
    p_ref[0:YC] = sides[0]
    p_ref[YC : 2 * YC] = sides[1]


HALF = YC // 2
WIDTH = HALF + 1


def node_between(low, high):
    ground = low[2] + high[0]
    return ground, 1.0 / (ground + low[1] + high[1])


def merged_coefficients(low, high):
    ground, inv = node_between(low, high)
    low_inv, high_inv = low[1] * inv, high[1] * inv
    return low[0] + low_inv * ground, low_inv * high[1], high[2] + high_inv * ground


def merged_sides(low, high):
    _, inv = node_between(low, high)
    side = low[3] + high[4]
    return high[3] + high[1] * inv * side, low[4] + low[1] * inv * side


def first_numbers(pair_ref, rows):
    return [[pair_ref[core, rows(q), :] for q in range(5)] for core in range(2)]


def later_numbers(pair_ref, more_ref):
    return [
        [pair_ref[core, later_rows(q), :] for q in range(3)]
        + [more_ref[core, main_rows(q), :] for q in range(2)]
        for core in range(2)
    ]


def my_half(number):
    half = number.shape[0] // 2
    core = lax.rem(lax.axis_index("gz"), 2)
    return jnp.where(core == 0, number[:half], number[half:])


def merge_kernel(pair_ref, pay_ref, p_ref, sem, *, copies):
    p_ref[32:40] = jnp.zeros((8, XC), jnp.float32)
    low, high = first_numbers(pair_ref, main_rows)
    for q, number in enumerate(merged_coefficients(low, high) + merged_sides(low, high)):
        p_ref[WIDTH * q : WIDTH * q + HALF] = my_half(number)
    low, high = first_numbers(pair_ref, wide_rows)
    for q, number in enumerate(merged_coefficients(low, high) + merged_sides(low, high)):
        p_ref[WIDTH * q + HALF : WIDTH * q + WIDTH] = my_half(number)
    low, high = ([pair_ref[core, later_rows(q), :] for q in range(3)] for core in range(2))
    for q, number in enumerate(merged_coefficients(low, high)):
        row = 5 * WIDTH + HALF * q
        p_ref[row : row + HALF] = my_half(number)
    spread(p_ref, pay_ref, sem, copies)


def later_merge_kernel(pair_ref, more_ref, pay_ref, p_ref, sem, *, copies):
    low, high = later_numbers(pair_ref, more_ref)
    for q, number in enumerate(merged_sides(low, high)):
        p_ref[HALF * q : HALF * q + HALF] = my_half(number)
    spread(p_ref, pay_ref, sem, copies)


def chain_kernel(all_ref, out_ref, s_ref, *, chips):
    s_ref[0] = jnp.zeros((WIDTH, XC), jnp.float32)

    def put(j, value):
        s_ref[j + 1] = value

    chain(chips, lambda j, q: all_ref[j, WIDTH * q : WIDTH * q + WIDTH, :], put)
    me = lax.div(lax.axis_index("gz"), 2)
    then = jnp.minimum(me + 1, chips - 1)
    own, after = s_ref[me + 1], s_ref[then + 1]
    numbers = [all_ref[then, WIDTH * q : WIDTH * q + WIDTH, :] for q in (0, 1, 4)]
    out_ref[8:16] = jnp.zeros((8, XC), jnp.float32)
    out_ref[0:WIDTH] = s_ref[me]
    out_ref[WIDTH : 2 * WIDTH] = own
    out_ref[2 * WIDTH : 3 * WIDTH] = numbers[0] * own + numbers[1] * (own - after) - numbers[2]


def later_chain_kernel(all_ref, more_ref, out_ref, s_ref, *, chips):
    s_ref[0] = jnp.zeros((HALF, XC), jnp.float32)

    def put(j, value):
        s_ref[j + 1] = value

    def read(j, q):
        if q < 3:
            return all_ref[j, 5 * WIDTH + HALF * q : 5 * WIDTH + HALF * (q + 1), :]
        return more_ref[j, HALF * (q - 3) : HALF * (q - 2), :]

    chain(chips, read, put)
    me = lax.div(lax.axis_index("gz"), 2)
    out_ref[0:HALF] = s_ref[me]
    out_ref[HALF : 2 * HALF] = s_ref[me + 1]


def ends_of(low, high, before, last):
    _, inv = node_between(low, high)
    node = (low[3] + high[4] + low[1] * before + high[1] * last) * inv
    upper = lax.rem(lax.axis_index("gz"), 2) == 1
    return jnp.where(upper, node, before), jnp.where(upper, last, node), node


def joined(res_ref, u_ref, width, count):
    for q in range(count):
        for core in range(2):
            rows = pl.ds(HALF * core, HALF)
            u_ref[q, rows, :] = res_ref[core, width * q : width * q + HALF, :]


def back_kernel(pair_ref, more_ref, res_ref, co_z_ref, side_z_ref, t_ref, u_ref):
    joined(res_ref, u_ref, HALF, 2)
    low, high = later_numbers(pair_ref, more_ref)
    before, own, _ = ends_of(low, high, u_ref[0], u_ref[1])

    def place(i, value):
        t_ref[z_rows(i), :] = value

    substitute(ZC, before, own, co_z_ref, side_z_ref, place)


def turn_kernel(
    pair_ref,
    res_ref,
    co_z_ref,
    side_z_ref,
    co_wide_ref,
    side_wide_ref,
    z_entry_ref,
    c_ref,
    m_ref,
    x_ref,
    co_y_ref,
    below_ref,
    above_ref,
    south_ref,
    north_ref,
    pay_ref,
    side_y_ref,
    fluxz_ref,
    cure_ref,
    u_ref,
    w_ref,
    t_ref,
    e_ref,
    k_ref,
    g_ref,
    fy_ref,
    r_ref,
    p_ref,
    sem,
    *,
    groups_y,
    groups_z,
):
    joined(res_ref, u_ref, WIDTH, 3)
    low, high = first_numbers(pair_ref, main_rows)
    last = u_ref[1]
    before, own, node = ends_of(low, high, u_ref[0], last)

    def place(i, value):
        t_ref[z_rows(i), :] = value

    substitute(ZC, before, own, co_z_ref, side_z_ref, place)
    me = lax.axis_index("gz")
    inside = high[0] * node + high[1] * (node - last) - high[4]
    current = jnp.where(lax.rem(me, 2) == 1, u_ref[2], inside)
    above = jnp.where(me == groups_z - 1, 0.0, own - current / z_entry_ref[...])

    for q in range(2):
        for core in range(2):
            row = WIDTH * q + HALF
            w_ref[q, core : core + 1] = res_ref[core, row : row + 1, :]
    low, high = first_numbers(pair_ref, wide_rows)
    before_wide, own_wide, _ = ends_of(low, high, w_ref[0], w_ref[1])

    def place_wide(i, value):
        e_ref[2 * i : 2 * i + 2] = value

    substitute(ZC, before_wide, own_wide, co_wide_ref, side_wide_ref, place_wide)
    row = lax.axis_index("gy")
    south = jnp.where(row == 0, 0.0, e_ref[pl.ds(0, ZC, stride=2), :])
    north = jnp.where(row == groups_y - 1, 0.0, e_ref[pl.ds(1, ZC, stride=2), :])
    flow_rhs(
        t_ref,
        c_ref,
        m_ref,
        x_ref,
        (before, above),
        (south, north),
        (below_ref[2], above_ref[2]),
        (south_ref[2], north_ref[2]),
        (fluxz_ref, cure_ref),
        (k_ref, g_ref, fy_ref, r_ref),
    )
    side, back_side = reduce_sides(YC, lambda i: r_ref[y_rows(i), :], co_y_ref, side_y_ref)
    p_ref[0:ZC] = side
    p_ref[ZC : 2 * ZC] = back_side
    spread(p_ref, pay_ref, sem, groups_y)


def call(kernel, outs, scratch=(), spread_to=0, **static):
    out_specs = [pl.BlockSpec(memory_space=pltpu.VMEM)] * len(outs)
    shapes = [pltpu.VMEM(shape, jnp.float32) for shape in scratch]
    if spread_to:
        out_specs[0] = pl.BlockSpec(memory_space=pl.ANY)
        shapes.append(pltpu.SemaphoreType.DMA((spread_to,)))
    return pl.pallas_call(
        functools.partial(kernel, **static),
        out_shape=tuple(outs),
        out_specs=tuple(out_specs),
        scratch_shapes=shapes,
        compiler_params=pltpu.CompilerParams(vmem_limit_bytes=12 * 1024 * 1024),
        name=kernel.__name__,
    )


def body(warmth, cure, label):
    groups_z, groups_y = lax.axis_size("gz"), lax.axis_size("gy")
    chips = groups_z // 2
    up = {a: [(i, i + 1) for i in range(n - 1)] for a, n in (("gz", groups_z), ("gy", groups_y))}
    down = {a: [(j, i) for i, j in up[a]] for a in up}
    pairs = [[2 * i, 2 * i + 1] for i in range(chips)]
    same_core = [[2 * i + core for i in range(chips)] for core in range(2)]
    cells = (ROWS, XC)
    block = f32(*cells)

    zlo, zhi, ylo, yhi, t, c, m = pl.pallas_call(
        edges_kernel,
        out_shape=(
            f32(3, YC, XC),
            f32(3, YC, XC),
            f32(3, ZC, XC),
            f32(3, ZC, XC),
            block,
            block,
            jax.ShapeDtypeStruct(cells, jnp.int32),
        ),
        in_specs=[pl.BlockSpec(memory_space=pltpu.HBM)] * 3,
        scratch_shapes=[pltpu.SemaphoreType.DMA((3,))],
        compiler_params=pltpu.CompilerParams(vmem_limit_bytes=12 * 1024 * 1024),
        name="edges_kernel",
    )(*(pltpu.with_memory_space_constraint(a.reshape(cells), pltpu.HBM) for a in (warmth, cure, label)))
    z_halo = (lax.ppermute(zhi, "gz", up["gz"]), lax.ppermute(zlo, "gz", down["gz"]))
    y_halo = (lax.ppermute(yhi, "gy", up["gy"]), lax.ppermute(ylo, "gy", down["gy"]))

    def gather_y(pay):
        return lax.all_to_all(pay, "gy", 0, 0, tiled=True)

    def gather_z(pay):
        return lax.all_to_all(pay, "gz", 0, 0, tiled=True, axis_index_groups=same_core)

    def share(numbers):
        return lax.all_gather(numbers, "gz", axis_index_groups=pairs)

    sizes = dict(groups_y=groups_y, groups_z=groups_z)
    co_y, side_y = f32(3, YC - 1, ZC, XC), f32(YC - 1, ZC, XC)
    co_z, side_z, num_z = f32(3, ZC - 1, YC, XC), f32(ZC - 1, YC, XC), f32(3, YC, XC)
    x_shape = f32(2 * ROUNDS + 2, ROWS, XC)
    line = (groups_y + 1, ZC, XC)

    (x1,) = call(x_kernel, [x_shape])(c, m)
    pay, co_y1, side, co_y2, fluxz, c1, y_entry = call(
        front_kernel,
        [f32(groups_y, 8 * ZC + 8, XC), co_y, side_y, co_y, block, block, f32(ZC, XC)],
        [cells] * 4 + [(8 * ZC + 8, XC)],
        spread_to=groups_y,
        groups=groups_y,
    )(t, c, m, x1, *z_halo, *y_halo)
    x2, co_z1, num_z1, co_z2, num_z2, z_entry = call(
        ahead_kernel,
        [x_shape, co_z, num_z, co_z, num_z, f32(YC, XC)],
        groups_z=groups_z,
    )(c, c1, m, *z_halo)
    everyone = gather_y(pay)
    numbers, side, co_wide, side_wide = call(
        middle_kernel,
        [f32(SHARED, XC), side_z, f32(3, ZC - 1, 2, XC), f32(ZC - 1, 2, XC)],
        [line, cells, (7, 40, XC)],
        **sizes,
    )(everyone, co_y1, side, fluxz, m, co_z1, num_z1, num_z2, y_entry, *y_halo)
    pair = share(numbers)
    (pay,) = call(
        merge_kernel, [f32(chips, 40, XC)], [(40, XC)], spread_to=chips, copies=chips
    )(pair)
    column = gather_z(pay)
    (found,) = call(chain_kernel, [f32(16, XC)], [(chips + 1, WIDTH, XC)], chips=chips)(column)
    pay, side, fluxz, c2 = call(
        turn_kernel,
        [f32(groups_y, 2 * ZC, XC), side_y, block, block],
        [(3, YC, XC), (2, 2, XC), cells, (2 * ZC, XC)] + [cells] * 4 + [(2 * ZC, XC)],
        spread_to=groups_y,
        **sizes,
    )(
        pair,
        share(found),
        co_z1,
        side,
        co_wide,
        side_wide,
        z_entry,
        c1,
        m,
        x2,
        co_y2,
        *z_halo,
        *y_halo,
    )
    numbers, side = call(
        later_middle_kernel, [f32(2 * YC, XC), side_z], [line, cells], groups_y=groups_y
    )(everyone, gather_y(pay), co_y2, side, fluxz, m, co_z2)
    more = share(numbers)
    (pay,) = call(
        later_merge_kernel, [f32(chips, YC, XC)], [(YC, XC)], spread_to=chips, copies=chips
    )(pair, more)
    (found,) = call(
        later_chain_kernel, [f32(YC, XC)], [(chips + 1, HALF, XC)], chips=chips
    )(column, gather_z(pay))
    (t2,) = call(back_kernel, [block], [(2, YC, XC)])(pair, more, share(found), co_z2, side)
    return t2.reshape(warmth.shape), c2.reshape(cure.shape)


def solution(mesh):
    return jax.shard_map(
        body,
        mesh=mesh,
        in_specs=(P("gz", "gy", None),) * 3,
        out_specs=(P("gz", "gy", None),) * 2,
        check_vma=False,
    )
```

```python
import functools

import jax
import jax.numpy as jnp
from jax import lax
from jax.experimental import pallas as pl
from jax.experimental.pallas import tpu as pltpu
from jax.sharding import PartitionSpec as P

ZC = 16
YC = 8
XC = 128
ROWS = ZC * YC


def f32(*shape):
    return jax.ShapeDtypeStruct(shape, jnp.float32)


def conduct_of(label, cure):
    return jnp.where(label == 1, 40.0, jnp.where(label == 2, 20.0, 0.6 + 0.8 * cure))


def store_of(label):
    return jnp.where(label == 1, 3.0 / 60.0, jnp.where(label == 2, 2.0 / 60.0, 1.0 / 60.0))


def store_by(k):
    return jnp.where(k > 30.0, 3.0 / 60.0, jnp.where(k > 10.0, 2.0 / 60.0, 1.0 / 60.0))


def cure_of(label, warmth, cure):
    speed = 0.3 * jnp.exp(8.0 * warmth)
    return jnp.where(label == 0, 1.0 - (1.0 - cure) * jnp.exp(-speed), cure)


def y_rows(y):
    return pl.ds(y, ZC, stride=YC)


def z_rows(z):
    return pl.ds(z * YC, YC)


def edges_kernel(
    t_in, c_in, m_in, zlo_ref, zhi_ref, ylo_ref, yhi_ref, t_ref, c_ref, m_ref, sem
):
    copies = [
        pltpu.make_async_copy(src, dst, sem.at[i])
        for i, (src, dst) in enumerate(((t_in, t_ref), (c_in, c_ref), (m_in, m_ref)))
    ]
    for copy in copies:
        copy.start()
    for copy in copies:
        copy.wait()

    def put(out, rows):
        t, c, m = t_ref[rows, :], c_ref[rows, :], m_ref[rows, :]
        out[0] = t
        out[1] = conduct_of(m, c)
        out[2] = conduct_of(m, cure_of(m, t, c))

    put(zlo_ref, z_rows(0))
    put(zhi_ref, z_rows(ZC - 1))
    put(ylo_ref, y_rows(0))
    put(yhi_ref, y_rows(YC - 1))


def spread(one_ref, out_ref, sem, count):
    copies = [pltpu.make_async_copy(one_ref, out_ref.at[d], sem.at[d]) for d in range(count)]
    for copy in copies:
        copy.start()
    for copy in copies:
        copy.wait()


def reduce_coefficients(count, store, faces, entry, co_ref):
    ground, edge = store(0), entry
    back_ground = None
    for i in range(count - 1):
        face = faces(i)
        inv = 1.0 / (ground + edge + face)
        edge_inv, face_inv = edge * inv, face * inv
        co_ref[0, i] = inv
        co_ref[1, i] = edge_inv
        co_ref[2, i] = face_inv
        more = edge_inv * ground
        back_ground = more if i == 0 else back_ground + more
        ground = store(i + 1) + face_inv * ground
        edge = edge_inv * face
    return back_ground, edge, ground


def reduce_sides(count, right, co_ref, side_ref):
    side = right(0)
    back_side = None
    for i in range(count - 1):
        side_ref[i] = side * co_ref[0, i]
        more = co_ref[1, i] * side
        back_side = more if i == 0 else back_side + more
        side = right(i + 1) + co_ref[2, i] * side
    return side, back_side


def substitute(count, before, own, co_ref, side_ref, put):
    value = own
    put(count - 1, value)
    for i in range(count - 2, -1, -1):
        value = (side_ref[i] + co_ref[1, i] * before) + co_ref[2, i] * value
        put(i, value)


def edge_lanes():
    lane = lax.broadcasted_iota(jnp.int32, (YC, XC), 1)
    return lane == 0, lane == XC - 1


ROUNDS = 7


def x_coefficients(c_ref, m_ref, x_ref):
    first_lane, last_lane = edge_lanes()
    batch = 4
    for z0 in range(0, ZC, batch):
        gs, ls, rs, stores = [], [], [], []
        for z in range(z0, z0 + batch):
            rows = z_rows(z)
            m = m_ref[rows, :]
            k, g = conduct_of(m, c_ref[rows, :]), store_of(m)
            face_left = 0.5 * (k + jnp.where(first_lane, 0.0, pltpu.roll(k, 1, 1)))
            face_right = jnp.where(last_lane, 0.5 * k, pltpu.roll(face_left, XC - 1, 1))
            x_ref[2 * ROUNDS + 1, rows, :] = face_left
            gs.append(
                g
                + jnp.where(first_lane, face_left, 0.0)
                + jnp.where(last_lane, face_right, 0.0)
            )
            ls.append(jnp.where(first_lane, 0.0, face_left))
            rs.append(jnp.where(last_lane, 0.0, face_right))
            stores.append(g)
        for level in range(ROUNDS):
            low, high = 1 << level, XC - (1 << level)
            for b in range(batch):
                rows = z_rows(z0 + b)
                ground, left, right = gs[b], ls[b], rs[b]
                inv = 1.0 / (ground + left + right)
                to_left = left * pltpu.roll(inv, low, 1)
                to_right = right * pltpu.roll(inv, high, 1)
                x_ref[2 * level, rows, :] = to_left
                x_ref[2 * level + 1, rows, :] = to_right
                gs[b] = (
                    ground
                    + to_left * pltpu.roll(ground, low, 1)
                    + to_right * pltpu.roll(ground, high, 1)
                )
                if level + 1 < ROUNDS:
                    ls[b] = to_left * pltpu.roll(left, low, 1)
                    rs[b] = to_right * pltpu.roll(right, high, 1)
        for b in range(batch):
            x_ref[2 * ROUNDS, z_rows(z0 + b), :] = stores[b] / gs[b]


def x_kernel(c_ref, m_ref, x_ref):
    x_coefficients(c_ref, m_ref, x_ref)


def z_coefficients(groups_z, c_ref, m_ref, below, above, co_ref, num_ref, row):
    ks = [below]
    for z in range(ZC):
        ks.append(conduct_of(m_ref[z_rows(z), :], c_ref[z_rows(z), :]))
    ks.append(above)
    faces = [0.5 * (ks[i] + ks[i + 1]) for i in range(ZC + 1)]
    numbers = reduce_coefficients(
        ZC,
        lambda i: store_of(m_ref[z_rows(i), :]),
        lambda i: faces[i + 1],
        faces[0],
        co_ref,
    )
    at_end = lax.axis_index("gz") == groups_z - 1
    num_ref[row : row + YC] = numbers[0]
    num_ref[row + YC : row + 2 * YC] = numbers[1]
    num_ref[row + 2 * YC : row + 3 * YC] = numbers[2] + jnp.where(at_end, faces[ZC], 0.0)
    return faces[ZC]


def ahead_kernel(
    c_ref,
    next_c_ref,
    m_ref,
    below_ref,
    above_ref,
    x_ref,
    co1_ref,
    co2_ref,
    num_ref,
    entry_ref,
    *,
    groups_z,
):
    x_coefficients(next_c_ref, m_ref, x_ref)
    entry_ref[...] = z_coefficients(
        groups_z, c_ref, m_ref, below_ref[1], above_ref[1], co1_ref, num_ref, 0
    )
    z_coefficients(
        groups_z, next_c_ref, m_ref, below_ref[2], above_ref[2], co2_ref, num_ref, 3 * YC
    )


def flow_rhs(t_ref, c_ref, m_ref, x_ref, zt, yt, zk, yk, outs, scratch):
    fluxz_ref, cure_ref = outs
    k_ref, g_ref, fy_ref, r_ref = scratch
    t, c, m = t_ref[...], c_ref[...], m_ref[...]
    k_ref[...] = conduct_of(m, c)
    g_ref[...] = store_of(m)
    cure_ref[...] = cure_of(m, t, c)

    ks = [yk[0]] + [k_ref[y_rows(y), :] for y in range(YC)] + [yk[1]]
    ts = [yt[0]] + [t_ref[y_rows(y), :] for y in range(YC)] + [yt[1]]
    face_y = [0.5 * (ks[i] + ks[i + 1]) for i in range(YC + 1)]
    flow_y = [face_y[i] * (ts[i + 1] - ts[i]) for i in range(YC + 1)]
    for y in range(YC):
        fy_ref[y_rows(y), :] = flow_y[y + 1] - flow_y[y]

    first_lane, last_lane = edge_lanes()
    k_prev, t_prev = zk[0], zt[0]
    flow_prev = 0.5 * (k_prev + k_ref[z_rows(0), :]) * (t_ref[z_rows(0), :] - t_prev)
    batch = 4
    for z0 in range(0, ZC, batch):
        sides = []
        for z in range(z0, z0 + batch):
            rows = z_rows(z)
            kz, tz = k_ref[rows, :], t_ref[rows, :]
            k_next = k_ref[z_rows(z + 1), :] if z + 1 < ZC else zk[1]
            t_next = t_ref[z_rows(z + 1), :] if z + 1 < ZC else zt[1]
            flow_next = 0.5 * (kz + k_next) * (t_next - tz)
            flux_z = flow_next - flow_prev
            flow_prev = flow_next
            fluxz_ref[rows, :] = flux_z
            t_left = jnp.where(first_lane, 0.0, pltpu.roll(tz, 1, 1))
            flow_left = x_ref[2 * ROUNDS + 1, rows, :] * (tz - t_left)
            flow_right = jnp.where(last_lane, -0.5 * kz * tz, pltpu.roll(flow_left, XC - 1, 1))
            delta = cure_ref[rows, :] - c_ref[rows, :]
            sides.append(
                g_ref[rows, :] * (tz + 0.4 * delta)
                + (flow_right - flow_left)
                + 2.0 * (fy_ref[rows, :] + flux_z)
            )
        for level in range(ROUNDS):
            low, high = 1 << level, XC - (1 << level)
            for b in range(batch):
                rows = z_rows(z0 + b)
                side = sides[b]
                sides[b] = (
                    side
                    + x_ref[2 * level, rows, :] * pltpu.roll(side, low, 1)
                    + x_ref[2 * level + 1, rows, :] * pltpu.roll(side, high, 1)
                )
        for b in range(batch):
            rows = z_rows(z0 + b)
            r_ref[rows, :] = x_ref[2 * ROUNDS, rows, :] * sides[b] - fy_ref[rows, :]
    return face_y


def front_kernel(
    t_ref,
    c_ref,
    m_ref,
    x_ref,
    below_ref,
    above_ref,
    south_ref,
    north_ref,
    pay_ref,
    co1_ref,
    side_ref,
    co2_ref,
    fluxz_ref,
    cure_ref,
    entry_ref,
    k_ref,
    g_ref,
    fy_ref,
    r_ref,
    p_ref,
    sem,
    *,
    groups,
):
    face_y = flow_rhs(
        t_ref,
        c_ref,
        m_ref,
        x_ref,
        (below_ref[0], above_ref[0]),
        (south_ref[0], north_ref[0]),
        (below_ref[1], above_ref[1]),
        (south_ref[1], north_ref[1]),
        (fluxz_ref, cure_ref),
        (k_ref, g_ref, fy_ref, r_ref),
    )
    entry_ref[...] = face_y[YC]
    at_end = lax.axis_index("gy") == groups - 1
    back_ground, edge, ground = reduce_coefficients(
        YC, lambda i: g_ref[y_rows(i), :], lambda i: face_y[i + 1], face_y[0], co1_ref
    )
    ground = ground + jnp.where(at_end, face_y[YC], 0.0)
    side, back_side = reduce_sides(YC, lambda i: r_ref[y_rows(i), :], co1_ref, side_ref)
    for y, row in ((0, 8 * ZC), (YC - 1, 8 * ZC + 4)):
        for i, corner in enumerate((below_ref[0], above_ref[0], below_ref[1], above_ref[1])):
            p_ref[row + i : row + i + 1] = corner[y : y + 1]
    k_ref[...] = conduct_of(m_ref[...], cure_ref[...])
    ks = [south_ref[2]] + [k_ref[y_rows(y), :] for y in range(YC)] + [north_ref[2]]
    faces = [0.5 * (ks[i] + ks[i + 1]) for i in range(YC + 1)]
    back_ground2, edge2, ground2 = reduce_coefficients(
        YC, lambda i: g_ref[y_rows(i), :], lambda i: faces[i + 1], faces[0], co2_ref
    )
    ground2 = ground2 + jnp.where(at_end, faces[YC], 0.0)
    numbers = (back_ground, edge, ground, side, back_side, back_ground2, edge2, ground2)
    for q, number in enumerate(numbers):
        p_ref[ZC * q : ZC * q + ZC] = number
    spread(p_ref, pay_ref, sem, groups)


def chain(count, read, put):
    def ground_of(j):
        return read(j, 2) + read(j + 1, 0) if j + 1 < count else read(j, 2)

    def side_of(j):
        return read(j, 3) + read(j + 1, 4) if j + 1 < count else read(j, 3)

    half = count // 2
    gain, part = [None] * count, [None] * count
    ground_l, side_l = ground_of(0) + read(0, 1), side_of(0)
    ground_r, side_r = ground_of(count - 1), side_of(count - 1)
    for i in range(half - 1):
        edge = read(i + 1, 1)
        inv = 1.0 / (ground_l + edge)
        gain[i], part[i] = edge * inv, side_l * inv
        ground_l = ground_of(i + 1) + gain[i] * ground_l
        side_l = side_of(i + 1) + gain[i] * side_l
        j = count - 1 - i
        edge = read(j, 1)
        inv = 1.0 / (ground_r + edge)
        gain[j], part[j] = edge * inv, side_r * inv
        ground_r = ground_of(j - 1) + gain[j] * ground_r
        side_r = side_of(j - 1) + gain[j] * side_r
    edge = read(half, 1)
    inv = 1.0 / (ground_l * ground_r + edge * (ground_l + ground_r))
    low = (side_l * (ground_r + edge) + edge * side_r) * inv
    high = (side_r * (ground_l + edge) + edge * side_l) * inv
    put(half - 1, low)
    put(half, high)
    for i in range(half - 2, -1, -1):
        low = part[i] + gain[i] * low
        put(i, low)
        j = count - 1 - i
        high = part[j] + gain[j] * high
        put(j, high)


def first_of_next(own, after, back_ground, edge, back_side, entry):
    return own - (back_ground * own + edge * (own - after) - back_side) / entry


def y_solution(groups_y, read, co_ref, side_ref, s_ref, v_ref):
    s_ref[0] = jnp.zeros((ZC, XC), jnp.float32)

    def put(j, value):
        s_ref[j + 1] = value

    chain(groups_y, read, put)
    me = lax.axis_index("gy")

    def place(i, value):
        v_ref[y_rows(i), :] = value

    before, own = s_ref[me], s_ref[me + 1]
    substitute(YC, before, own, co_ref, side_ref, place)
    return before, own


def block_rows(q):
    return pl.ds(YC * q, YC)


def wide_rows(q):
    return pl.ds(2 * YC + 2 * q, 2)


def middle_kernel(
    all_ref,
    co_y_ref,
    side_y_ref,
    fluxz_ref,
    m_ref,
    co_z_ref,
    y_entry_ref,
    south_ref,
    north_ref,
    p_ref,
    side_z_ref,
    co_wide_ref,
    side_wide_ref,
    s_ref,
    v_ref,
    h_ref,
    *,
    groups_y,
    groups_z,
):
    def read(j, q):
        return all_ref[j, ZC * q : ZC * q + ZC, :]

    before, own = y_solution(groups_y, read, co_y_ref, side_y_ref, s_ref, v_ref)

    def right(i):
        return store_of(m_ref[z_rows(i), :]) * v_ref[z_rows(i), :] - fluxz_ref[z_rows(i), :]

    sides = reduce_sides(ZC, right, co_z_ref, side_z_ref)
    p_ref[24:32, :] = jnp.zeros((8, XC), jnp.float32)
    p_ref[block_rows(0), :] = sides[0]
    p_ref[block_rows(1), :] = sides[1]

    me = lax.axis_index("gy")
    then = jnp.minimum(me + 1, groups_y - 1)
    north = first_of_next(
        own,
        s_ref[then + 1],
        all_ref[then, 0:16, :],
        all_ref[then, 16:32, :],
        all_ref[then, 64:80, :],
        y_entry_ref[...],
    )
    last = jnp.maximum(me - 1, 0)
    beside = (
        (0, before, south_ref, all_ref[last, 8 * ZC + 4 : 8 * ZC + 8, :]),
        (1, north, north_ref, all_ref[then, 8 * ZC : 8 * ZC + 4, :]),
    )
    for side, value, halo_ref, corners in beside:
        rows = pl.ds(2 + side, ZC, stride=2)
        for q in range(2):
            h_ref[q, rows, :] = halo_ref[q]
            h_ref[q, side : side + 1, :] = corners[2 * q : 2 * q + 1]
            h_ref[q, 34 + side : 35 + side, :] = corners[2 * q + 1 : 2 * q + 2]
        h_ref[2, rows, :] = value
    faces = 0.5 * (h_ref[1, 0:34, :] + h_ref[1, 2:36, :])
    h_ref[3, 0:34, :] = faces
    h_ref[4, 0:34, :] = faces * (h_ref[0, 2:36, :] - h_ref[0, 0:34, :])
    capacity = store_by(h_ref[1, 2:34, :])
    h_ref[5, 0:32, :] = capacity
    h_ref[6, 0:32, :] = capacity * h_ref[2, 2:34, :] - (h_ref[4, 2:34, :] - h_ref[4, 0:32, :])
    numbers = reduce_coefficients(
        ZC,
        lambda i: h_ref[5, 2 * i : 2 * i + 2, :],
        lambda i: h_ref[3, 2 * i + 2 : 2 * i + 4, :],
        h_ref[3, 0:2, :],
        co_wide_ref,
    )
    sides = reduce_sides(
        ZC, lambda i: h_ref[6, 2 * i : 2 * i + 2, :], co_wide_ref, side_wide_ref
    )
    at_end = lax.axis_index("gz") == groups_z - 1
    p_ref[wide_rows(0), :] = numbers[0]
    p_ref[wide_rows(1), :] = numbers[1]
    p_ref[wide_rows(2), :] = numbers[2] + jnp.where(at_end, h_ref[3, 32:34, :], 0.0)
    p_ref[wide_rows(3), :] = sides[0]
    p_ref[wide_rows(4), :] = sides[1]


def later_middle_kernel(
    all_ref,
    more_ref,
    co_y_ref,
    side_y_ref,
    fluxz_ref,
    m_ref,
    co_z_ref,
    p_ref,
    side_z_ref,
    s_ref,
    v_ref,
    *,
    groups_y,
):
    def read(j, q):
        if q < 3:
            return all_ref[j, ZC * (5 + q) : ZC * (6 + q), :]
        return more_ref[j, ZC * (q - 3) : ZC * (q - 2), :]

    y_solution(groups_y, read, co_y_ref, side_y_ref, s_ref, v_ref)

    def right(i):
        return store_of(m_ref[z_rows(i), :]) * v_ref[z_rows(i), :] - fluxz_ref[z_rows(i), :]

    sides = reduce_sides(ZC, right, co_z_ref, side_z_ref)
    p_ref[0:YC] = sides[0]
    p_ref[YC : 2 * YC] = sides[1]


HALF = YC // 2


def node_between(low, high):
    ground = low[2] + high[0]
    return ground, 1.0 / (ground + low[1] + high[1])


def merged_coefficients(low, high):
    ground, inv = node_between(low, high)
    low_inv, high_inv = low[1] * inv, high[1] * inv
    return low[0] + low_inv * ground, low_inv * high[1], high[2] + high_inv * ground


def merged_sides(low, high):
    _, inv = node_between(low, high)
    side = low[3] + high[4]
    return high[3] + high[1] * inv * side, low[4] + low[1] * inv * side


def block_numbers(coef_ref, side_ref, step):
    return [
        [coef_ref[core, block_rows(3 * step + q), :] for q in range(3)]
        + [side_ref[core, block_rows(q), :] for q in range(2)]
        for core in range(2)
    ]


def wide_numbers(side_ref):
    return [[side_ref[core, wide_rows(q), :] for q in range(5)] for core in range(2)]


def my_half(number):
    half = number.shape[0] // 2
    core = lax.rem(lax.axis_index("gz"), 2)
    return jnp.where(core == 0, number[:half], number[half:])


def halves(q):
    return pl.ds(HALF * q, HALF)


def links_kernel(coef_ref, link_ref, low_ref, high_ref):
    for step in range(2):
        low, high = (
            [coef_ref[core, block_rows(3 * step + q), :] for q in range(3)] for core in range(2)
        )
        back_ground, edge, ground = merged_coefficients(low, high)
        link_ref[halves(step), :] = my_half(edge)
        low_ref[halves(step), :] = my_half(back_ground + edge)
        high_ref[halves(step), :] = my_half(ground + edge)


def merge_kernel(
    coef_ref,
    pair_ref,
    link_ref,
    low_ref,
    high_ref,
    from_low_ref,
    from_high_ref,
    pay_ref,
    scale_ref,
    p_ref,
    sem,
    *,
    copies,
):
    p_ref[16:24] = jnp.zeros((8, XC), jnp.float32)
    for step in range(2):
        rows = halves(step)
        own = high_ref[rows, :] + from_high_ref[rows, :]
        root = jnp.sqrt(own)
        own_inv = 1.0 / root
        last_inv = 1.0 / jnp.sqrt(from_low_ref[rows, :] + low_ref[rows, :])
        scale_ref[halves(2 * step), :] = own_inv
        scale_ref[halves(2 * step + 1), :] = last_inv
        p_ref[halves(3 * step), :] = link_ref[rows, :] * (own_inv * last_inv)
        if step == 0:
            scale_ref[halves(4), :] = root
            scale_ref[halves(5), :] = from_high_ref[rows, :]
    low, high = block_numbers(coef_ref, pair_ref, 0)
    side, back_side = merged_sides(low, high)
    p_ref[halves(1), :] = my_half(side) * scale_ref[halves(0), :]
    p_ref[halves(2), :] = my_half(back_side) * scale_ref[halves(1), :]
    low, high = wide_numbers(pair_ref)
    for q, number in enumerate(merged_coefficients(low, high) + merged_sides(low, high)):
        p_ref[16 + q : 17 + q] = my_half(number)
    spread(p_ref, pay_ref, sem, copies)


def later_merge_kernel(coef_ref, more_ref, scale_ref, pay_ref, p_ref, sem, *, copies):
    side, back_side = merged_sides(*block_numbers(coef_ref, more_ref, 1))
    p_ref[halves(0), :] = my_half(side) * scale_ref[halves(2), :]
    p_ref[halves(1), :] = my_half(back_side) * scale_ref[halves(3), :]
    spread(p_ref, pay_ref, sem, copies)


def unit_chain(count, link, side_of, put):
    half = count // 2
    gain, part = [None] * count, [None] * count
    diag_l = diag_r = None
    side_l, side_r = side_of(0), side_of(count - 1)
    for i in range(half - 1):
        j = count - 1 - i
        edge_l, edge_r = link(i + 1), link(j)
        if i == 0:
            gain[i], part[i], gain[j], part[j] = edge_l, side_l, edge_r, side_r
        else:
            inv_l, inv_r = 1.0 / diag_l, 1.0 / diag_r
            gain[i], part[i] = edge_l * inv_l, side_l * inv_l
            gain[j], part[j] = edge_r * inv_r, side_r * inv_r
        diag_l = 1.0 - edge_l * gain[i]
        side_l = side_of(i + 1) + edge_l * part[i]
        diag_r = 1.0 - edge_r * gain[j]
        side_r = side_of(j - 1) + edge_r * part[j]
    edge = link(half)
    if half == 1:
        diag_l = diag_r = jnp.ones_like(edge)
    inv = 1.0 / (diag_l * diag_r - edge * edge)
    low = (side_l * diag_r + edge * side_r) * inv
    high = (side_r * diag_l + edge * side_l) * inv
    put(half - 1, low)
    put(half, high)
    for i in range(half - 2, -1, -1):
        low = part[i] + gain[i] * low
        put(i, low)
        j = count - 1 - i
        high = part[j] + gain[j] * high
        put(j, high)


def chain_kernel(all_ref, scale_ref, out_ref, s_ref, w_ref, *, chips):
    s_ref[0] = jnp.zeros((HALF, XC), jnp.float32)
    w_ref[0] = jnp.zeros((1, XC), jnp.float32)

    def side_of(j):
        side = all_ref[j, halves(1), :]
        return side + all_ref[j + 1, halves(2), :] if j + 1 < chips else side

    def put(j, value):
        s_ref[j + 1] = value

    def put_wide(j, value):
        w_ref[j + 1] = value

    unit_chain(chips, lambda j: all_ref[j, halves(0), :], side_of, put)
    chain(chips, lambda j, q: all_ref[j, 16 + q : 17 + q, :], put_wide)
    me = lax.div(lax.axis_index("gz"), 2)
    then = jnp.minimum(me + 1, chips - 1)
    own = s_ref[me + 1] * scale_ref[halves(0), :]
    inflow = all_ref[then, halves(0), :] * s_ref[then + 1] + all_ref[then, halves(2), :]
    out_ref[8:16] = jnp.zeros((8, XC), jnp.float32)
    out_ref[halves(0), :] = s_ref[me] * scale_ref[halves(1), :]
    out_ref[halves(1), :] = own
    out_ref[halves(2), :] = scale_ref[halves(5), :] * own - scale_ref[halves(4), :] * inflow
    out_ref[12:13] = w_ref[me]
    out_ref[13:14] = w_ref[me + 1]


def later_chain_kernel(all_ref, more_ref, scale_ref, out_ref, s_ref, *, chips):
    s_ref[0] = jnp.zeros((HALF, XC), jnp.float32)

    def side_of(j):
        side = more_ref[j, halves(0), :]
        return side + more_ref[j + 1, halves(1), :] if j + 1 < chips else side

    def put(j, value):
        s_ref[j + 1] = value

    unit_chain(chips, lambda j: all_ref[j, halves(3), :], side_of, put)
    me = lax.div(lax.axis_index("gz"), 2)
    out_ref[halves(0), :] = s_ref[me] * scale_ref[halves(3), :]
    out_ref[halves(1), :] = s_ref[me + 1] * scale_ref[halves(2), :]


def ends_of(low, high, before, last):
    _, inv = node_between(low, high)
    node = (low[3] + high[4] + low[1] * before + high[1] * last) * inv
    upper = lax.rem(lax.axis_index("gz"), 2) == 1
    return jnp.where(upper, node, before), jnp.where(upper, last, node), node


def joined(res_ref, u_ref, count):
    for q in range(count):
        for core in range(2):
            u_ref[q, halves(core), :] = res_ref[core, halves(q), :]


def back_kernel(coef_ref, more_ref, res_ref, co_z_ref, side_z_ref, t_ref, u_ref):
    joined(res_ref, u_ref, 2)
    low, high = block_numbers(coef_ref, more_ref, 1)
    before, own, _ = ends_of(low, high, u_ref[0], u_ref[1])

    def place(i, value):
        t_ref[z_rows(i), :] = value

    substitute(ZC, before, own, co_z_ref, side_z_ref, place)


def turn_kernel(
    coef_ref,
    pair_ref,
    res_ref,
    co_z_ref,
    side_z_ref,
    co_wide_ref,
    side_wide_ref,
    z_entry_ref,
    c_ref,
    m_ref,
    x_ref,
    co_y_ref,
    below_ref,
    above_ref,
    south_ref,
    north_ref,
    pay_ref,
    side_y_ref,
    fluxz_ref,
    cure_ref,
    u_ref,
    w_ref,
    t_ref,
    e_ref,
    k_ref,
    g_ref,
    fy_ref,
    r_ref,
    p_ref,
    sem,
    *,
    groups_y,
    groups_z,
):
    joined(res_ref, u_ref, 3)
    low, high = block_numbers(coef_ref, pair_ref, 0)
    last = u_ref[1]
    before, own, node = ends_of(low, high, u_ref[0], last)

    def place(i, value):
        t_ref[z_rows(i), :] = value

    substitute(ZC, before, own, co_z_ref, side_z_ref, place)
    me = lax.axis_index("gz")
    inside = high[0] * node + high[1] * (node - last) - high[4]
    current = jnp.where(lax.rem(me, 2) == 1, u_ref[2], inside)
    above = jnp.where(me == groups_z - 1, 0.0, own - current / z_entry_ref[...])

    for q in range(2):
        for core in range(2):
            w_ref[q, core : core + 1] = res_ref[core, 12 + q : 13 + q, :]
    low, high = wide_numbers(pair_ref)
    before_wide, own_wide, _ = ends_of(low, high, w_ref[0], w_ref[1])

    def place_wide(i, value):
        e_ref[2 * i : 2 * i + 2] = value

    substitute(ZC, before_wide, own_wide, co_wide_ref, side_wide_ref, place_wide)
    row = lax.axis_index("gy")
    south = jnp.where(row == 0, 0.0, e_ref[pl.ds(0, ZC, stride=2), :])
    north = jnp.where(row == groups_y - 1, 0.0, e_ref[pl.ds(1, ZC, stride=2), :])
    flow_rhs(
        t_ref,
        c_ref,
        m_ref,
        x_ref,
        (before, above),
        (south, north),
        (below_ref[2], above_ref[2]),
        (south_ref[2], north_ref[2]),
        (fluxz_ref, cure_ref),
        (k_ref, g_ref, fy_ref, r_ref),
    )
    side, back_side = reduce_sides(YC, lambda i: r_ref[y_rows(i), :], co_y_ref, side_y_ref)
    p_ref[0:ZC] = side
    p_ref[ZC : 2 * ZC] = back_side
    spread(p_ref, pay_ref, sem, groups_y)


def call(kernel, outs, scratch=(), spread_to=0, **static):
    out_specs = [pl.BlockSpec(memory_space=pltpu.VMEM)] * len(outs)
    shapes = [pltpu.VMEM(shape, jnp.float32) for shape in scratch]
    if spread_to:
        out_specs[0] = pl.BlockSpec(memory_space=pl.ANY)
        shapes.append(pltpu.SemaphoreType.DMA((spread_to,)))
    return pl.pallas_call(
        functools.partial(kernel, **static),
        out_shape=tuple(outs),
        out_specs=tuple(out_specs),
        scratch_shapes=shapes,
        compiler_params=pltpu.CompilerParams(vmem_limit_bytes=12 * 1024 * 1024),
        name=kernel.__name__,
    )


def body(warmth, cure, label):
    groups_z, groups_y = lax.axis_size("gz"), lax.axis_size("gy")
    chips = groups_z // 2
    up = {a: [(i, i + 1) for i in range(n - 1)] for a, n in (("gz", groups_z), ("gy", groups_y))}
    down = {a: [(j, i) for i, j in up[a]] for a in up}
    pairs = [[2 * i, 2 * i + 1] for i in range(chips)]
    same_core = [[2 * i + core for i in range(chips)] for core in range(2)]
    cells = (ROWS, XC)
    block = f32(*cells)

    zlo, zhi, ylo, yhi, t, c, m = pl.pallas_call(
        edges_kernel,
        out_shape=(
            f32(3, YC, XC),
            f32(3, YC, XC),
            f32(3, ZC, XC),
            f32(3, ZC, XC),
            block,
            block,
            jax.ShapeDtypeStruct(cells, jnp.int32),
        ),
        in_specs=[pl.BlockSpec(memory_space=pltpu.HBM)] * 3,
        scratch_shapes=[pltpu.SemaphoreType.DMA((3,))],
        compiler_params=pltpu.CompilerParams(vmem_limit_bytes=12 * 1024 * 1024),
        name="edges_kernel",
    )(*(pltpu.with_memory_space_constraint(a.reshape(cells), pltpu.HBM) for a in (warmth, cure, label)))
    z_halo = (lax.ppermute(zhi, "gz", up["gz"]), lax.ppermute(zlo, "gz", down["gz"]))
    y_halo = (lax.ppermute(yhi, "gy", up["gy"]), lax.ppermute(ylo, "gy", down["gy"]))

    def gather_y(pay):
        return lax.all_to_all(pay, "gy", 0, 0, tiled=True)

    def gather_z(pay):
        return lax.all_to_all(pay, "gz", 0, 0, tiled=True, axis_index_groups=same_core)

    def share(numbers):
        return lax.all_gather(numbers, "gz", axis_index_groups=pairs)

    sizes = dict(groups_y=groups_y, groups_z=groups_z)
    co_y, side_y = f32(3, YC - 1, ZC, XC), f32(YC - 1, ZC, XC)
    co_z, side_z = f32(3, ZC - 1, YC, XC), f32(ZC - 1, YC, XC)
    next_chip = [(i, i + 2) for i in range(groups_z - 2)]
    last_chip = [(j, i) for i, j in next_chip]
    x_shape = f32(2 * ROUNDS + 2, ROWS, XC)
    line = (groups_y + 1, ZC, XC)

    (x1,) = call(x_kernel, [x_shape])(c, m)
    pay, co_y1, side, co_y2, fluxz, c1, y_entry = call(
        front_kernel,
        [f32(groups_y, 8 * ZC + 8, XC), co_y, side_y, co_y, block, block, f32(ZC, XC)],
        [cells] * 4 + [(8 * ZC + 8, XC)],
        spread_to=groups_y,
        groups=groups_y,
    )(t, c, m, x1, *z_halo, *y_halo)
    x2, co_z1, co_z2, numbers, z_entry = call(
        ahead_kernel,
        [x_shape, co_z, co_z, f32(6 * YC, XC), f32(YC, XC)],
        groups_z=groups_z,
    )(c, c1, m, *z_halo)
    coef = share(numbers)
    link, low, high = call(links_kernel, [f32(YC, XC)] * 3)(coef)
    from_low = lax.ppermute(high, "gz", next_chip)
    from_high = lax.ppermute(low, "gz", last_chip)
    everyone = gather_y(pay)
    numbers, side, co_wide, side_wide = call(
        middle_kernel,
        [f32(4 * YC, XC), side_z, f32(3, ZC - 1, 2, XC), f32(ZC - 1, 2, XC)],
        [line, cells, (7, 40, XC)],
        **sizes,
    )(everyone, co_y1, side, fluxz, m, co_z1, y_entry, *y_halo)
    pair = share(numbers)
    pay, scale = call(
        merge_kernel,
        [f32(chips, 24, XC), f32(24, XC)],
        [(24, XC)],
        spread_to=chips,
        copies=chips,
    )(coef, pair, link, low, high, from_low, from_high)
    column = gather_z(pay)
    half_line = (chips + 1, HALF, XC)
    (found,) = call(
        chain_kernel, [f32(16, XC)], [half_line, (chips + 1, 1, XC)], chips=chips
    )(column, scale)
    pay, side, fluxz, c2 = call(
        turn_kernel,
        [f32(groups_y, 2 * ZC, XC), side_y, block, block],
        [(3, YC, XC), (2, 2, XC), cells, (2 * ZC, XC)] + [cells] * 4 + [(2 * ZC, XC)],
        spread_to=groups_y,
        **sizes,
    )(
        coef,
        pair,
        share(found),
        co_z1,
        side,
        co_wide,
        side_wide,
        z_entry,
        c1,
        m,
        x2,
        co_y2,
        *z_halo,
        *y_halo,
    )
    numbers, side = call(
        later_middle_kernel, [f32(2 * YC, XC), side_z], [line, cells], groups_y=groups_y
    )(everyone, gather_y(pay), co_y2, side, fluxz, m, co_z2)
    more = share(numbers)
    (pay,) = call(
        later_merge_kernel, [f32(chips, YC, XC)], [(YC, XC)], spread_to=chips, copies=chips
    )(coef, more, scale)
    (found,) = call(later_chain_kernel, [f32(YC, XC)], [half_line], chips=chips)(
        column, gather_z(pay), scale
    )
    (t2,) = call(back_kernel, [block], [(2, YC, XC)])(coef, more, share(found), co_z2, side)
    return t2.reshape(warmth.shape), c2.reshape(cure.shape)


def solution(mesh):
    return jax.shard_map(
        body,
        mesh=mesh,
        in_specs=(P("gz", "gy", None),) * 3,
        out_specs=(P("gz", "gy", None),) * 2,
        check_vma=False,
    )
```

```python
import functools

import jax
import jax.numpy as jnp
from jax import lax
from jax.experimental import pallas as pl
from jax.experimental.pallas import tpu as pltpu
from jax.sharding import PartitionSpec as P

ZC = 16
YC = 8
XC = 128
ROWS = ZC * YC


def f32(*shape):
    return jax.ShapeDtypeStruct(shape, jnp.float32)


def conduct_of(label, cure):
    return jnp.where(label == 1, 40.0, jnp.where(label == 2, 20.0, 0.6 + 0.8 * cure))


def store_of(label):
    return jnp.where(label == 1, 3.0 / 60.0, jnp.where(label == 2, 2.0 / 60.0, 1.0 / 60.0))


def store_by(k):
    return jnp.where(k > 30.0, 3.0 / 60.0, jnp.where(k > 10.0, 2.0 / 60.0, 1.0 / 60.0))


def cure_of(label, warmth, cure):
    speed = 0.3 * jnp.exp(8.0 * warmth)
    return jnp.where(label == 0, 1.0 - (1.0 - cure) * jnp.exp(-speed), cure)


def y_rows(y):
    return pl.ds(y, ZC, stride=YC)


def z_rows(z):
    return pl.ds(z * YC, YC)


def edges_kernel(
    t_in, c_in, m_in, zlo_ref, zhi_ref, ylo_ref, yhi_ref, t_ref, c_ref, m_ref, sem
):
    copies = [
        pltpu.make_async_copy(src, dst, sem.at[i])
        for i, (src, dst) in enumerate(((t_in, t_ref), (c_in, c_ref), (m_in, m_ref)))
    ]
    for copy in copies:
        copy.start()
    for copy in copies:
        copy.wait()

    def put(out, rows):
        t, c, m = t_ref[rows, :], c_ref[rows, :], m_ref[rows, :]
        out[0] = t
        out[1] = conduct_of(m, c)
        out[2] = conduct_of(m, cure_of(m, t, c))

    put(zlo_ref, z_rows(0))
    put(zhi_ref, z_rows(ZC - 1))
    put(ylo_ref, y_rows(0))
    put(yhi_ref, y_rows(YC - 1))


def spread(one_ref, out_ref, sem, count):
    copies = [pltpu.make_async_copy(one_ref, out_ref.at[d], sem.at[d]) for d in range(count)]
    for copy in copies:
        copy.start()
    for copy in copies:
        copy.wait()


def reduce_coefficients(count, store, faces, entry, co_ref):
    ground, edge = store(0), entry
    back_ground = None
    for i in range(count - 1):
        face = faces(i)
        inv = 1.0 / (ground + edge + face)
        edge_inv, face_inv = edge * inv, face * inv
        co_ref[0, i] = inv
        co_ref[1, i] = edge_inv
        co_ref[2, i] = face_inv
        more = edge_inv * ground
        back_ground = more if i == 0 else back_ground + more
        ground = store(i + 1) + face_inv * ground
        edge = edge_inv * face
    return back_ground, edge, ground


def reduce_sides(count, right, co_ref, side_ref):
    side = right(0)
    back_side = None
    for i in range(count - 1):
        side_ref[i] = side * co_ref[0, i]
        more = co_ref[1, i] * side
        back_side = more if i == 0 else back_side + more
        side = right(i + 1) + co_ref[2, i] * side
    return side, back_side


def substitute(count, before, own, co_ref, side_ref, put):
    value = own
    put(count - 1, value)
    for i in range(count - 2, -1, -1):
        value = (side_ref[i] + co_ref[1, i] * before) + co_ref[2, i] * value
        put(i, value)


def edge_lanes():
    lane = lax.broadcasted_iota(jnp.int32, (YC, XC), 1)
    return lane == 0, lane == XC - 1


ROUNDS = 7


def x_coefficients(c_ref, m_ref, x_ref):
    first_lane, last_lane = edge_lanes()
    batch = 4
    for z0 in range(0, ZC, batch):
        gs, ls, rs, stores = [], [], [], []
        for z in range(z0, z0 + batch):
            rows = z_rows(z)
            m = m_ref[rows, :]
            k, g = conduct_of(m, c_ref[rows, :]), store_of(m)
            face_left = 0.5 * (k + jnp.where(first_lane, 0.0, pltpu.roll(k, 1, 1)))
            face_right = jnp.where(last_lane, 0.5 * k, pltpu.roll(face_left, XC - 1, 1))
            x_ref[2 * ROUNDS + 1, rows, :] = face_left
            gs.append(
                g
                + jnp.where(first_lane, face_left, 0.0)
                + jnp.where(last_lane, face_right, 0.0)
            )
            ls.append(jnp.where(first_lane, 0.0, face_left))
            rs.append(jnp.where(last_lane, 0.0, face_right))
            stores.append(g)
        for level in range(ROUNDS):
            low, high = 1 << level, XC - (1 << level)
            for b in range(batch):
                rows = z_rows(z0 + b)
                ground, left, right = gs[b], ls[b], rs[b]
                inv = 1.0 / (ground + left + right)
                to_left = left * pltpu.roll(inv, low, 1)
                to_right = right * pltpu.roll(inv, high, 1)
                x_ref[2 * level, rows, :] = to_left
                x_ref[2 * level + 1, rows, :] = to_right
                gs[b] = (
                    ground
                    + to_left * pltpu.roll(ground, low, 1)
                    + to_right * pltpu.roll(ground, high, 1)
                )
                if level + 1 < ROUNDS:
                    ls[b] = to_left * pltpu.roll(left, low, 1)
                    rs[b] = to_right * pltpu.roll(right, high, 1)
        for b in range(batch):
            x_ref[2 * ROUNDS, z_rows(z0 + b), :] = stores[b] / gs[b]


def x_kernel(c_ref, m_ref, x_ref):
    x_coefficients(c_ref, m_ref, x_ref)


def z_coefficients(groups_z, c_ref, m_ref, below, above, co_ref, num_ref, row):
    ks = [below]
    for z in range(ZC):
        ks.append(conduct_of(m_ref[z_rows(z), :], c_ref[z_rows(z), :]))
    ks.append(above)
    faces = [0.5 * (ks[i] + ks[i + 1]) for i in range(ZC + 1)]
    numbers = reduce_coefficients(
        ZC,
        lambda i: store_of(m_ref[z_rows(i), :]),
        lambda i: faces[i + 1],
        faces[0],
        co_ref,
    )
    at_end = lax.axis_index("gz") == groups_z - 1
    num_ref[row : row + YC] = numbers[0]
    num_ref[row + YC : row + 2 * YC] = numbers[1]
    num_ref[row + 2 * YC : row + 3 * YC] = numbers[2] + jnp.where(at_end, faces[ZC], 0.0)
    return faces[ZC]


def ahead_kernel(
    c_ref,
    next_c_ref,
    m_ref,
    below_ref,
    above_ref,
    south_ref,
    north_ref,
    x_ref,
    co1_ref,
    co2_ref,
    num_ref,
    entry_ref,
    co_y_ref,
    link_ref,
    low_ref,
    high_ref,
    k_ref,
    g_ref,
    *,
    groups_y,
    groups_z,
):
    m = m_ref[...]
    k_ref[...] = conduct_of(m, next_c_ref[...])
    g_ref[...] = store_of(m)
    ks = [south_ref[2]] + [k_ref[y_rows(y), :] for y in range(YC)] + [north_ref[2]]
    faces = [0.5 * (ks[i] + ks[i + 1]) for i in range(YC + 1)]
    back_ground, edge, ground = reduce_coefficients(
        YC, lambda i: g_ref[y_rows(i), :], lambda i: faces[i + 1], faces[0], co_y_ref
    )
    at_end = lax.axis_index("gy") == groups_y - 1
    link_ref[...] = edge
    low_ref[...] = back_ground + edge
    high_ref[...] = ground + edge + jnp.where(at_end, faces[YC], 0.0)
    x_coefficients(next_c_ref, m_ref, x_ref)
    entry_ref[...] = z_coefficients(
        groups_z, c_ref, m_ref, below_ref[1], above_ref[1], co1_ref, num_ref, 0
    )
    z_coefficients(
        groups_z, next_c_ref, m_ref, below_ref[2], above_ref[2], co2_ref, num_ref, 3 * YC
    )


def flow_rhs(t_ref, c_ref, m_ref, x_ref, zt, yt, zk, yk, outs, scratch):
    fluxz_ref, cure_ref = outs
    k_ref, g_ref, fy_ref, r_ref = scratch
    t, c, m = t_ref[...], c_ref[...], m_ref[...]
    k_ref[...] = conduct_of(m, c)
    g_ref[...] = store_of(m)
    cure_ref[...] = cure_of(m, t, c)

    ks = [yk[0]] + [k_ref[y_rows(y), :] for y in range(YC)] + [yk[1]]
    ts = [yt[0]] + [t_ref[y_rows(y), :] for y in range(YC)] + [yt[1]]
    face_y = [0.5 * (ks[i] + ks[i + 1]) for i in range(YC + 1)]
    flow_y = [face_y[i] * (ts[i + 1] - ts[i]) for i in range(YC + 1)]
    for y in range(YC):
        fy_ref[y_rows(y), :] = flow_y[y + 1] - flow_y[y]

    first_lane, last_lane = edge_lanes()
    k_prev, t_prev = zk[0], zt[0]
    flow_prev = 0.5 * (k_prev + k_ref[z_rows(0), :]) * (t_ref[z_rows(0), :] - t_prev)
    batch = 4
    for z0 in range(0, ZC, batch):
        sides = []
        for z in range(z0, z0 + batch):
            rows = z_rows(z)
            kz, tz = k_ref[rows, :], t_ref[rows, :]
            k_next = k_ref[z_rows(z + 1), :] if z + 1 < ZC else zk[1]
            t_next = t_ref[z_rows(z + 1), :] if z + 1 < ZC else zt[1]
            flow_next = 0.5 * (kz + k_next) * (t_next - tz)
            flux_z = flow_next - flow_prev
            flow_prev = flow_next
            fluxz_ref[rows, :] = flux_z
            t_left = jnp.where(first_lane, 0.0, pltpu.roll(tz, 1, 1))
            flow_left = x_ref[2 * ROUNDS + 1, rows, :] * (tz - t_left)
            flow_right = jnp.where(last_lane, -0.5 * kz * tz, pltpu.roll(flow_left, XC - 1, 1))
            delta = cure_ref[rows, :] - c_ref[rows, :]
            sides.append(
                g_ref[rows, :] * (tz + 0.4 * delta)
                + (flow_right - flow_left)
                + 2.0 * (fy_ref[rows, :] + flux_z)
            )
        for level in range(ROUNDS):
            low, high = 1 << level, XC - (1 << level)
            for b in range(batch):
                rows = z_rows(z0 + b)
                side = sides[b]
                sides[b] = (
                    side
                    + x_ref[2 * level, rows, :] * pltpu.roll(side, low, 1)
                    + x_ref[2 * level + 1, rows, :] * pltpu.roll(side, high, 1)
                )
        for b in range(batch):
            rows = z_rows(z0 + b)
            r_ref[rows, :] = x_ref[2 * ROUNDS, rows, :] * sides[b] - fy_ref[rows, :]
    return face_y


def front_kernel(
    t_ref,
    c_ref,
    m_ref,
    x_ref,
    below_ref,
    above_ref,
    south_ref,
    north_ref,
    pay_ref,
    co1_ref,
    side_ref,
    fluxz_ref,
    cure_ref,
    entry_ref,
    k_ref,
    g_ref,
    fy_ref,
    r_ref,
    p_ref,
    sem,
    *,
    groups,
):
    face_y = flow_rhs(
        t_ref,
        c_ref,
        m_ref,
        x_ref,
        (below_ref[0], above_ref[0]),
        (south_ref[0], north_ref[0]),
        (below_ref[1], above_ref[1]),
        (south_ref[1], north_ref[1]),
        (fluxz_ref, cure_ref),
        (k_ref, g_ref, fy_ref, r_ref),
    )
    entry_ref[...] = face_y[YC]
    at_end = lax.axis_index("gy") == groups - 1
    back_ground, edge, ground = reduce_coefficients(
        YC, lambda i: g_ref[y_rows(i), :], lambda i: face_y[i + 1], face_y[0], co1_ref
    )
    ground = ground + jnp.where(at_end, face_y[YC], 0.0)
    side, back_side = reduce_sides(YC, lambda i: r_ref[y_rows(i), :], co1_ref, side_ref)
    for y, row in ((0, 5 * ZC), (YC - 1, 5 * ZC + 4)):
        for i, corner in enumerate((below_ref[0], above_ref[0], below_ref[1], above_ref[1])):
            p_ref[row + i : row + i + 1] = corner[y : y + 1]
    numbers = (back_ground, edge, ground, side, back_side)
    for q, number in enumerate(numbers):
        p_ref[ZC * q : ZC * q + ZC] = number
    spread(p_ref, pay_ref, sem, groups)


def chain(count, read, put):
    def ground_of(j):
        return read(j, 2) + read(j + 1, 0) if j + 1 < count else read(j, 2)

    def side_of(j):
        return read(j, 3) + read(j + 1, 4) if j + 1 < count else read(j, 3)

    half = count // 2
    gain, part = [None] * count, [None] * count
    ground_l, side_l = ground_of(0) + read(0, 1), side_of(0)
    ground_r, side_r = ground_of(count - 1), side_of(count - 1)
    for i in range(half - 1):
        edge = read(i + 1, 1)
        inv = 1.0 / (ground_l + edge)
        gain[i], part[i] = edge * inv, side_l * inv
        ground_l = ground_of(i + 1) + gain[i] * ground_l
        side_l = side_of(i + 1) + gain[i] * side_l
        j = count - 1 - i
        edge = read(j, 1)
        inv = 1.0 / (ground_r + edge)
        gain[j], part[j] = edge * inv, side_r * inv
        ground_r = ground_of(j - 1) + gain[j] * ground_r
        side_r = side_of(j - 1) + gain[j] * side_r
    edge = read(half, 1)
    inv = 1.0 / (ground_l * ground_r + edge * (ground_l + ground_r))
    low = (side_l * (ground_r + edge) + edge * side_r) * inv
    high = (side_r * (ground_l + edge) + edge * side_l) * inv
    put(half - 1, low)
    put(half, high)
    for i in range(half - 2, -1, -1):
        low = part[i] + gain[i] * low
        put(i, low)
        j = count - 1 - i
        high = part[j] + gain[j] * high
        put(j, high)


def first_of_next(own, after, back_ground, edge, back_side, entry):
    return own - (back_ground * own + edge * (own - after) - back_side) / entry


def substitute_y(before, own, co_ref, side_ref, v_ref):
    def place(i, value):
        v_ref[y_rows(i), :] = value

    substitute(YC, before, own, co_ref, side_ref, place)


def block_rows(q):
    return pl.ds(YC * q, YC)


def wide_rows(q):
    return pl.ds(2 * YC + 2 * q, 2)


def middle_kernel(
    all_ref,
    co_y_ref,
    side_y_ref,
    fluxz_ref,
    m_ref,
    co_z_ref,
    y_entry_ref,
    south_ref,
    north_ref,
    p_ref,
    side_z_ref,
    co_wide_ref,
    side_wide_ref,
    s_ref,
    v_ref,
    h_ref,
    *,
    groups_y,
    groups_z,
):
    def read(j, q):
        return all_ref[j, ZC * q : ZC * q + ZC, :]

    s_ref[0] = jnp.zeros((ZC, XC), jnp.float32)

    def put(j, value):
        s_ref[j + 1] = value

    chain(groups_y, read, put)
    me = lax.axis_index("gy")
    before, own = s_ref[me], s_ref[me + 1]
    substitute_y(before, own, co_y_ref, side_y_ref, v_ref)

    def right(i):
        return store_of(m_ref[z_rows(i), :]) * v_ref[z_rows(i), :] - fluxz_ref[z_rows(i), :]

    sides = reduce_sides(ZC, right, co_z_ref, side_z_ref)
    p_ref[24:32, :] = jnp.zeros((8, XC), jnp.float32)
    p_ref[block_rows(0), :] = sides[0]
    p_ref[block_rows(1), :] = sides[1]

    then = jnp.minimum(me + 1, groups_y - 1)
    north = first_of_next(
        own,
        s_ref[then + 1],
        all_ref[then, 0:16, :],
        all_ref[then, 16:32, :],
        all_ref[then, 64:80, :],
        y_entry_ref[...],
    )
    last = jnp.maximum(me - 1, 0)
    beside = (
        (0, before, south_ref, all_ref[last, 5 * ZC + 4 : 5 * ZC + 8, :]),
        (1, north, north_ref, all_ref[then, 5 * ZC : 5 * ZC + 4, :]),
    )
    for side, value, halo_ref, corners in beside:
        rows = pl.ds(2 + side, ZC, stride=2)
        for q in range(2):
            h_ref[q, rows, :] = halo_ref[q]
            h_ref[q, side : side + 1, :] = corners[2 * q : 2 * q + 1]
            h_ref[q, 34 + side : 35 + side, :] = corners[2 * q + 1 : 2 * q + 2]
        h_ref[2, rows, :] = value
    faces = 0.5 * (h_ref[1, 0:34, :] + h_ref[1, 2:36, :])
    h_ref[3, 0:34, :] = faces
    h_ref[4, 0:34, :] = faces * (h_ref[0, 2:36, :] - h_ref[0, 0:34, :])
    capacity = store_by(h_ref[1, 2:34, :])
    h_ref[5, 0:32, :] = capacity
    h_ref[6, 0:32, :] = capacity * h_ref[2, 2:34, :] - (h_ref[4, 2:34, :] - h_ref[4, 0:32, :])
    numbers = reduce_coefficients(
        ZC,
        lambda i: h_ref[5, 2 * i : 2 * i + 2, :],
        lambda i: h_ref[3, 2 * i + 2 : 2 * i + 4, :],
        h_ref[3, 0:2, :],
        co_wide_ref,
    )
    sides = reduce_sides(
        ZC, lambda i: h_ref[6, 2 * i : 2 * i + 2, :], co_wide_ref, side_wide_ref
    )
    at_end = lax.axis_index("gz") == groups_z - 1
    p_ref[wide_rows(0), :] = numbers[0]
    p_ref[wide_rows(1), :] = numbers[1]
    p_ref[wide_rows(2), :] = numbers[2] + jnp.where(at_end, h_ref[3, 32:34, :], 0.0)
    p_ref[wide_rows(3), :] = sides[0]
    p_ref[wide_rows(4), :] = sides[1]


def later_middle_kernel(
    all_ref,
    scale_ref,
    co_y_ref,
    side_y_ref,
    fluxz_ref,
    m_ref,
    co_z_ref,
    p_ref,
    side_z_ref,
    s_ref,
    v_ref,
    *,
    groups_y,
):
    s_ref[0] = jnp.zeros((ZC, XC), jnp.float32)

    def side_of(j):
        side = all_ref[j, ZC : 2 * ZC, :]
        return side + all_ref[j + 1, 2 * ZC : 3 * ZC, :] if j + 1 < groups_y else side

    def put(j, value):
        s_ref[j + 1] = value

    unit_chain(groups_y, lambda j: all_ref[j, 0:ZC, :], side_of, put)
    me = lax.axis_index("gy")
    before, own = s_ref[me] * scale_ref[1], s_ref[me + 1] * scale_ref[0]
    substitute_y(before, own, co_y_ref, side_y_ref, v_ref)

    def right(i):
        return store_of(m_ref[z_rows(i), :]) * v_ref[z_rows(i), :] - fluxz_ref[z_rows(i), :]

    sides = reduce_sides(ZC, right, co_z_ref, side_z_ref)
    p_ref[0:YC] = sides[0]
    p_ref[YC : 2 * YC] = sides[1]


HALF = YC // 2


def node_between(low, high):
    ground = low[2] + high[0]
    return ground, 1.0 / (ground + low[1] + high[1])


def merged_coefficients(low, high):
    ground, inv = node_between(low, high)
    low_inv, high_inv = low[1] * inv, high[1] * inv
    return low[0] + low_inv * ground, low_inv * high[1], high[2] + high_inv * ground


def merged_sides(low, high):
    _, inv = node_between(low, high)
    side = low[3] + high[4]
    return high[3] + high[1] * inv * side, low[4] + low[1] * inv * side


def block_numbers(coef_ref, side_ref, step):
    return [
        [coef_ref[core, block_rows(3 * step + q), :] for q in range(3)]
        + [side_ref[core, block_rows(q), :] for q in range(2)]
        for core in range(2)
    ]


def wide_numbers(side_ref):
    return [[side_ref[core, wide_rows(q), :] for q in range(5)] for core in range(2)]


def my_half(number):
    half = number.shape[0] // 2
    core = lax.rem(lax.axis_index("gz"), 2)
    return jnp.where(core == 0, number[:half], number[half:])


def halves(q):
    return pl.ds(HALF * q, HALF)


def links_kernel(coef_ref, link_ref, low_ref, high_ref):
    for step in range(2):
        low, high = (
            [coef_ref[core, block_rows(3 * step + q), :] for q in range(3)] for core in range(2)
        )
        back_ground, edge, ground = merged_coefficients(low, high)
        link_ref[halves(step), :] = my_half(edge)
        low_ref[halves(step), :] = my_half(back_ground + edge)
        high_ref[halves(step), :] = my_half(ground + edge)


def merge_kernel(
    coef_ref,
    pair_ref,
    link_ref,
    low_ref,
    high_ref,
    from_low_ref,
    from_high_ref,
    pay_ref,
    scale_ref,
    p_ref,
    sem,
    *,
    copies,
):
    p_ref[16:24] = jnp.zeros((8, XC), jnp.float32)
    for step in range(2):
        rows = halves(step)
        own = high_ref[rows, :] + from_high_ref[rows, :]
        root = jnp.sqrt(own)
        own_inv = 1.0 / root
        last_inv = 1.0 / jnp.sqrt(from_low_ref[rows, :] + low_ref[rows, :])
        scale_ref[halves(2 * step), :] = own_inv
        scale_ref[halves(2 * step + 1), :] = last_inv
        p_ref[halves(3 * step), :] = link_ref[rows, :] * (own_inv * last_inv)
        if step == 0:
            scale_ref[halves(4), :] = root
            scale_ref[halves(5), :] = from_high_ref[rows, :]
    low, high = block_numbers(coef_ref, pair_ref, 0)
    side, back_side = merged_sides(low, high)
    p_ref[halves(1), :] = my_half(side) * scale_ref[halves(0), :]
    p_ref[halves(2), :] = my_half(back_side) * scale_ref[halves(1), :]
    low, high = wide_numbers(pair_ref)
    for q, number in enumerate(merged_coefficients(low, high) + merged_sides(low, high)):
        p_ref[16 + q : 17 + q] = my_half(number)
    spread(p_ref, pay_ref, sem, copies)


def later_merge_kernel(coef_ref, more_ref, scale_ref, pay_ref, p_ref, sem, *, copies):
    side, back_side = merged_sides(*block_numbers(coef_ref, more_ref, 1))
    p_ref[halves(0), :] = my_half(side) * scale_ref[halves(2), :]
    p_ref[halves(1), :] = my_half(back_side) * scale_ref[halves(3), :]
    spread(p_ref, pay_ref, sem, copies)


def unit_chain(count, link, side_of, put):
    half = count // 2
    gain, part = [None] * count, [None] * count
    diag_l = diag_r = None
    side_l, side_r = side_of(0), side_of(count - 1)
    for i in range(half - 1):
        j = count - 1 - i
        edge_l, edge_r = link(i + 1), link(j)
        if i == 0:
            gain[i], part[i], gain[j], part[j] = edge_l, side_l, edge_r, side_r
        else:
            inv_l, inv_r = 1.0 / diag_l, 1.0 / diag_r
            gain[i], part[i] = edge_l * inv_l, side_l * inv_l
            gain[j], part[j] = edge_r * inv_r, side_r * inv_r
        diag_l = 1.0 - edge_l * gain[i]
        side_l = side_of(i + 1) + edge_l * part[i]
        diag_r = 1.0 - edge_r * gain[j]
        side_r = side_of(j - 1) + edge_r * part[j]
    edge = link(half)
    if half == 1:
        diag_l = diag_r = jnp.ones_like(edge)
    inv = 1.0 / (diag_l * diag_r - edge * edge)
    low = (side_l * diag_r + edge * side_r) * inv
    high = (side_r * diag_l + edge * side_l) * inv
    put(half - 1, low)
    put(half, high)
    for i in range(half - 2, -1, -1):
        low = part[i] + gain[i] * low
        put(i, low)
        j = count - 1 - i
        high = part[j] + gain[j] * high
        put(j, high)


def chain_kernel(all_ref, scale_ref, out_ref, s_ref, w_ref, *, chips):
    s_ref[0] = jnp.zeros((HALF, XC), jnp.float32)
    w_ref[0] = jnp.zeros((1, XC), jnp.float32)

    def side_of(j):
        side = all_ref[j, halves(1), :]
        return side + all_ref[j + 1, halves(2), :] if j + 1 < chips else side

    def put(j, value):
        s_ref[j + 1] = value

    def put_wide(j, value):
        w_ref[j + 1] = value

    unit_chain(chips, lambda j: all_ref[j, halves(0), :], side_of, put)
    chain(chips, lambda j, q: all_ref[j, 16 + q : 17 + q, :], put_wide)
    me = lax.div(lax.axis_index("gz"), 2)
    then = jnp.minimum(me + 1, chips - 1)
    own = s_ref[me + 1] * scale_ref[halves(0), :]
    inflow = all_ref[then, halves(0), :] * s_ref[then + 1] + all_ref[then, halves(2), :]
    out_ref[8:16] = jnp.zeros((8, XC), jnp.float32)
    out_ref[halves(0), :] = s_ref[me] * scale_ref[halves(1), :]
    out_ref[halves(1), :] = own
    out_ref[halves(2), :] = scale_ref[halves(5), :] * own - scale_ref[halves(4), :] * inflow
    out_ref[12:13] = w_ref[me]
    out_ref[13:14] = w_ref[me + 1]


def later_chain_kernel(all_ref, more_ref, scale_ref, out_ref, s_ref, *, chips):
    s_ref[0] = jnp.zeros((HALF, XC), jnp.float32)

    def side_of(j):
        side = more_ref[j, halves(0), :]
        return side + more_ref[j + 1, halves(1), :] if j + 1 < chips else side

    def put(j, value):
        s_ref[j + 1] = value

    unit_chain(chips, lambda j: all_ref[j, halves(3), :], side_of, put)
    me = lax.div(lax.axis_index("gz"), 2)
    out_ref[halves(0), :] = s_ref[me] * scale_ref[halves(3), :]
    out_ref[halves(1), :] = s_ref[me + 1] * scale_ref[halves(2), :]


def ends_of(low, high, before, last):
    _, inv = node_between(low, high)
    node = (low[3] + high[4] + low[1] * before + high[1] * last) * inv
    upper = lax.rem(lax.axis_index("gz"), 2) == 1
    return jnp.where(upper, node, before), jnp.where(upper, last, node), node


def joined(res_ref, u_ref, count):
    for q in range(count):
        for core in range(2):
            u_ref[q, halves(core), :] = res_ref[core, halves(q), :]


def back_kernel(coef_ref, more_ref, res_ref, co_z_ref, side_z_ref, t_ref, u_ref):
    joined(res_ref, u_ref, 2)
    low, high = block_numbers(coef_ref, more_ref, 1)
    before, own, _ = ends_of(low, high, u_ref[0], u_ref[1])

    def place(i, value):
        t_ref[z_rows(i), :] = value

    substitute(ZC, before, own, co_z_ref, side_z_ref, place)


def turn_kernel(
    coef_ref,
    pair_ref,
    res_ref,
    co_z_ref,
    side_z_ref,
    co_wide_ref,
    side_wide_ref,
    z_entry_ref,
    c_ref,
    m_ref,
    x_ref,
    co_y_ref,
    link_ref,
    low_ref,
    high_ref,
    from_low_ref,
    from_high_ref,
    below_ref,
    above_ref,
    south_ref,
    north_ref,
    pay_ref,
    side_y_ref,
    fluxz_ref,
    cure_ref,
    scale_ref,
    u_ref,
    w_ref,
    t_ref,
    e_ref,
    k_ref,
    g_ref,
    fy_ref,
    r_ref,
    p_ref,
    sem,
    *,
    groups_y,
    groups_z,
):
    joined(res_ref, u_ref, 3)
    low, high = block_numbers(coef_ref, pair_ref, 0)
    last = u_ref[1]
    before, own, node = ends_of(low, high, u_ref[0], last)

    def place(i, value):
        t_ref[z_rows(i), :] = value

    substitute(ZC, before, own, co_z_ref, side_z_ref, place)
    me = lax.axis_index("gz")
    inside = high[0] * node + high[1] * (node - last) - high[4]
    current = jnp.where(lax.rem(me, 2) == 1, u_ref[2], inside)
    above = jnp.where(me == groups_z - 1, 0.0, own - current / z_entry_ref[...])

    for q in range(2):
        for core in range(2):
            w_ref[q, core : core + 1] = res_ref[core, 12 + q : 13 + q, :]
    low, high = wide_numbers(pair_ref)
    before_wide, own_wide, _ = ends_of(low, high, w_ref[0], w_ref[1])

    def place_wide(i, value):
        e_ref[2 * i : 2 * i + 2] = value

    substitute(ZC, before_wide, own_wide, co_wide_ref, side_wide_ref, place_wide)
    row = lax.axis_index("gy")
    south = jnp.where(row == 0, 0.0, e_ref[pl.ds(0, ZC, stride=2), :])
    north = jnp.where(row == groups_y - 1, 0.0, e_ref[pl.ds(1, ZC, stride=2), :])
    flow_rhs(
        t_ref,
        c_ref,
        m_ref,
        x_ref,
        (before, above),
        (south, north),
        (below_ref[2], above_ref[2]),
        (south_ref[2], north_ref[2]),
        (fluxz_ref, cure_ref),
        (k_ref, g_ref, fy_ref, r_ref),
    )
    side, back_side = reduce_sides(YC, lambda i: r_ref[y_rows(i), :], co_y_ref, side_y_ref)
    own_inv = 1.0 / jnp.sqrt(high_ref[...] + from_high_ref[...])
    last_inv = 1.0 / jnp.sqrt(from_low_ref[...] + low_ref[...])
    scale_ref[0] = own_inv
    scale_ref[1] = last_inv
    p_ref[0:ZC] = link_ref[...] * (own_inv * last_inv)
    p_ref[ZC : 2 * ZC] = side * own_inv
    p_ref[2 * ZC : 3 * ZC] = back_side * last_inv
    spread(p_ref, pay_ref, sem, groups_y)


def call(kernel, outs, scratch=(), spread_to=0, **static):
    out_specs = [pl.BlockSpec(memory_space=pltpu.VMEM)] * len(outs)
    shapes = [pltpu.VMEM(shape, jnp.float32) for shape in scratch]
    if spread_to:
        out_specs[0] = pl.BlockSpec(memory_space=pl.ANY)
        shapes.append(pltpu.SemaphoreType.DMA((spread_to,)))
    return pl.pallas_call(
        functools.partial(kernel, **static),
        out_shape=tuple(outs),
        out_specs=tuple(out_specs),
        scratch_shapes=shapes,
        compiler_params=pltpu.CompilerParams(vmem_limit_bytes=12 * 1024 * 1024),
        name=kernel.__name__,
    )


def body(warmth, cure, label):
    groups_z, groups_y = lax.axis_size("gz"), lax.axis_size("gy")
    chips = groups_z // 2
    up = {a: [(i, i + 1) for i in range(n - 1)] for a, n in (("gz", groups_z), ("gy", groups_y))}
    down = {a: [(j, i) for i, j in up[a]] for a in up}
    pairs = [[2 * i, 2 * i + 1] for i in range(chips)]
    same_core = [[2 * i + core for i in range(chips)] for core in range(2)]
    cells = (ROWS, XC)
    block = f32(*cells)

    zlo, zhi, ylo, yhi, t, c, m = pl.pallas_call(
        edges_kernel,
        out_shape=(
            f32(3, YC, XC),
            f32(3, YC, XC),
            f32(3, ZC, XC),
            f32(3, ZC, XC),
            block,
            block,
            jax.ShapeDtypeStruct(cells, jnp.int32),
        ),
        in_specs=[pl.BlockSpec(memory_space=pltpu.HBM)] * 3,
        scratch_shapes=[pltpu.SemaphoreType.DMA((3,))],
        compiler_params=pltpu.CompilerParams(vmem_limit_bytes=12 * 1024 * 1024),
        name="edges_kernel",
    )(*(pltpu.with_memory_space_constraint(a.reshape(cells), pltpu.HBM) for a in (warmth, cure, label)))
    z_halo = (lax.ppermute(zhi, "gz", up["gz"]), lax.ppermute(zlo, "gz", down["gz"]))
    y_halo = (lax.ppermute(yhi, "gy", up["gy"]), lax.ppermute(ylo, "gy", down["gy"]))

    def gather_y(pay):
        return lax.all_to_all(pay, "gy", 0, 0, tiled=True)

    def gather_z(pay):
        return lax.all_to_all(pay, "gz", 0, 0, tiled=True, axis_index_groups=same_core)

    def share(numbers):
        return lax.all_gather(numbers, "gz", axis_index_groups=pairs)

    sizes = dict(groups_y=groups_y, groups_z=groups_z)
    co_y, side_y = f32(3, YC - 1, ZC, XC), f32(YC - 1, ZC, XC)
    co_z, side_z = f32(3, ZC - 1, YC, XC), f32(ZC - 1, YC, XC)
    next_chip = [(i, i + 2) for i in range(groups_z - 2)]
    last_chip = [(j, i) for i, j in next_chip]
    x_shape = f32(2 * ROUNDS + 2, ROWS, XC)
    line = (groups_y + 1, ZC, XC)

    (x1,) = call(x_kernel, [x_shape])(c, m)
    pay, co_y1, side, fluxz, c1, y_entry = call(
        front_kernel,
        [f32(groups_y, 5 * ZC + 8, XC), co_y, side_y, block, block, f32(ZC, XC)],
        [cells] * 4 + [(5 * ZC + 8, XC)],
        spread_to=groups_y,
        groups=groups_y,
    )(t, c, m, x1, *z_halo, *y_halo)
    y_row = f32(ZC, XC)
    x2, co_z1, co_z2, numbers, z_entry, co_y2, link_y, low_y, high_y = call(
        ahead_kernel,
        [x_shape, co_z, co_z, f32(6 * YC, XC), f32(YC, XC), co_y, y_row, y_row, y_row],
        [cells] * 2,
        **sizes,
    )(c, c1, m, *z_halo, *y_halo)
    coef = share(numbers)
    link, low, high = call(links_kernel, [f32(YC, XC)] * 3)(coef)
    from_low = lax.ppermute(high, "gz", next_chip)
    from_high = lax.ppermute(low, "gz", last_chip)
    everyone = gather_y(pay)
    numbers, side, co_wide, side_wide = call(
        middle_kernel,
        [f32(4 * YC, XC), side_z, f32(3, ZC - 1, 2, XC), f32(ZC - 1, 2, XC)],
        [line, cells, (7, 40, XC)],
        **sizes,
    )(everyone, co_y1, side, fluxz, m, co_z1, y_entry, *y_halo)
    pair = share(numbers)
    pay, scale = call(
        merge_kernel,
        [f32(chips, 24, XC), f32(24, XC)],
        [(24, XC)],
        spread_to=chips,
        copies=chips,
    )(coef, pair, link, low, high, from_low, from_high)
    pay, send_low, send_high = lax.optimization_barrier((pay, low_y, high_y))
    column = gather_z(pay)
    from_south = lax.ppermute(send_high, "gy", up["gy"])
    from_north = lax.ppermute(send_low, "gy", down["gy"])
    half_line = (chips + 1, HALF, XC)
    (found,) = call(
        chain_kernel, [f32(16, XC)], [half_line, (chips + 1, 1, XC)], chips=chips
    )(column, scale)
    pay, side, fluxz, c2, scale_y = call(
        turn_kernel,
        [f32(groups_y, 3 * ZC, XC), side_y, block, block, f32(2, ZC, XC)],
        [(3, YC, XC), (2, 2, XC), cells, (2 * ZC, XC)] + [cells] * 4 + [(3 * ZC, XC)],
        spread_to=groups_y,
        **sizes,
    )(
        coef,
        pair,
        share(found),
        co_z1,
        side,
        co_wide,
        side_wide,
        z_entry,
        c1,
        m,
        x2,
        co_y2,
        link_y,
        low_y,
        high_y,
        from_south,
        from_north,
        *z_halo,
        *y_halo,
    )
    numbers, side = call(
        later_middle_kernel, [f32(2 * YC, XC), side_z], [line, cells], groups_y=groups_y
    )(gather_y(pay), scale_y, co_y2, side, fluxz, m, co_z2)
    more = share(numbers)
    (pay,) = call(
        later_merge_kernel, [f32(chips, YC, XC)], [(YC, XC)], spread_to=chips, copies=chips
    )(coef, more, scale)
    (found,) = call(later_chain_kernel, [f32(YC, XC)], [half_line], chips=chips)(
        column, gather_z(pay), scale
    )
    (t2,) = call(back_kernel, [block], [(2, YC, XC)])(coef, more, share(found), co_z2, side)
    return t2.reshape(warmth.shape), c2.reshape(cure.shape)


def solution(mesh):
    return jax.shard_map(
        body,
        mesh=mesh,
        in_specs=(P("gz", "gy", None),) * 3,
        out_specs=(P("gz", "gy", None),) * 2,
        check_vma=False,
    )
```

```python
import functools

import jax
import jax.numpy as jnp
from jax import lax
from jax.experimental import pallas as pl
from jax.experimental.pallas import tpu as pltpu
from jax.sharding import PartitionSpec as P

ZC = 16
YC = 8
XC = 128
ROWS = ZC * YC


def f32(*shape):
    return jax.ShapeDtypeStruct(shape, jnp.float32)


def conduct_of(label, cure):
    return jnp.where(label == 1, 40.0, jnp.where(label == 2, 20.0, 0.6 + 0.8 * cure))


def store_of(label):
    return jnp.where(label == 1, 3.0 / 60.0, jnp.where(label == 2, 2.0 / 60.0, 1.0 / 60.0))


def store_by(k):
    return jnp.where(k > 30.0, 3.0 / 60.0, jnp.where(k > 10.0, 2.0 / 60.0, 1.0 / 60.0))


def cure_of(label, warmth, cure):
    speed = 0.3 * jnp.exp(8.0 * warmth)
    return jnp.where(label == 0, 1.0 - (1.0 - cure) * jnp.exp(-speed), cure)


def y_rows(y):
    return pl.ds(y, ZC, stride=YC)


def z_rows(z):
    return pl.ds(z * YC, YC)


def edges_kernel(
    t_in, c_in, m_in, zlo_ref, zhi_ref, ylo_ref, yhi_ref, t_ref, c_ref, m_ref, sem
):
    copies = [
        pltpu.make_async_copy(src, dst, sem.at[i])
        for i, (src, dst) in enumerate(((t_in, t_ref), (c_in, c_ref), (m_in, m_ref)))
    ]
    for copy in copies:
        copy.start()
    for copy in copies:
        copy.wait()

    def put(out, rows):
        t, c, m = t_ref[rows, :], c_ref[rows, :], m_ref[rows, :]
        out[0] = t
        out[1] = conduct_of(m, c)
        out[2] = conduct_of(m, cure_of(m, t, c))

    put(zlo_ref, z_rows(0))
    put(zhi_ref, z_rows(ZC - 1))
    put(ylo_ref, y_rows(0))
    put(yhi_ref, y_rows(YC - 1))


def spread(one_ref, out_ref, sem, count):
    copies = [pltpu.make_async_copy(one_ref, out_ref.at[d], sem.at[d]) for d in range(count)]
    for copy in copies:
        copy.start()
    for copy in copies:
        copy.wait()


def reduce_coefficients(count, store, faces, entry, co_ref):
    ground, edge = store(0), entry
    back_ground = None
    for i in range(count - 1):
        face = faces(i)
        inv = 1.0 / (ground + edge + face)
        edge_inv, face_inv = edge * inv, face * inv
        co_ref[0, i] = inv
        co_ref[1, i] = edge_inv
        co_ref[2, i] = face_inv
        more = edge_inv * ground
        back_ground = more if i == 0 else back_ground + more
        ground = store(i + 1) + face_inv * ground
        edge = edge_inv * face
    return back_ground, edge, ground


def reduce_sides(count, right, co_ref, side_ref):
    side = right(0)
    back_side = None
    for i in range(count - 1):
        side_ref[i] = side * co_ref[0, i]
        more = co_ref[1, i] * side
        back_side = more if i == 0 else back_side + more
        side = right(i + 1) + co_ref[2, i] * side
    return side, back_side


def substitute(count, before, own, co_ref, side_ref, put):
    value = own
    put(count - 1, value)
    for i in range(count - 2, -1, -1):
        value = (side_ref[i] + co_ref[1, i] * before) + co_ref[2, i] * value
        put(i, value)


def edge_lanes():
    lane = lax.broadcasted_iota(jnp.int32, (YC, XC), 1)
    return lane == 0, lane == XC - 1


ROUNDS = 7


def x_coefficients(c_ref, m_ref, x_ref):
    first_lane, last_lane = edge_lanes()
    batch = 4
    for z0 in range(0, ZC, batch):
        gs, ls, rs, stores = [], [], [], []
        for z in range(z0, z0 + batch):
            rows = z_rows(z)
            m = m_ref[rows, :]
            k, g = conduct_of(m, c_ref[rows, :]), store_of(m)
            face_left = 0.5 * (k + jnp.where(first_lane, 0.0, pltpu.roll(k, 1, 1)))
            face_right = jnp.where(last_lane, 0.5 * k, pltpu.roll(face_left, XC - 1, 1))
            x_ref[2 * ROUNDS + 1, rows, :] = face_left
            gs.append(
                g
                + jnp.where(first_lane, face_left, 0.0)
                + jnp.where(last_lane, face_right, 0.0)
            )
            ls.append(jnp.where(first_lane, 0.0, face_left))
            rs.append(jnp.where(last_lane, 0.0, face_right))
            stores.append(g)
        for level in range(ROUNDS):
            low, high = 1 << level, XC - (1 << level)
            for b in range(batch):
                rows = z_rows(z0 + b)
                ground, left, right = gs[b], ls[b], rs[b]
                inv = 1.0 / (ground + left + right)
                to_left = left * pltpu.roll(inv, low, 1)
                to_right = right * pltpu.roll(inv, high, 1)
                x_ref[2 * level, rows, :] = to_left
                x_ref[2 * level + 1, rows, :] = to_right
                gs[b] = (
                    ground
                    + to_left * pltpu.roll(ground, low, 1)
                    + to_right * pltpu.roll(ground, high, 1)
                )
                if level + 1 < ROUNDS:
                    ls[b] = to_left * pltpu.roll(left, low, 1)
                    rs[b] = to_right * pltpu.roll(right, high, 1)
        for b in range(batch):
            x_ref[2 * ROUNDS, z_rows(z0 + b), :] = stores[b] / gs[b]


def x_kernel(c_ref, m_ref, x_ref):
    x_coefficients(c_ref, m_ref, x_ref)


def z_coefficients(groups_z, c_ref, m_ref, below, above, co_ref, num_ref, row):
    ks = [below]
    for z in range(ZC):
        ks.append(conduct_of(m_ref[z_rows(z), :], c_ref[z_rows(z), :]))
    ks.append(above)
    faces = [0.5 * (ks[i] + ks[i + 1]) for i in range(ZC + 1)]
    numbers = reduce_coefficients(
        ZC,
        lambda i: store_of(m_ref[z_rows(i), :]),
        lambda i: faces[i + 1],
        faces[0],
        co_ref,
    )
    at_end = lax.axis_index("gz") == groups_z - 1
    num_ref[row : row + YC] = numbers[0]
    num_ref[row + YC : row + 2 * YC] = numbers[1]
    num_ref[row + 2 * YC : row + 3 * YC] = numbers[2] + jnp.where(at_end, faces[ZC], 0.0)
    return faces[ZC]


def columns_kernel(
    c_ref,
    next_c_ref,
    m_ref,
    below_ref,
    above_ref,
    co1_ref,
    co2_ref,
    num_ref,
    entry_ref,
    *,
    groups_z,
):
    entry_ref[...] = z_coefficients(
        groups_z, c_ref, m_ref, below_ref[1], above_ref[1], co1_ref, num_ref, 0
    )
    z_coefficients(
        groups_z, next_c_ref, m_ref, below_ref[2], above_ref[2], co2_ref, num_ref, 3 * YC
    )


def ahead_kernel(
    next_c_ref,
    m_ref,
    south_ref,
    north_ref,
    x_ref,
    co_y_ref,
    link_ref,
    low_ref,
    high_ref,
    k_ref,
    g_ref,
    *,
    groups_y,
):
    m = m_ref[...]
    k_ref[...] = conduct_of(m, next_c_ref[...])
    g_ref[...] = store_of(m)
    ks = [south_ref[2]] + [k_ref[y_rows(y), :] for y in range(YC)] + [north_ref[2]]
    faces = [0.5 * (ks[i] + ks[i + 1]) for i in range(YC + 1)]
    back_ground, edge, ground = reduce_coefficients(
        YC, lambda i: g_ref[y_rows(i), :], lambda i: faces[i + 1], faces[0], co_y_ref
    )
    at_end = lax.axis_index("gy") == groups_y - 1
    link_ref[...] = edge
    low_ref[...] = back_ground + edge
    high_ref[...] = ground + edge + jnp.where(at_end, faces[YC], 0.0)
    x_coefficients(next_c_ref, m_ref, x_ref)


def flow_rhs(t_ref, c_ref, m_ref, x_ref, zt, yt, zk, yk, outs, scratch):
    fluxz_ref, cure_ref = outs
    k_ref, g_ref, fy_ref, r_ref = scratch
    t, c, m = t_ref[...], c_ref[...], m_ref[...]
    k_ref[...] = conduct_of(m, c)
    g_ref[...] = store_of(m)
    cure_ref[...] = cure_of(m, t, c)

    ks = [yk[0]] + [k_ref[y_rows(y), :] for y in range(YC)] + [yk[1]]
    ts = [yt[0]] + [t_ref[y_rows(y), :] for y in range(YC)] + [yt[1]]
    face_y = [0.5 * (ks[i] + ks[i + 1]) for i in range(YC + 1)]
    flow_y = [face_y[i] * (ts[i + 1] - ts[i]) for i in range(YC + 1)]
    for y in range(YC):
        fy_ref[y_rows(y), :] = flow_y[y + 1] - flow_y[y]

    first_lane, last_lane = edge_lanes()
    k_prev, t_prev = zk[0], zt[0]
    flow_prev = 0.5 * (k_prev + k_ref[z_rows(0), :]) * (t_ref[z_rows(0), :] - t_prev)
    batch = 4
    for z0 in range(0, ZC, batch):
        sides = []
        for z in range(z0, z0 + batch):
            rows = z_rows(z)
            kz, tz = k_ref[rows, :], t_ref[rows, :]
            k_next = k_ref[z_rows(z + 1), :] if z + 1 < ZC else zk[1]
            t_next = t_ref[z_rows(z + 1), :] if z + 1 < ZC else zt[1]
            flow_next = 0.5 * (kz + k_next) * (t_next - tz)
            flux_z = flow_next - flow_prev
            flow_prev = flow_next
            fluxz_ref[rows, :] = flux_z
            t_left = jnp.where(first_lane, 0.0, pltpu.roll(tz, 1, 1))
            flow_left = x_ref[2 * ROUNDS + 1, rows, :] * (tz - t_left)
            flow_right = jnp.where(last_lane, -0.5 * kz * tz, pltpu.roll(flow_left, XC - 1, 1))
            delta = cure_ref[rows, :] - c_ref[rows, :]
            sides.append(
                g_ref[rows, :] * (tz + 0.4 * delta)
                + (flow_right - flow_left)
                + 2.0 * (fy_ref[rows, :] + flux_z)
            )
        for level in range(ROUNDS):
            low, high = 1 << level, XC - (1 << level)
            for b in range(batch):
                rows = z_rows(z0 + b)
                side = sides[b]
                sides[b] = (
                    side
                    + x_ref[2 * level, rows, :] * pltpu.roll(side, low, 1)
                    + x_ref[2 * level + 1, rows, :] * pltpu.roll(side, high, 1)
                )
        for b in range(batch):
            rows = z_rows(z0 + b)
            r_ref[rows, :] = x_ref[2 * ROUNDS, rows, :] * sides[b] - fy_ref[rows, :]
    return face_y


def front_kernel(
    t_ref,
    c_ref,
    m_ref,
    x_ref,
    below_ref,
    above_ref,
    south_ref,
    north_ref,
    pay_ref,
    co1_ref,
    side_ref,
    fluxz_ref,
    cure_ref,
    entry_ref,
    k_ref,
    g_ref,
    fy_ref,
    r_ref,
    p_ref,
    sem,
    *,
    groups,
):
    face_y = flow_rhs(
        t_ref,
        c_ref,
        m_ref,
        x_ref,
        (below_ref[0], above_ref[0]),
        (south_ref[0], north_ref[0]),
        (below_ref[1], above_ref[1]),
        (south_ref[1], north_ref[1]),
        (fluxz_ref, cure_ref),
        (k_ref, g_ref, fy_ref, r_ref),
    )
    entry_ref[...] = face_y[YC]
    at_end = lax.axis_index("gy") == groups - 1
    back_ground, edge, ground = reduce_coefficients(
        YC, lambda i: g_ref[y_rows(i), :], lambda i: face_y[i + 1], face_y[0], co1_ref
    )
    ground = ground + jnp.where(at_end, face_y[YC], 0.0)
    side, back_side = reduce_sides(YC, lambda i: r_ref[y_rows(i), :], co1_ref, side_ref)
    for y, row in ((0, 5 * ZC), (YC - 1, 5 * ZC + 4)):
        for i, corner in enumerate((below_ref[0], above_ref[0], below_ref[1], above_ref[1])):
            p_ref[row + i : row + i + 1] = corner[y : y + 1]
    numbers = (back_ground, edge, ground, side, back_side)
    for q, number in enumerate(numbers):
        p_ref[ZC * q : ZC * q + ZC] = number
    spread(p_ref, pay_ref, sem, groups)


def chain(count, read, put):
    def ground_of(j):
        return read(j, 2) + read(j + 1, 0) if j + 1 < count else read(j, 2)

    def side_of(j):
        return read(j, 3) + read(j + 1, 4) if j + 1 < count else read(j, 3)

    half = count // 2
    gain, part = [None] * count, [None] * count
    ground_l, side_l = ground_of(0) + read(0, 1), side_of(0)
    ground_r, side_r = ground_of(count - 1), side_of(count - 1)
    for i in range(half - 1):
        edge = read(i + 1, 1)
        inv = 1.0 / (ground_l + edge)
        gain[i], part[i] = edge * inv, side_l * inv
        ground_l = ground_of(i + 1) + gain[i] * ground_l
        side_l = side_of(i + 1) + gain[i] * side_l
        j = count - 1 - i
        edge = read(j, 1)
        inv = 1.0 / (ground_r + edge)
        gain[j], part[j] = edge * inv, side_r * inv
        ground_r = ground_of(j - 1) + gain[j] * ground_r
        side_r = side_of(j - 1) + gain[j] * side_r
    edge = read(half, 1)
    inv = 1.0 / (ground_l * ground_r + edge * (ground_l + ground_r))
    low = (side_l * (ground_r + edge) + edge * side_r) * inv
    high = (side_r * (ground_l + edge) + edge * side_l) * inv
    put(half - 1, low)
    put(half, high)
    for i in range(half - 2, -1, -1):
        low = part[i] + gain[i] * low
        put(i, low)
        j = count - 1 - i
        high = part[j] + gain[j] * high
        put(j, high)


def first_of_next(own, after, back_ground, edge, back_side, entry):
    return own - (back_ground * own + edge * (own - after) - back_side) / entry


def substitute_y(before, own, co_ref, side_ref, v_ref):
    def place(i, value):
        v_ref[y_rows(i), :] = value

    substitute(YC, before, own, co_ref, side_ref, place)


def block_rows(q):
    return pl.ds(YC * q, YC)


def wide_rows(q):
    return pl.ds(2 * YC + 2 * q, 2)


def middle_kernel(
    all_ref,
    co_y_ref,
    side_y_ref,
    fluxz_ref,
    m_ref,
    co_z_ref,
    y_entry_ref,
    south_ref,
    north_ref,
    p_ref,
    side_z_ref,
    co_wide_ref,
    side_wide_ref,
    s_ref,
    v_ref,
    h_ref,
    *,
    groups_y,
    groups_z,
):
    def read(j, q):
        return all_ref[j, ZC * q : ZC * q + ZC, :]

    s_ref[0] = jnp.zeros((ZC, XC), jnp.float32)

    def put(j, value):
        s_ref[j + 1] = value

    chain(groups_y, read, put)
    me = lax.axis_index("gy")
    before, own = s_ref[me], s_ref[me + 1]
    substitute_y(before, own, co_y_ref, side_y_ref, v_ref)

    def right(i):
        return store_of(m_ref[z_rows(i), :]) * v_ref[z_rows(i), :] - fluxz_ref[z_rows(i), :]

    sides = reduce_sides(ZC, right, co_z_ref, side_z_ref)
    p_ref[24:32, :] = jnp.zeros((8, XC), jnp.float32)
    p_ref[block_rows(0), :] = sides[0]
    p_ref[block_rows(1), :] = sides[1]

    then = jnp.minimum(me + 1, groups_y - 1)
    north = first_of_next(
        own,
        s_ref[then + 1],
        all_ref[then, 0:16, :],
        all_ref[then, 16:32, :],
        all_ref[then, 64:80, :],
        y_entry_ref[...],
    )
    last = jnp.maximum(me - 1, 0)
    beside = (
        (0, before, south_ref, all_ref[last, 5 * ZC + 4 : 5 * ZC + 8, :]),
        (1, north, north_ref, all_ref[then, 5 * ZC : 5 * ZC + 4, :]),
    )
    for side, value, halo_ref, corners in beside:
        rows = pl.ds(2 + side, ZC, stride=2)
        for q in range(2):
            h_ref[q, rows, :] = halo_ref[q]
            h_ref[q, side : side + 1, :] = corners[2 * q : 2 * q + 1]
            h_ref[q, 34 + side : 35 + side, :] = corners[2 * q + 1 : 2 * q + 2]
        h_ref[2, rows, :] = value
    faces = 0.5 * (h_ref[1, 0:34, :] + h_ref[1, 2:36, :])
    h_ref[3, 0:34, :] = faces
    h_ref[4, 0:34, :] = faces * (h_ref[0, 2:36, :] - h_ref[0, 0:34, :])
    capacity = store_by(h_ref[1, 2:34, :])
    h_ref[5, 0:32, :] = capacity
    h_ref[6, 0:32, :] = capacity * h_ref[2, 2:34, :] - (h_ref[4, 2:34, :] - h_ref[4, 0:32, :])
    numbers = reduce_coefficients(
        ZC,
        lambda i: h_ref[5, 2 * i : 2 * i + 2, :],
        lambda i: h_ref[3, 2 * i + 2 : 2 * i + 4, :],
        h_ref[3, 0:2, :],
        co_wide_ref,
    )
    sides = reduce_sides(
        ZC, lambda i: h_ref[6, 2 * i : 2 * i + 2, :], co_wide_ref, side_wide_ref
    )
    at_end = lax.axis_index("gz") == groups_z - 1
    p_ref[wide_rows(0), :] = numbers[0]
    p_ref[wide_rows(1), :] = numbers[1]
    p_ref[wide_rows(2), :] = numbers[2] + jnp.where(at_end, h_ref[3, 32:34, :], 0.0)
    p_ref[wide_rows(3), :] = sides[0]
    p_ref[wide_rows(4), :] = sides[1]


def later_middle_kernel(
    all_ref,
    scale_ref,
    co_y_ref,
    side_y_ref,
    fluxz_ref,
    m_ref,
    co_z_ref,
    p_ref,
    side_z_ref,
    s_ref,
    v_ref,
    *,
    groups_y,
):
    s_ref[0] = jnp.zeros((ZC, XC), jnp.float32)

    def side_of(j):
        side = all_ref[j, ZC : 2 * ZC, :]
        return side + all_ref[j + 1, 2 * ZC : 3 * ZC, :] if j + 1 < groups_y else side

    def put(j, value):
        s_ref[j + 1] = value

    unit_chain(groups_y, lambda j: all_ref[j, 0:ZC, :], side_of, put)
    me = lax.axis_index("gy")
    before, own = s_ref[me] * scale_ref[1], s_ref[me + 1] * scale_ref[0]
    substitute_y(before, own, co_y_ref, side_y_ref, v_ref)

    def right(i):
        return store_of(m_ref[z_rows(i), :]) * v_ref[z_rows(i), :] - fluxz_ref[z_rows(i), :]

    sides = reduce_sides(ZC, right, co_z_ref, side_z_ref)
    p_ref[0:YC] = sides[0]
    p_ref[YC : 2 * YC] = sides[1]


HALF = YC // 2


def node_between(low, high):
    ground = low[2] + high[0]
    return ground, 1.0 / (ground + low[1] + high[1])


def merged_coefficients(low, high):
    ground, inv = node_between(low, high)
    low_inv, high_inv = low[1] * inv, high[1] * inv
    return low[0] + low_inv * ground, low_inv * high[1], high[2] + high_inv * ground


def merged_sides(low, high):
    _, inv = node_between(low, high)
    side = low[3] + high[4]
    return high[3] + high[1] * inv * side, low[4] + low[1] * inv * side


def block_numbers(coef_ref, side_ref, step):
    return [
        [coef_ref[core, block_rows(3 * step + q), :] for q in range(3)]
        + [side_ref[core, block_rows(q), :] for q in range(2)]
        for core in range(2)
    ]


def wide_numbers(side_ref):
    return [[side_ref[core, wide_rows(q), :] for q in range(5)] for core in range(2)]


def my_half(number):
    half = number.shape[0] // 2
    core = lax.rem(lax.axis_index("gz"), 2)
    return jnp.where(core == 0, number[:half], number[half:])


def halves(q):
    return pl.ds(HALF * q, HALF)


def links_kernel(coef_ref, link_ref, low_ref, high_ref):
    for step in range(2):
        low, high = (
            [coef_ref[core, block_rows(3 * step + q), :] for q in range(3)] for core in range(2)
        )
        back_ground, edge, ground = merged_coefficients(low, high)
        link_ref[halves(step), :] = my_half(edge)
        low_ref[halves(step), :] = my_half(back_ground + edge)
        high_ref[halves(step), :] = my_half(ground + edge)


def merge_kernel(
    coef_ref,
    pair_ref,
    link_ref,
    low_ref,
    high_ref,
    from_low_ref,
    from_high_ref,
    pay_ref,
    scale_ref,
    p_ref,
    sem,
    *,
    copies,
):
    p_ref[16:24] = jnp.zeros((8, XC), jnp.float32)
    for step in range(2):
        rows = halves(step)
        own = high_ref[rows, :] + from_high_ref[rows, :]
        root = jnp.sqrt(own)
        own_inv = 1.0 / root
        last_inv = 1.0 / jnp.sqrt(from_low_ref[rows, :] + low_ref[rows, :])
        scale_ref[halves(2 * step), :] = own_inv
        scale_ref[halves(2 * step + 1), :] = last_inv
        p_ref[halves(3 * step), :] = link_ref[rows, :] * (own_inv * last_inv)
        if step == 0:
            scale_ref[halves(4), :] = root
            scale_ref[halves(5), :] = from_high_ref[rows, :]
    low, high = block_numbers(coef_ref, pair_ref, 0)
    side, back_side = merged_sides(low, high)
    p_ref[halves(1), :] = my_half(side) * scale_ref[halves(0), :]
    p_ref[halves(2), :] = my_half(back_side) * scale_ref[halves(1), :]
    low, high = wide_numbers(pair_ref)
    for q, number in enumerate(merged_coefficients(low, high) + merged_sides(low, high)):
        p_ref[16 + q : 17 + q] = my_half(number)
    spread(p_ref, pay_ref, sem, copies)


def later_merge_kernel(coef_ref, more_ref, scale_ref, pay_ref, p_ref, sem, *, copies):
    side, back_side = merged_sides(*block_numbers(coef_ref, more_ref, 1))
    p_ref[halves(0), :] = my_half(side) * scale_ref[halves(2), :]
    p_ref[halves(1), :] = my_half(back_side) * scale_ref[halves(3), :]
    spread(p_ref, pay_ref, sem, copies)


def unit_chain(count, link, side_of, put):
    half = count // 2
    gain, part = [None] * count, [None] * count
    diag_l = diag_r = None
    side_l, side_r = side_of(0), side_of(count - 1)
    for i in range(half - 1):
        j = count - 1 - i
        edge_l, edge_r = link(i + 1), link(j)
        if i == 0:
            gain[i], part[i], gain[j], part[j] = edge_l, side_l, edge_r, side_r
        else:
            inv_l, inv_r = 1.0 / diag_l, 1.0 / diag_r
            gain[i], part[i] = edge_l * inv_l, side_l * inv_l
            gain[j], part[j] = edge_r * inv_r, side_r * inv_r
        diag_l = 1.0 - edge_l * gain[i]
        side_l = side_of(i + 1) + edge_l * part[i]
        diag_r = 1.0 - edge_r * gain[j]
        side_r = side_of(j - 1) + edge_r * part[j]
    edge = link(half)
    if half == 1:
        diag_l = diag_r = jnp.ones_like(edge)
    inv = 1.0 / (diag_l * diag_r - edge * edge)
    low = (side_l * diag_r + edge * side_r) * inv
    high = (side_r * diag_l + edge * side_l) * inv
    put(half - 1, low)
    put(half, high)
    for i in range(half - 2, -1, -1):
        low = part[i] + gain[i] * low
        put(i, low)
        j = count - 1 - i
        high = part[j] + gain[j] * high
        put(j, high)


def chain_kernel(all_ref, scale_ref, out_ref, s_ref, w_ref, *, chips):
    s_ref[0] = jnp.zeros((HALF, XC), jnp.float32)
    w_ref[0] = jnp.zeros((1, XC), jnp.float32)

    def side_of(j):
        side = all_ref[j, halves(1), :]
        return side + all_ref[j + 1, halves(2), :] if j + 1 < chips else side

    def put(j, value):
        s_ref[j + 1] = value

    def put_wide(j, value):
        w_ref[j + 1] = value

    unit_chain(chips, lambda j: all_ref[j, halves(0), :], side_of, put)
    chain(chips, lambda j, q: all_ref[j, 16 + q : 17 + q, :], put_wide)
    me = lax.div(lax.axis_index("gz"), 2)
    then = jnp.minimum(me + 1, chips - 1)
    own = s_ref[me + 1] * scale_ref[halves(0), :]
    inflow = all_ref[then, halves(0), :] * s_ref[then + 1] + all_ref[then, halves(2), :]
    out_ref[8:16] = jnp.zeros((8, XC), jnp.float32)
    out_ref[halves(0), :] = s_ref[me] * scale_ref[halves(1), :]
    out_ref[halves(1), :] = own
    out_ref[halves(2), :] = scale_ref[halves(5), :] * own - scale_ref[halves(4), :] * inflow
    out_ref[12:13] = w_ref[me]
    out_ref[13:14] = w_ref[me + 1]


def later_chain_kernel(all_ref, more_ref, scale_ref, out_ref, s_ref, *, chips):
    s_ref[0] = jnp.zeros((HALF, XC), jnp.float32)

    def side_of(j):
        side = more_ref[j, halves(0), :]
        return side + more_ref[j + 1, halves(1), :] if j + 1 < chips else side

    def put(j, value):
        s_ref[j + 1] = value

    unit_chain(chips, lambda j: all_ref[j, halves(3), :], side_of, put)
    me = lax.div(lax.axis_index("gz"), 2)
    out_ref[halves(0), :] = s_ref[me] * scale_ref[halves(3), :]
    out_ref[halves(1), :] = s_ref[me + 1] * scale_ref[halves(2), :]


def ends_of(low, high, before, last):
    _, inv = node_between(low, high)
    node = (low[3] + high[4] + low[1] * before + high[1] * last) * inv
    upper = lax.rem(lax.axis_index("gz"), 2) == 1
    return jnp.where(upper, node, before), jnp.where(upper, last, node), node


def joined(res_ref, u_ref, count):
    for q in range(count):
        for core in range(2):
            u_ref[q, halves(core), :] = res_ref[core, halves(q), :]


def back_kernel(coef_ref, more_ref, res_ref, co_z_ref, side_z_ref, t_ref, u_ref):
    joined(res_ref, u_ref, 2)
    low, high = block_numbers(coef_ref, more_ref, 1)
    before, own, _ = ends_of(low, high, u_ref[0], u_ref[1])

    def place(i, value):
        t_ref[z_rows(i), :] = value

    substitute(ZC, before, own, co_z_ref, side_z_ref, place)


def turn_kernel(
    coef_ref,
    pair_ref,
    res_ref,
    co_z_ref,
    side_z_ref,
    co_wide_ref,
    side_wide_ref,
    z_entry_ref,
    c_ref,
    m_ref,
    x_ref,
    co_y_ref,
    link_ref,
    low_ref,
    high_ref,
    from_low_ref,
    from_high_ref,
    below_ref,
    above_ref,
    south_ref,
    north_ref,
    pay_ref,
    side_y_ref,
    fluxz_ref,
    cure_ref,
    scale_ref,
    u_ref,
    w_ref,
    t_ref,
    e_ref,
    k_ref,
    g_ref,
    fy_ref,
    r_ref,
    p_ref,
    sem,
    *,
    groups_y,
    groups_z,
):
    joined(res_ref, u_ref, 3)
    low, high = block_numbers(coef_ref, pair_ref, 0)
    last = u_ref[1]
    before, own, node = ends_of(low, high, u_ref[0], last)

    def place(i, value):
        t_ref[z_rows(i), :] = value

    substitute(ZC, before, own, co_z_ref, side_z_ref, place)
    me = lax.axis_index("gz")
    inside = high[0] * node + high[1] * (node - last) - high[4]
    current = jnp.where(lax.rem(me, 2) == 1, u_ref[2], inside)
    above = jnp.where(me == groups_z - 1, 0.0, own - current / z_entry_ref[...])

    for q in range(2):
        for core in range(2):
            w_ref[q, core : core + 1] = res_ref[core, 12 + q : 13 + q, :]
    low, high = wide_numbers(pair_ref)
    before_wide, own_wide, _ = ends_of(low, high, w_ref[0], w_ref[1])

    def place_wide(i, value):
        e_ref[2 * i : 2 * i + 2] = value

    substitute(ZC, before_wide, own_wide, co_wide_ref, side_wide_ref, place_wide)
    row = lax.axis_index("gy")
    south = jnp.where(row == 0, 0.0, e_ref[pl.ds(0, ZC, stride=2), :])
    north = jnp.where(row == groups_y - 1, 0.0, e_ref[pl.ds(1, ZC, stride=2), :])
    flow_rhs(
        t_ref,
        c_ref,
        m_ref,
        x_ref,
        (before, above),
        (south, north),
        (below_ref[2], above_ref[2]),
        (south_ref[2], north_ref[2]),
        (fluxz_ref, cure_ref),
        (k_ref, g_ref, fy_ref, r_ref),
    )
    side, back_side = reduce_sides(YC, lambda i: r_ref[y_rows(i), :], co_y_ref, side_y_ref)
    own_inv = 1.0 / jnp.sqrt(high_ref[...] + from_high_ref[...])
    last_inv = 1.0 / jnp.sqrt(from_low_ref[...] + low_ref[...])
    scale_ref[0] = own_inv
    scale_ref[1] = last_inv
    p_ref[0:ZC] = link_ref[...] * (own_inv * last_inv)
    p_ref[ZC : 2 * ZC] = side * own_inv
    p_ref[2 * ZC : 3 * ZC] = back_side * last_inv
    spread(p_ref, pay_ref, sem, groups_y)


def call(kernel, outs, scratch=(), spread_to=0, **static):
    out_specs = [pl.BlockSpec(memory_space=pltpu.VMEM)] * len(outs)
    shapes = [pltpu.VMEM(shape, jnp.float32) for shape in scratch]
    if spread_to:
        out_specs[0] = pl.BlockSpec(memory_space=pl.ANY)
        shapes.append(pltpu.SemaphoreType.DMA((spread_to,)))
    return pl.pallas_call(
        functools.partial(kernel, **static),
        out_shape=tuple(outs),
        out_specs=tuple(out_specs),
        scratch_shapes=shapes,
        compiler_params=pltpu.CompilerParams(vmem_limit_bytes=12 * 1024 * 1024),
        name=kernel.__name__,
    )


def body(warmth, cure, label):
    groups_z, groups_y = lax.axis_size("gz"), lax.axis_size("gy")
    chips = groups_z // 2
    up = {a: [(i, i + 1) for i in range(n - 1)] for a, n in (("gz", groups_z), ("gy", groups_y))}
    down = {a: [(j, i) for i, j in up[a]] for a in up}
    pairs = [[2 * i, 2 * i + 1] for i in range(chips)]
    same_core = [[2 * i + core for i in range(chips)] for core in range(2)]
    cells = (ROWS, XC)
    block = f32(*cells)

    zlo, zhi, ylo, yhi, t, c, m = pl.pallas_call(
        edges_kernel,
        out_shape=(
            f32(3, YC, XC),
            f32(3, YC, XC),
            f32(3, ZC, XC),
            f32(3, ZC, XC),
            block,
            block,
            jax.ShapeDtypeStruct(cells, jnp.int32),
        ),
        in_specs=[pl.BlockSpec(memory_space=pltpu.HBM)] * 3,
        scratch_shapes=[pltpu.SemaphoreType.DMA((3,))],
        compiler_params=pltpu.CompilerParams(vmem_limit_bytes=12 * 1024 * 1024),
        name="edges_kernel",
    )(*(pltpu.with_memory_space_constraint(a.reshape(cells), pltpu.HBM) for a in (warmth, cure, label)))
    z_halo = (lax.ppermute(zhi, "gz", up["gz"]), lax.ppermute(zlo, "gz", down["gz"]))
    y_halo = (lax.ppermute(yhi, "gy", up["gy"]), lax.ppermute(ylo, "gy", down["gy"]))

    def gather_y(pay):
        return lax.all_to_all(pay, "gy", 0, 0, tiled=True)

    def gather_z(pay):
        return lax.all_to_all(pay, "gz", 0, 0, tiled=True, axis_index_groups=same_core)

    def share(numbers):
        return lax.all_gather(numbers, "gz", axis_index_groups=pairs)

    sizes = dict(groups_y=groups_y, groups_z=groups_z)
    co_y, side_y = f32(3, YC - 1, ZC, XC), f32(YC - 1, ZC, XC)
    co_z, side_z = f32(3, ZC - 1, YC, XC), f32(ZC - 1, YC, XC)
    next_chip = [(i, i + 2) for i in range(groups_z - 2)]
    last_chip = [(j, i) for i, j in next_chip]
    x_shape = f32(2 * ROUNDS + 2, ROWS, XC)
    line = (groups_y + 1, ZC, XC)

    (x1,) = call(x_kernel, [x_shape])(c, m)
    pay, co_y1, side, fluxz, c1, y_entry = call(
        front_kernel,
        [f32(groups_y, 5 * ZC + 8, XC), co_y, side_y, block, block, f32(ZC, XC)],
        [cells] * 4 + [(5 * ZC + 8, XC)],
        spread_to=groups_y,
        groups=groups_y,
    )(t, c, m, x1, *z_halo, *y_halo)
    co_z1, co_z2, numbers, z_entry = call(
        columns_kernel,
        [co_z, co_z, f32(6 * YC, XC), f32(YC, XC)],
        groups_z=groups_z,
    )(c, c1, m, *z_halo)
    coef = share(numbers)
    link, low, high = call(links_kernel, [f32(YC, XC)] * 3)(coef)
    from_low = lax.ppermute(high, "gz", next_chip)
    from_high = lax.ppermute(low, "gz", last_chip)
    y_row = f32(ZC, XC)
    x2, co_y2, link_y, low_y, high_y = call(
        ahead_kernel,
        [x_shape, co_y, y_row, y_row, y_row],
        [cells] * 2,
        groups_y=groups_y,
    )(c1, m, *y_halo)
    everyone = gather_y(pay)
    numbers, side, co_wide, side_wide = call(
        middle_kernel,
        [f32(4 * YC, XC), side_z, f32(3, ZC - 1, 2, XC), f32(ZC - 1, 2, XC)],
        [line, cells, (7, 40, XC)],
        **sizes,
    )(everyone, co_y1, side, fluxz, m, co_z1, y_entry, *y_halo)
    pair = share(numbers)
    pay, scale = call(
        merge_kernel,
        [f32(chips, 24, XC), f32(24, XC)],
        [(24, XC)],
        spread_to=chips,
        copies=chips,
    )(coef, pair, link, low, high, from_low, from_high)
    pay, send_low, send_high = lax.optimization_barrier((pay, low_y, high_y))
    column = gather_z(pay)
    from_south = lax.ppermute(send_high, "gy", up["gy"])
    from_north = lax.ppermute(send_low, "gy", down["gy"])
    half_line = (chips + 1, HALF, XC)
    (found,) = call(
        chain_kernel, [f32(16, XC)], [half_line, (chips + 1, 1, XC)], chips=chips
    )(column, scale)
    pay, side, fluxz, c2, scale_y = call(
        turn_kernel,
        [f32(groups_y, 3 * ZC, XC), side_y, block, block, f32(2, ZC, XC)],
        [(3, YC, XC), (2, 2, XC), cells, (2 * ZC, XC)] + [cells] * 4 + [(3 * ZC, XC)],
        spread_to=groups_y,
        **sizes,
    )(
        coef,
        pair,
        share(found),
        co_z1,
        side,
        co_wide,
        side_wide,
        z_entry,
        c1,
        m,
        x2,
        co_y2,
        link_y,
        low_y,
        high_y,
        from_south,
        from_north,
        *z_halo,
        *y_halo,
    )
    numbers, side = call(
        later_middle_kernel, [f32(2 * YC, XC), side_z], [line, cells], groups_y=groups_y
    )(gather_y(pay), scale_y, co_y2, side, fluxz, m, co_z2)
    more = share(numbers)
    (pay,) = call(
        later_merge_kernel, [f32(chips, YC, XC)], [(YC, XC)], spread_to=chips, copies=chips
    )(coef, more, scale)
    (found,) = call(later_chain_kernel, [f32(YC, XC)], [half_line], chips=chips)(
        column, gather_z(pay), scale
    )
    (t2,) = call(back_kernel, [block], [(2, YC, XC)])(coef, more, share(found), co_z2, side)
    return t2.reshape(warmth.shape), c2.reshape(cure.shape)


def solution(mesh):
    return jax.shard_map(
        body,
        mesh=mesh,
        in_specs=(P("gz", "gy", None),) * 3,
        out_specs=(P("gz", "gy", None),) * 2,
        check_vma=False,
    )
```

```python
import functools

import jax
import jax.numpy as jnp
from jax import lax
from jax.experimental import pallas as pl
from jax.experimental.pallas import tpu as pltpu
from jax.sharding import PartitionSpec as P

ZC = 16
YC = 8
XC = 128
ROWS = ZC * YC


def f32(*shape):
    return jax.ShapeDtypeStruct(shape, jnp.float32)


def conduct_of(label, cure):
    return jnp.where(label == 1, 40.0, jnp.where(label == 2, 20.0, 0.6 + 0.8 * cure))


def store_of(label):
    return jnp.where(label == 1, 3.0 / 60.0, jnp.where(label == 2, 2.0 / 60.0, 1.0 / 60.0))


def store_by(k):
    return jnp.where(k > 30.0, 3.0 / 60.0, jnp.where(k > 10.0, 2.0 / 60.0, 1.0 / 60.0))


def cure_of(label, warmth, cure):
    speed = 0.3 * jnp.exp(8.0 * warmth)
    return jnp.where(label == 0, 1.0 - (1.0 - cure) * jnp.exp(-speed), cure)


def y_rows(y):
    return pl.ds(y, ZC, stride=YC)


def z_rows(z):
    return pl.ds(z * YC, YC)


def edges_kernel(
    t_in, c_in, m_in, zlo_ref, zhi_ref, ylo_ref, yhi_ref, t_ref, c_ref, m_ref, sem
):
    copies = [
        pltpu.make_async_copy(src, dst, sem.at[i])
        for i, (src, dst) in enumerate(((t_in, t_ref), (c_in, c_ref), (m_in, m_ref)))
    ]
    for copy in copies:
        copy.start()
    for copy in copies:
        copy.wait()

    def put(out, rows):
        t, c, m = t_ref[rows, :], c_ref[rows, :], m_ref[rows, :]
        out[0] = t
        out[1] = conduct_of(m, c)
        out[2] = conduct_of(m, cure_of(m, t, c))

    put(zlo_ref, z_rows(0))
    put(zhi_ref, z_rows(ZC - 1))
    put(ylo_ref, y_rows(0))
    put(yhi_ref, y_rows(YC - 1))


def spread(one_ref, out_ref, sem, count):
    copies = [pltpu.make_async_copy(one_ref, out_ref.at[d], sem.at[d]) for d in range(count)]
    for copy in copies:
        copy.start()
    for copy in copies:
        copy.wait()


def reduce_coefficients(count, store, faces, entry, co_ref):
    ground, edge = store(0), entry
    back_ground = None
    for i in range(count - 1):
        face = faces(i)
        inv = 1.0 / (ground + edge + face)
        edge_inv, face_inv = edge * inv, face * inv
        co_ref[0, i] = inv
        co_ref[1, i] = edge_inv
        co_ref[2, i] = face_inv
        more = edge_inv * ground
        back_ground = more if i == 0 else back_ground + more
        ground = store(i + 1) + face_inv * ground
        edge = edge_inv * face
    return back_ground, edge, ground


def reduce_sides(count, right, co_ref, side_ref):
    side = right(0)
    back_side = None
    for i in range(count - 1):
        side_ref[i] = side * co_ref[0, i]
        more = co_ref[1, i] * side
        back_side = more if i == 0 else back_side + more
        side = right(i + 1) + co_ref[2, i] * side
    return side, back_side


def substitute(count, before, own, co_ref, side_ref, put):
    value = own
    put(count - 1, value)
    for i in range(count - 2, -1, -1):
        value = (side_ref[i] + co_ref[1, i] * before) + co_ref[2, i] * value
        put(i, value)


def edge_lanes():
    lane = lax.broadcasted_iota(jnp.int32, (YC, XC), 1)
    return lane == 0, lane == XC - 1


ROUNDS = 7


def x_coefficients(c_ref, m_ref, x_ref):
    first_lane, last_lane = edge_lanes()
    batch = 4
    for z0 in range(0, ZC, batch):
        gs, ls, rs, stores = [], [], [], []
        for z in range(z0, z0 + batch):
            rows = z_rows(z)
            m = m_ref[rows, :]
            k, g = conduct_of(m, c_ref[rows, :]), store_of(m)
            face_left = 0.5 * (k + jnp.where(first_lane, 0.0, pltpu.roll(k, 1, 1)))
            face_right = jnp.where(last_lane, 0.5 * k, pltpu.roll(face_left, XC - 1, 1))
            x_ref[2 * ROUNDS + 1, rows, :] = face_left
            gs.append(
                g
                + jnp.where(first_lane, face_left, 0.0)
                + jnp.where(last_lane, face_right, 0.0)
            )
            ls.append(jnp.where(first_lane, 0.0, face_left))
            rs.append(jnp.where(last_lane, 0.0, face_right))
            stores.append(g)
        for level in range(ROUNDS):
            low, high = 1 << level, XC - (1 << level)
            for b in range(batch):
                rows = z_rows(z0 + b)
                ground, left, right = gs[b], ls[b], rs[b]
                inv = 1.0 / (ground + left + right)
                up, down = right * inv, left * inv
                x_ref[2 * level, rows, :] = up
                x_ref[2 * level + 1, rows, :] = down
                gs[b] = (
                    ground + pltpu.roll(up * ground, low, 1) + pltpu.roll(down * ground, high, 1)
                )
                if level + 1 < ROUNDS:
                    link = up * left
                    ls[b] = pltpu.roll(link, low, 1)
                    rs[b] = pltpu.roll(link, high, 1)
        for b in range(batch):
            x_ref[2 * ROUNDS, z_rows(z0 + b), :] = stores[b] / gs[b]


def x_kernel(c_ref, m_ref, x_ref):
    x_coefficients(c_ref, m_ref, x_ref)


def z_coefficients(groups_z, c_ref, m_ref, below, above, co_ref, num_ref, row):
    ks = [below]
    for z in range(ZC):
        ks.append(conduct_of(m_ref[z_rows(z), :], c_ref[z_rows(z), :]))
    ks.append(above)
    faces = [0.5 * (ks[i] + ks[i + 1]) for i in range(ZC + 1)]
    numbers = reduce_coefficients(
        ZC,
        lambda i: store_of(m_ref[z_rows(i), :]),
        lambda i: faces[i + 1],
        faces[0],
        co_ref,
    )
    at_end = lax.axis_index("gz") == groups_z - 1
    num_ref[row : row + YC] = numbers[0]
    num_ref[row + YC : row + 2 * YC] = numbers[1]
    num_ref[row + 2 * YC : row + 3 * YC] = numbers[2] + jnp.where(at_end, faces[ZC], 0.0)
    return faces[ZC]


def ahead_kernel(
    c_ref,
    next_c_ref,
    m_ref,
    below_ref,
    above_ref,
    south_ref,
    north_ref,
    x_ref,
    co1_ref,
    co2_ref,
    num_ref,
    entry_ref,
    co_y_ref,
    link_ref,
    low_ref,
    high_ref,
    k_ref,
    g_ref,
    *,
    groups_y,
    groups_z,
):
    m = m_ref[...]
    k_ref[...] = conduct_of(m, next_c_ref[...])
    g_ref[...] = store_of(m)
    ks = [south_ref[2]] + [k_ref[y_rows(y), :] for y in range(YC)] + [north_ref[2]]
    faces = [0.5 * (ks[i] + ks[i + 1]) for i in range(YC + 1)]
    back_ground, edge, ground = reduce_coefficients(
        YC, lambda i: g_ref[y_rows(i), :], lambda i: faces[i + 1], faces[0], co_y_ref
    )
    at_end = lax.axis_index("gy") == groups_y - 1
    link_ref[...] = edge
    low_ref[...] = back_ground + edge
    high_ref[...] = ground + edge + jnp.where(at_end, faces[YC], 0.0)
    x_coefficients(next_c_ref, m_ref, x_ref)
    entry_ref[...] = z_coefficients(
        groups_z, c_ref, m_ref, below_ref[1], above_ref[1], co1_ref, num_ref, 0
    )
    z_coefficients(
        groups_z, next_c_ref, m_ref, below_ref[2], above_ref[2], co2_ref, num_ref, 3 * YC
    )


def flow_rhs(t_ref, c_ref, m_ref, x_ref, zt, yt, zk, yk, outs, scratch):
    fluxz_ref, cure_ref = outs
    k_ref, g_ref, fy_ref, r_ref = scratch
    t, c, m = t_ref[...], c_ref[...], m_ref[...]
    k_ref[...] = conduct_of(m, c)
    g_ref[...] = store_of(m)
    cure_ref[...] = cure_of(m, t, c)

    ks = [yk[0]] + [k_ref[y_rows(y), :] for y in range(YC)] + [yk[1]]
    ts = [yt[0]] + [t_ref[y_rows(y), :] for y in range(YC)] + [yt[1]]
    face_y = [0.5 * (ks[i] + ks[i + 1]) for i in range(YC + 1)]
    flow_y = [face_y[i] * (ts[i + 1] - ts[i]) for i in range(YC + 1)]
    for y in range(YC):
        fy_ref[y_rows(y), :] = flow_y[y + 1] - flow_y[y]

    first_lane, last_lane = edge_lanes()
    k_prev, t_prev = zk[0], zt[0]
    flow_prev = 0.5 * (k_prev + k_ref[z_rows(0), :]) * (t_ref[z_rows(0), :] - t_prev)
    batch = 4
    for z0 in range(0, ZC, batch):
        sides = []
        for z in range(z0, z0 + batch):
            rows = z_rows(z)
            kz, tz = k_ref[rows, :], t_ref[rows, :]
            k_next = k_ref[z_rows(z + 1), :] if z + 1 < ZC else zk[1]
            t_next = t_ref[z_rows(z + 1), :] if z + 1 < ZC else zt[1]
            flow_next = 0.5 * (kz + k_next) * (t_next - tz)
            flux_z = flow_next - flow_prev
            flow_prev = flow_next
            fluxz_ref[rows, :] = flux_z
            t_left = jnp.where(first_lane, 0.0, pltpu.roll(tz, 1, 1))
            flow_left = x_ref[2 * ROUNDS + 1, rows, :] * (tz - t_left)
            flow_right = jnp.where(last_lane, -0.5 * kz * tz, pltpu.roll(flow_left, XC - 1, 1))
            delta = cure_ref[rows, :] - c_ref[rows, :]
            sides.append(
                g_ref[rows, :] * (tz + 0.4 * delta)
                + (flow_right - flow_left)
                + 2.0 * (fy_ref[rows, :] + flux_z)
            )
        for level in range(ROUNDS):
            low, high = 1 << level, XC - (1 << level)
            for b in range(batch):
                rows = z_rows(z0 + b)
                side = sides[b]
                sides[b] = (
                    side
                    + pltpu.roll(x_ref[2 * level, rows, :] * side, low, 1)
                    + pltpu.roll(x_ref[2 * level + 1, rows, :] * side, high, 1)
                )
        for b in range(batch):
            rows = z_rows(z0 + b)
            r_ref[rows, :] = x_ref[2 * ROUNDS, rows, :] * sides[b] - fy_ref[rows, :]
    return face_y


def front_kernel(
    t_ref,
    c_ref,
    m_ref,
    x_ref,
    below_ref,
    above_ref,
    south_ref,
    north_ref,
    pay_ref,
    co1_ref,
    side_ref,
    fluxz_ref,
    cure_ref,
    entry_ref,
    k_ref,
    g_ref,
    fy_ref,
    r_ref,
    p_ref,
    sem,
    *,
    groups,
):
    face_y = flow_rhs(
        t_ref,
        c_ref,
        m_ref,
        x_ref,
        (below_ref[0], above_ref[0]),
        (south_ref[0], north_ref[0]),
        (below_ref[1], above_ref[1]),
        (south_ref[1], north_ref[1]),
        (fluxz_ref, cure_ref),
        (k_ref, g_ref, fy_ref, r_ref),
    )
    entry_ref[...] = face_y[YC]
    at_end = lax.axis_index("gy") == groups - 1
    back_ground, edge, ground = reduce_coefficients(
        YC, lambda i: g_ref[y_rows(i), :], lambda i: face_y[i + 1], face_y[0], co1_ref
    )
    ground = ground + jnp.where(at_end, face_y[YC], 0.0)
    side, back_side = reduce_sides(YC, lambda i: r_ref[y_rows(i), :], co1_ref, side_ref)
    for y, row in ((0, 5 * ZC), (YC - 1, 5 * ZC + 4)):
        for i, corner in enumerate((below_ref[0], above_ref[0], below_ref[1], above_ref[1])):
            p_ref[row + i : row + i + 1] = corner[y : y + 1]
    numbers = (back_ground, edge, ground, side, back_side)
    for q, number in enumerate(numbers):
        p_ref[ZC * q : ZC * q + ZC] = number
    spread(p_ref, pay_ref, sem, groups)


def chain(count, read, put):
    def ground_of(j):
        return read(j, 2) + read(j + 1, 0) if j + 1 < count else read(j, 2)

    def side_of(j):
        return read(j, 3) + read(j + 1, 4) if j + 1 < count else read(j, 3)

    half = count // 2
    gain, part = [None] * count, [None] * count
    ground_l, side_l = ground_of(0) + read(0, 1), side_of(0)
    ground_r, side_r = ground_of(count - 1), side_of(count - 1)
    for i in range(half - 1):
        edge = read(i + 1, 1)
        inv = 1.0 / (ground_l + edge)
        gain[i], part[i] = edge * inv, side_l * inv
        ground_l = ground_of(i + 1) + gain[i] * ground_l
        side_l = side_of(i + 1) + gain[i] * side_l
        j = count - 1 - i
        edge = read(j, 1)
        inv = 1.0 / (ground_r + edge)
        gain[j], part[j] = edge * inv, side_r * inv
        ground_r = ground_of(j - 1) + gain[j] * ground_r
        side_r = side_of(j - 1) + gain[j] * side_r
    edge = read(half, 1)
    inv = 1.0 / (ground_l * ground_r + edge * (ground_l + ground_r))
    low = (side_l * (ground_r + edge) + edge * side_r) * inv
    high = (side_r * (ground_l + edge) + edge * side_l) * inv
    put(half - 1, low)
    put(half, high)
    for i in range(half - 2, -1, -1):
        low = part[i] + gain[i] * low
        put(i, low)
        j = count - 1 - i
        high = part[j] + gain[j] * high
        put(j, high)


def first_of_next(own, after, back_ground, edge, back_side, entry):
    return own - (back_ground * own + edge * (own - after) - back_side) / entry


def substitute_y(before, own, co_ref, side_ref, v_ref):
    def place(i, value):
        v_ref[y_rows(i), :] = value

    substitute(YC, before, own, co_ref, side_ref, place)


def block_rows(q):
    return pl.ds(YC * q, YC)


def wide_rows(q):
    return pl.ds(2 * YC + 2 * q, 2)


def middle_kernel(
    all_ref,
    co_y_ref,
    side_y_ref,
    fluxz_ref,
    m_ref,
    co_z_ref,
    y_entry_ref,
    south_ref,
    north_ref,
    p_ref,
    side_z_ref,
    co_wide_ref,
    side_wide_ref,
    s_ref,
    v_ref,
    h_ref,
    *,
    groups_y,
    groups_z,
):
    def read(j, q):
        return all_ref[j, ZC * q : ZC * q + ZC, :]

    s_ref[0] = jnp.zeros((ZC, XC), jnp.float32)

    def put(j, value):
        s_ref[j + 1] = value

    chain(groups_y, read, put)
    me = lax.axis_index("gy")
    before, own = s_ref[me], s_ref[me + 1]
    substitute_y(before, own, co_y_ref, side_y_ref, v_ref)

    def right(i):
        return store_of(m_ref[z_rows(i), :]) * v_ref[z_rows(i), :] - fluxz_ref[z_rows(i), :]

    sides = reduce_sides(ZC, right, co_z_ref, side_z_ref)
    p_ref[24:32, :] = jnp.zeros((8, XC), jnp.float32)
    p_ref[block_rows(0), :] = sides[0]
    p_ref[block_rows(1), :] = sides[1]

    then = jnp.minimum(me + 1, groups_y - 1)
    north = first_of_next(
        own,
        s_ref[then + 1],
        all_ref[then, 0:16, :],
        all_ref[then, 16:32, :],
        all_ref[then, 64:80, :],
        y_entry_ref[...],
    )
    last = jnp.maximum(me - 1, 0)
    beside = (
        (0, before, south_ref, all_ref[last, 5 * ZC + 4 : 5 * ZC + 8, :]),
        (1, north, north_ref, all_ref[then, 5 * ZC : 5 * ZC + 4, :]),
    )
    for side, value, halo_ref, corners in beside:
        rows = pl.ds(2 + side, ZC, stride=2)
        for q in range(2):
            h_ref[q, rows, :] = halo_ref[q]
            h_ref[q, side : side + 1, :] = corners[2 * q : 2 * q + 1]
            h_ref[q, 34 + side : 35 + side, :] = corners[2 * q + 1 : 2 * q + 2]
        h_ref[2, rows, :] = value
    faces = 0.5 * (h_ref[1, 0:34, :] + h_ref[1, 2:36, :])
    h_ref[3, 0:34, :] = faces
    h_ref[4, 0:34, :] = faces * (h_ref[0, 2:36, :] - h_ref[0, 0:34, :])
    capacity = store_by(h_ref[1, 2:34, :])
    h_ref[5, 0:32, :] = capacity
    h_ref[6, 0:32, :] = capacity * h_ref[2, 2:34, :] - (h_ref[4, 2:34, :] - h_ref[4, 0:32, :])
    numbers = reduce_coefficients(
        ZC,
        lambda i: h_ref[5, 2 * i : 2 * i + 2, :],
        lambda i: h_ref[3, 2 * i + 2 : 2 * i + 4, :],
        h_ref[3, 0:2, :],
        co_wide_ref,
    )
    sides = reduce_sides(
        ZC, lambda i: h_ref[6, 2 * i : 2 * i + 2, :], co_wide_ref, side_wide_ref
    )
    at_end = lax.axis_index("gz") == groups_z - 1
    p_ref[wide_rows(0), :] = numbers[0]
    p_ref[wide_rows(1), :] = numbers[1]
    p_ref[wide_rows(2), :] = numbers[2] + jnp.where(at_end, h_ref[3, 32:34, :], 0.0)
    p_ref[wide_rows(3), :] = sides[0]
    p_ref[wide_rows(4), :] = sides[1]


def later_middle_kernel(
    all_ref,
    scale_ref,
    co_y_ref,
    side_y_ref,
    fluxz_ref,
    m_ref,
    co_z_ref,
    p_ref,
    side_z_ref,
    s_ref,
    v_ref,
    *,
    groups_y,
):
    s_ref[0] = jnp.zeros((ZC, XC), jnp.float32)

    def side_of(j):
        side = all_ref[j, ZC : 2 * ZC, :]
        return side + all_ref[j + 1, 2 * ZC : 3 * ZC, :] if j + 1 < groups_y else side

    def put(j, value):
        s_ref[j + 1] = value

    unit_chain(groups_y, lambda j: all_ref[j, 0:ZC, :], side_of, put)
    me = lax.axis_index("gy")
    before, own = s_ref[me] * scale_ref[1], s_ref[me + 1] * scale_ref[0]
    substitute_y(before, own, co_y_ref, side_y_ref, v_ref)

    def right(i):
        return store_of(m_ref[z_rows(i), :]) * v_ref[z_rows(i), :] - fluxz_ref[z_rows(i), :]

    sides = reduce_sides(ZC, right, co_z_ref, side_z_ref)
    p_ref[0:YC] = sides[0]
    p_ref[YC : 2 * YC] = sides[1]


HALF = YC // 2


def node_between(low, high):
    ground = low[2] + high[0]
    return ground, 1.0 / (ground + low[1] + high[1])


def merged_coefficients(low, high):
    ground, inv = node_between(low, high)
    low_inv, high_inv = low[1] * inv, high[1] * inv
    return low[0] + low_inv * ground, low_inv * high[1], high[2] + high_inv * ground


def merged_sides(low, high):
    _, inv = node_between(low, high)
    side = low[3] + high[4]
    return high[3] + high[1] * inv * side, low[4] + low[1] * inv * side


def block_numbers(coef_ref, side_ref, step):
    return [
        [coef_ref[core, block_rows(3 * step + q), :] for q in range(3)]
        + [side_ref[core, block_rows(q), :] for q in range(2)]
        for core in range(2)
    ]


def wide_numbers(side_ref):
    return [[side_ref[core, wide_rows(q), :] for q in range(5)] for core in range(2)]


def my_half(number):
    half = number.shape[0] // 2
    core = lax.rem(lax.axis_index("gz"), 2)
    return jnp.where(core == 0, number[:half], number[half:])


def halves(q):
    return pl.ds(HALF * q, HALF)


def links_kernel(coef_ref, link_ref, low_ref, high_ref):
    for step in range(2):
        low, high = (
            [coef_ref[core, block_rows(3 * step + q), :] for q in range(3)] for core in range(2)
        )
        back_ground, edge, ground = merged_coefficients(low, high)
        link_ref[halves(step), :] = my_half(edge)
        low_ref[halves(step), :] = my_half(back_ground + edge)
        high_ref[halves(step), :] = my_half(ground + edge)


def merge_kernel(
    coef_ref,
    pair_ref,
    link_ref,
    low_ref,
    high_ref,
    from_low_ref,
    from_high_ref,
    pay_ref,
    scale_ref,
    p_ref,
    sem,
    *,
    copies,
):
    p_ref[16:24] = jnp.zeros((8, XC), jnp.float32)
    for step in range(2):
        rows = halves(step)
        own = high_ref[rows, :] + from_high_ref[rows, :]
        root = jnp.sqrt(own)
        own_inv = 1.0 / root
        last_inv = 1.0 / jnp.sqrt(from_low_ref[rows, :] + low_ref[rows, :])
        scale_ref[halves(2 * step), :] = own_inv
        scale_ref[halves(2 * step + 1), :] = last_inv
        p_ref[halves(3 * step), :] = link_ref[rows, :] * (own_inv * last_inv)
        if step == 0:
            scale_ref[halves(4), :] = root
            scale_ref[halves(5), :] = from_high_ref[rows, :]
    low, high = block_numbers(coef_ref, pair_ref, 0)
    side, back_side = merged_sides(low, high)
    p_ref[halves(1), :] = my_half(side) * scale_ref[halves(0), :]
    p_ref[halves(2), :] = my_half(back_side) * scale_ref[halves(1), :]
    low, high = wide_numbers(pair_ref)
    for q, number in enumerate(merged_coefficients(low, high) + merged_sides(low, high)):
        p_ref[16 + q : 17 + q] = my_half(number)
    spread(p_ref, pay_ref, sem, copies)


def later_merge_kernel(coef_ref, more_ref, scale_ref, pay_ref, p_ref, sem, *, copies):
    side, back_side = merged_sides(*block_numbers(coef_ref, more_ref, 1))
    p_ref[halves(0), :] = my_half(side) * scale_ref[halves(2), :]
    p_ref[halves(1), :] = my_half(back_side) * scale_ref[halves(3), :]
    spread(p_ref, pay_ref, sem, copies)


def unit_chain(count, link, side_of, put):
    half = count // 2
    gain, part = [None] * count, [None] * count
    diag_l = diag_r = None
    side_l, side_r = side_of(0), side_of(count - 1)
    for i in range(half - 1):
        j = count - 1 - i
        edge_l, edge_r = link(i + 1), link(j)
        if i == 0:
            gain[i], part[i], gain[j], part[j] = edge_l, side_l, edge_r, side_r
        else:
            inv_l, inv_r = 1.0 / diag_l, 1.0 / diag_r
            gain[i], part[i] = edge_l * inv_l, side_l * inv_l
            gain[j], part[j] = edge_r * inv_r, side_r * inv_r
        diag_l = 1.0 - edge_l * gain[i]
        side_l = side_of(i + 1) + edge_l * part[i]
        diag_r = 1.0 - edge_r * gain[j]
        side_r = side_of(j - 1) + edge_r * part[j]
    edge = link(half)
    if half == 1:
        diag_l = diag_r = jnp.ones_like(edge)
    inv = 1.0 / (diag_l * diag_r - edge * edge)
    low = (side_l * diag_r + edge * side_r) * inv
    high = (side_r * diag_l + edge * side_l) * inv
    put(half - 1, low)
    put(half, high)
    for i in range(half - 2, -1, -1):
        low = part[i] + gain[i] * low
        put(i, low)
        j = count - 1 - i
        high = part[j] + gain[j] * high
        put(j, high)


def chain_kernel(all_ref, scale_ref, out_ref, s_ref, w_ref, *, chips):
    s_ref[0] = jnp.zeros((HALF, XC), jnp.float32)
    w_ref[0] = jnp.zeros((1, XC), jnp.float32)

    def side_of(j):
        side = all_ref[j, halves(1), :]
        return side + all_ref[j + 1, halves(2), :] if j + 1 < chips else side

    def put(j, value):
        s_ref[j + 1] = value

    def put_wide(j, value):
        w_ref[j + 1] = value

    unit_chain(chips, lambda j: all_ref[j, halves(0), :], side_of, put)
    chain(chips, lambda j, q: all_ref[j, 16 + q : 17 + q, :], put_wide)
    me = lax.div(lax.axis_index("gz"), 2)
    then = jnp.minimum(me + 1, chips - 1)
    own = s_ref[me + 1] * scale_ref[halves(0), :]
    inflow = all_ref[then, halves(0), :] * s_ref[then + 1] + all_ref[then, halves(2), :]
    out_ref[8:16] = jnp.zeros((8, XC), jnp.float32)
    out_ref[halves(0), :] = s_ref[me] * scale_ref[halves(1), :]
    out_ref[halves(1), :] = own
    out_ref[halves(2), :] = scale_ref[halves(5), :] * own - scale_ref[halves(4), :] * inflow
    out_ref[12:13] = w_ref[me]
    out_ref[13:14] = w_ref[me + 1]


def later_chain_kernel(all_ref, more_ref, scale_ref, out_ref, s_ref, *, chips):
    s_ref[0] = jnp.zeros((HALF, XC), jnp.float32)

    def side_of(j):
        side = more_ref[j, halves(0), :]
        return side + more_ref[j + 1, halves(1), :] if j + 1 < chips else side

    def put(j, value):
        s_ref[j + 1] = value

    unit_chain(chips, lambda j: all_ref[j, halves(3), :], side_of, put)
    me = lax.div(lax.axis_index("gz"), 2)
    out_ref[halves(0), :] = s_ref[me] * scale_ref[halves(3), :]
    out_ref[halves(1), :] = s_ref[me + 1] * scale_ref[halves(2), :]


def ends_of(low, high, before, last):
    _, inv = node_between(low, high)
    node = (low[3] + high[4] + low[1] * before + high[1] * last) * inv
    upper = lax.rem(lax.axis_index("gz"), 2) == 1
    return jnp.where(upper, node, before), jnp.where(upper, last, node), node


def joined(res_ref, u_ref, count):
    for q in range(count):
        for core in range(2):
            u_ref[q, halves(core), :] = res_ref[core, halves(q), :]


def back_kernel(coef_ref, more_ref, res_ref, co_z_ref, side_z_ref, t_ref, u_ref):
    joined(res_ref, u_ref, 2)
    low, high = block_numbers(coef_ref, more_ref, 1)
    before, own, _ = ends_of(low, high, u_ref[0], u_ref[1])

    def place(i, value):
        t_ref[z_rows(i), :] = value

    substitute(ZC, before, own, co_z_ref, side_z_ref, place)


def turn_kernel(
    coef_ref,
    pair_ref,
    res_ref,
    co_z_ref,
    side_z_ref,
    co_wide_ref,
    side_wide_ref,
    z_entry_ref,
    c_ref,
    m_ref,
    x_ref,
    co_y_ref,
    link_ref,
    low_ref,
    high_ref,
    from_low_ref,
    from_high_ref,
    below_ref,
    above_ref,
    south_ref,
    north_ref,
    pay_ref,
    side_y_ref,
    fluxz_ref,
    cure_ref,
    scale_ref,
    u_ref,
    w_ref,
    t_ref,
    e_ref,
    k_ref,
    g_ref,
    fy_ref,
    r_ref,
    p_ref,
    sem,
    *,
    groups_y,
    groups_z,
):
    joined(res_ref, u_ref, 3)
    low, high = block_numbers(coef_ref, pair_ref, 0)
    last = u_ref[1]
    before, own, node = ends_of(low, high, u_ref[0], last)

    def place(i, value):
        t_ref[z_rows(i), :] = value

    substitute(ZC, before, own, co_z_ref, side_z_ref, place)
    me = lax.axis_index("gz")
    inside = high[0] * node + high[1] * (node - last) - high[4]
    current = jnp.where(lax.rem(me, 2) == 1, u_ref[2], inside)
    above = jnp.where(me == groups_z - 1, 0.0, own - current / z_entry_ref[...])

    for q in range(2):
        for core in range(2):
            w_ref[q, core : core + 1] = res_ref[core, 12 + q : 13 + q, :]
    low, high = wide_numbers(pair_ref)
    before_wide, own_wide, _ = ends_of(low, high, w_ref[0], w_ref[1])

    def place_wide(i, value):
        e_ref[2 * i : 2 * i + 2] = value

    substitute(ZC, before_wide, own_wide, co_wide_ref, side_wide_ref, place_wide)
    row = lax.axis_index("gy")
    south = jnp.where(row == 0, 0.0, e_ref[pl.ds(0, ZC, stride=2), :])
    north = jnp.where(row == groups_y - 1, 0.0, e_ref[pl.ds(1, ZC, stride=2), :])
    flow_rhs(
        t_ref,
        c_ref,
        m_ref,
        x_ref,
        (before, above),
        (south, north),
        (below_ref[2], above_ref[2]),
        (south_ref[2], north_ref[2]),
        (fluxz_ref, cure_ref),
        (k_ref, g_ref, fy_ref, r_ref),
    )
    side, back_side = reduce_sides(YC, lambda i: r_ref[y_rows(i), :], co_y_ref, side_y_ref)
    own_inv = 1.0 / jnp.sqrt(high_ref[...] + from_high_ref[...])
    last_inv = 1.0 / jnp.sqrt(from_low_ref[...] + low_ref[...])
    scale_ref[0] = own_inv
    scale_ref[1] = last_inv
    p_ref[0:ZC] = link_ref[...] * (own_inv * last_inv)
    p_ref[ZC : 2 * ZC] = side * own_inv
    p_ref[2 * ZC : 3 * ZC] = back_side * last_inv
    spread(p_ref, pay_ref, sem, groups_y)


def call(kernel, outs, scratch=(), spread_to=0, **static):
    out_specs = [pl.BlockSpec(memory_space=pltpu.VMEM)] * len(outs)
    shapes = [pltpu.VMEM(shape, jnp.float32) for shape in scratch]
    if spread_to:
        out_specs[0] = pl.BlockSpec(memory_space=pl.ANY)
        shapes.append(pltpu.SemaphoreType.DMA((spread_to,)))
    return pl.pallas_call(
        functools.partial(kernel, **static),
        out_shape=tuple(outs),
        out_specs=tuple(out_specs),
        scratch_shapes=shapes,
        compiler_params=pltpu.CompilerParams(vmem_limit_bytes=12 * 1024 * 1024),
        name=kernel.__name__,
    )


def body(warmth, cure, label):
    groups_z, groups_y = lax.axis_size("gz"), lax.axis_size("gy")
    chips = groups_z // 2
    up = {a: [(i, i + 1) for i in range(n - 1)] for a, n in (("gz", groups_z), ("gy", groups_y))}
    down = {a: [(j, i) for i, j in up[a]] for a in up}
    pairs = [[2 * i, 2 * i + 1] for i in range(chips)]
    same_core = [[2 * i + core for i in range(chips)] for core in range(2)]
    cells = (ROWS, XC)
    block = f32(*cells)

    zlo, zhi, ylo, yhi, t, c, m = pl.pallas_call(
        edges_kernel,
        out_shape=(
            f32(3, YC, XC),
            f32(3, YC, XC),
            f32(3, ZC, XC),
            f32(3, ZC, XC),
            block,
            block,
            jax.ShapeDtypeStruct(cells, jnp.int32),
        ),
        in_specs=[pl.BlockSpec(memory_space=pltpu.HBM)] * 3,
        scratch_shapes=[pltpu.SemaphoreType.DMA((3,))],
        compiler_params=pltpu.CompilerParams(vmem_limit_bytes=12 * 1024 * 1024),
        name="edges_kernel",
    )(*(pltpu.with_memory_space_constraint(a.reshape(cells), pltpu.HBM) for a in (warmth, cure, label)))
    z_halo = (lax.ppermute(zhi, "gz", up["gz"]), lax.ppermute(zlo, "gz", down["gz"]))
    y_halo = (lax.ppermute(yhi, "gy", up["gy"]), lax.ppermute(ylo, "gy", down["gy"]))

    def gather_y(pay):
        return lax.all_to_all(pay, "gy", 0, 0, tiled=True)

    def gather_z(pay):
        return lax.all_to_all(pay, "gz", 0, 0, tiled=True, axis_index_groups=same_core)

    def share(numbers):
        return lax.all_gather(numbers, "gz", axis_index_groups=pairs)

    sizes = dict(groups_y=groups_y, groups_z=groups_z)
    co_y, side_y = f32(3, YC - 1, ZC, XC), f32(YC - 1, ZC, XC)
    co_z, side_z = f32(3, ZC - 1, YC, XC), f32(ZC - 1, YC, XC)
    next_chip = [(i, i + 2) for i in range(groups_z - 2)]
    last_chip = [(j, i) for i, j in next_chip]
    x_shape = f32(2 * ROUNDS + 2, ROWS, XC)
    line = (groups_y + 1, ZC, XC)

    (x1,) = call(x_kernel, [x_shape])(c, m)
    pay, co_y1, side, fluxz, c1, y_entry = call(
        front_kernel,
        [f32(groups_y, 5 * ZC + 8, XC), co_y, side_y, block, block, f32(ZC, XC)],
        [cells] * 4 + [(5 * ZC + 8, XC)],
        spread_to=groups_y,
        groups=groups_y,
    )(t, c, m, x1, *z_halo, *y_halo)
    y_row = f32(ZC, XC)
    x2, co_z1, co_z2, numbers, z_entry, co_y2, link_y, low_y, high_y = call(
        ahead_kernel,
        [x_shape, co_z, co_z, f32(6 * YC, XC), f32(YC, XC), co_y, y_row, y_row, y_row],
        [cells] * 2,
        **sizes,
    )(c, c1, m, *z_halo, *y_halo)
    coef = share(numbers)
    link, low, high = call(links_kernel, [f32(YC, XC)] * 3)(coef)
    from_low = lax.ppermute(high, "gz", next_chip)
    from_high = lax.ppermute(low, "gz", last_chip)
    everyone = gather_y(pay)
    numbers, side, co_wide, side_wide = call(
        middle_kernel,
        [f32(4 * YC, XC), side_z, f32(3, ZC - 1, 2, XC), f32(ZC - 1, 2, XC)],
        [line, cells, (7, 40, XC)],
        **sizes,
    )(everyone, co_y1, side, fluxz, m, co_z1, y_entry, *y_halo)
    pair = share(numbers)
    pay, scale = call(
        merge_kernel,
        [f32(chips, 24, XC), f32(24, XC)],
        [(24, XC)],
        spread_to=chips,
        copies=chips,
    )(coef, pair, link, low, high, from_low, from_high)
    pay, send_low, send_high = lax.optimization_barrier((pay, low_y, high_y))
    column = gather_z(pay)
    from_south = lax.ppermute(send_high, "gy", up["gy"])
    from_north = lax.ppermute(send_low, "gy", down["gy"])
    half_line = (chips + 1, HALF, XC)
    (found,) = call(
        chain_kernel, [f32(16, XC)], [half_line, (chips + 1, 1, XC)], chips=chips
    )(column, scale)
    pay, side, fluxz, c2, scale_y = call(
        turn_kernel,
        [f32(groups_y, 3 * ZC, XC), side_y, block, block, f32(2, ZC, XC)],
        [(3, YC, XC), (2, 2, XC), cells, (2 * ZC, XC)] + [cells] * 4 + [(3 * ZC, XC)],
        spread_to=groups_y,
        **sizes,
    )(
        coef,
        pair,
        share(found),
        co_z1,
        side,
        co_wide,
        side_wide,
        z_entry,
        c1,
        m,
        x2,
        co_y2,
        link_y,
        low_y,
        high_y,
        from_south,
        from_north,
        *z_halo,
        *y_halo,
    )
    numbers, side = call(
        later_middle_kernel, [f32(2 * YC, XC), side_z], [line, cells], groups_y=groups_y
    )(gather_y(pay), scale_y, co_y2, side, fluxz, m, co_z2)
    more = share(numbers)
    (pay,) = call(
        later_merge_kernel, [f32(chips, YC, XC)], [(YC, XC)], spread_to=chips, copies=chips
    )(coef, more, scale)
    (found,) = call(later_chain_kernel, [f32(YC, XC)], [half_line], chips=chips)(
        column, gather_z(pay), scale
    )
    (t2,) = call(back_kernel, [block], [(2, YC, XC)])(coef, more, share(found), co_z2, side)
    return t2.reshape(warmth.shape), c2.reshape(cure.shape)


def solution(mesh):
    return jax.shard_map(
        body,
        mesh=mesh,
        in_specs=(P("gz", "gy", None),) * 3,
        out_specs=(P("gz", "gy", None),) * 2,
        check_vma=False,
    )
```

```python
import functools

import jax
import jax.numpy as jnp
from jax import lax
from jax.experimental import pallas as pl
from jax.experimental.pallas import tpu as pltpu
from jax.sharding import PartitionSpec as P

ZC = 16
YC = 8
XC = 128
ROWS = ZC * YC


def f32(*shape):
    return jax.ShapeDtypeStruct(shape, jnp.float32)


def conduct_of(label, cure):
    return jnp.where(label == 1, 40.0, jnp.where(label == 2, 20.0, 0.6 + 0.8 * cure))


def store_of(label):
    return jnp.where(label == 1, 3.0 / 60.0, jnp.where(label == 2, 2.0 / 60.0, 1.0 / 60.0))


def store_by(k):
    return jnp.where(k > 30.0, 3.0 / 60.0, jnp.where(k > 10.0, 2.0 / 60.0, 1.0 / 60.0))


def cure_of(label, warmth, cure):
    speed = 0.3 * jnp.exp(8.0 * warmth)
    return jnp.where(label == 0, 1.0 - (1.0 - cure) * jnp.exp(-speed), cure)


def y_rows(y):
    return pl.ds(y, ZC, stride=YC)


def z_rows(z):
    return pl.ds(z * YC, YC)


def edges_kernel(
    t_in, c_in, m_in, zlo_ref, zhi_ref, ylo_ref, yhi_ref, t_ref, c_ref, m_ref, sem
):
    copies = [
        pltpu.make_async_copy(src, dst, sem.at[i])
        for i, (src, dst) in enumerate(((t_in, t_ref), (c_in, c_ref), (m_in, m_ref)))
    ]
    for copy in copies:
        copy.start()
    for copy in copies:
        copy.wait()

    def put(out, rows):
        t, c, m = t_ref[rows, :], c_ref[rows, :], m_ref[rows, :]
        out[0] = t
        out[1] = conduct_of(m, c)
        out[2] = conduct_of(m, cure_of(m, t, c))

    put(zlo_ref, z_rows(0))
    put(zhi_ref, z_rows(ZC - 1))
    put(ylo_ref, y_rows(0))
    put(yhi_ref, y_rows(YC - 1))


def spread(one_ref, out_ref, sem, count):
    copies = [pltpu.make_async_copy(one_ref, out_ref.at[d], sem.at[d]) for d in range(count)]
    for d, copy in enumerate(copies):
        copy.start(priority=d % 2)
    for copy in copies:
        copy.wait()


def reduce_coefficients(count, store, faces, entry, co_ref):
    ground, edge = store(0), entry
    back_ground = None
    for i in range(count - 1):
        face = faces(i)
        inv = 1.0 / (ground + edge + face)
        edge_inv, face_inv = edge * inv, face * inv
        co_ref[0, i] = inv
        co_ref[1, i] = edge_inv
        co_ref[2, i] = face_inv
        more = edge_inv * ground
        back_ground = more if i == 0 else back_ground + more
        ground = store(i + 1) + face_inv * ground
        edge = edge_inv * face
    return back_ground, edge, ground


def reduce_sides(count, right, co_ref, side_ref):
    side = right(0)
    back_side = None
    for i in range(count - 1):
        side_ref[i] = side * co_ref[0, i]
        more = co_ref[1, i] * side
        back_side = more if i == 0 else back_side + more
        side = right(i + 1) + co_ref[2, i] * side
    return side, back_side


def substitute(count, before, own, co_ref, side_ref, put):
    value = own
    put(count - 1, value)
    for i in range(count - 2, -1, -1):
        value = (side_ref[i] + co_ref[1, i] * before) + co_ref[2, i] * value
        put(i, value)


def edge_lanes():
    lane = lax.broadcasted_iota(jnp.int32, (YC, XC), 1)
    return lane == 0, lane == XC - 1


ROUNDS = 7


def x_coefficients(c_ref, m_ref, x_ref):
    first_lane, last_lane = edge_lanes()
    batch = 4
    for z0 in range(0, ZC, batch):
        gs, ls, rs, stores = [], [], [], []
        for z in range(z0, z0 + batch):
            rows = z_rows(z)
            m = m_ref[rows, :]
            k, g = conduct_of(m, c_ref[rows, :]), store_of(m)
            face_left = 0.5 * (k + jnp.where(first_lane, 0.0, pltpu.roll(k, 1, 1)))
            face_right = jnp.where(last_lane, 0.5 * k, pltpu.roll(face_left, XC - 1, 1))
            x_ref[2 * ROUNDS + 1, rows, :] = face_left
            gs.append(
                g
                + jnp.where(first_lane, face_left, 0.0)
                + jnp.where(last_lane, face_right, 0.0)
            )
            ls.append(jnp.where(first_lane, 0.0, face_left))
            rs.append(jnp.where(last_lane, 0.0, face_right))
            stores.append(g)
        for level in range(ROUNDS):
            low, high = 1 << level, XC - (1 << level)
            for b in range(batch):
                rows = z_rows(z0 + b)
                ground, left, right = gs[b], ls[b], rs[b]
                inv = 1.0 / (ground + left + right)
                up, down = right * inv, left * inv
                x_ref[2 * level, rows, :] = up
                x_ref[2 * level + 1, rows, :] = down
                gs[b] = (
                    ground + pltpu.roll(up * ground, low, 1) + pltpu.roll(down * ground, high, 1)
                )
                if level + 1 < ROUNDS:
                    link = up * left
                    ls[b] = pltpu.roll(link, low, 1)
                    rs[b] = pltpu.roll(link, high, 1)
        for b in range(batch):
            x_ref[2 * ROUNDS, z_rows(z0 + b), :] = stores[b] / gs[b]


def x_kernel(c_ref, m_ref, x_ref):
    x_coefficients(c_ref, m_ref, x_ref)


def z_coefficients(groups_z, c_ref, m_ref, below, above, co_ref, num_ref, row):
    ks = [below]
    for z in range(ZC):
        ks.append(conduct_of(m_ref[z_rows(z), :], c_ref[z_rows(z), :]))
    ks.append(above)
    faces = [0.5 * (ks[i] + ks[i + 1]) for i in range(ZC + 1)]
    numbers = reduce_coefficients(
        ZC,
        lambda i: store_of(m_ref[z_rows(i), :]),
        lambda i: faces[i + 1],
        faces[0],
        co_ref,
    )
    at_end = lax.axis_index("gz") == groups_z - 1
    num_ref[row : row + YC] = numbers[0]
    num_ref[row + YC : row + 2 * YC] = numbers[1]
    num_ref[row + 2 * YC : row + 3 * YC] = numbers[2] + jnp.where(at_end, faces[ZC], 0.0)
    return faces[ZC]


def ahead_kernel(
    c_ref,
    next_c_ref,
    m_ref,
    below_ref,
    above_ref,
    south_ref,
    north_ref,
    x_ref,
    co1_ref,
    co2_ref,
    num_ref,
    entry_ref,
    co_y_ref,
    link_ref,
    low_ref,
    high_ref,
    k_ref,
    g_ref,
    *,
    groups_y,
    groups_z,
):
    m = m_ref[...]
    k_ref[...] = conduct_of(m, next_c_ref[...])
    g_ref[...] = store_of(m)
    ks = [south_ref[2]] + [k_ref[y_rows(y), :] for y in range(YC)] + [north_ref[2]]
    faces = [0.5 * (ks[i] + ks[i + 1]) for i in range(YC + 1)]
    back_ground, edge, ground = reduce_coefficients(
        YC, lambda i: g_ref[y_rows(i), :], lambda i: faces[i + 1], faces[0], co_y_ref
    )
    at_end = lax.axis_index("gy") == groups_y - 1
    link_ref[...] = edge
    low_ref[...] = back_ground + edge
    high_ref[...] = ground + edge + jnp.where(at_end, faces[YC], 0.0)
    x_coefficients(next_c_ref, m_ref, x_ref)
    entry_ref[...] = z_coefficients(
        groups_z, c_ref, m_ref, below_ref[1], above_ref[1], co1_ref, num_ref, 0
    )
    z_coefficients(
        groups_z, next_c_ref, m_ref, below_ref[2], above_ref[2], co2_ref, num_ref, 3 * YC
    )


def flow_rhs(t_ref, c_ref, m_ref, x_ref, zt, yt, zk, yk, outs, scratch):
    fluxz_ref, cure_ref = outs
    k_ref, g_ref, fy_ref, r_ref = scratch
    t, c, m = t_ref[...], c_ref[...], m_ref[...]
    k_ref[...] = conduct_of(m, c)
    g_ref[...] = store_of(m)
    cure_ref[...] = cure_of(m, t, c)

    ks = [yk[0]] + [k_ref[y_rows(y), :] for y in range(YC)] + [yk[1]]
    ts = [yt[0]] + [t_ref[y_rows(y), :] for y in range(YC)] + [yt[1]]
    face_y = [0.5 * (ks[i] + ks[i + 1]) for i in range(YC + 1)]
    flow_y = [face_y[i] * (ts[i + 1] - ts[i]) for i in range(YC + 1)]
    for y in range(YC):
        fy_ref[y_rows(y), :] = flow_y[y + 1] - flow_y[y]

    first_lane, last_lane = edge_lanes()
    k_prev, t_prev = zk[0], zt[0]
    flow_prev = 0.5 * (k_prev + k_ref[z_rows(0), :]) * (t_ref[z_rows(0), :] - t_prev)
    batch = 4
    for z0 in range(0, ZC, batch):
        sides = []
        for z in range(z0, z0 + batch):
            rows = z_rows(z)
            kz, tz = k_ref[rows, :], t_ref[rows, :]
            k_next = k_ref[z_rows(z + 1), :] if z + 1 < ZC else zk[1]
            t_next = t_ref[z_rows(z + 1), :] if z + 1 < ZC else zt[1]
            flow_next = 0.5 * (kz + k_next) * (t_next - tz)
            flux_z = flow_next - flow_prev
            flow_prev = flow_next
            fluxz_ref[rows, :] = flux_z
            t_left = jnp.where(first_lane, 0.0, pltpu.roll(tz, 1, 1))
            flow_left = x_ref[2 * ROUNDS + 1, rows, :] * (tz - t_left)
            flow_right = jnp.where(last_lane, -0.5 * kz * tz, pltpu.roll(flow_left, XC - 1, 1))
            delta = cure_ref[rows, :] - c_ref[rows, :]
            sides.append(
                g_ref[rows, :] * (tz + 0.4 * delta)
                + (flow_right - flow_left)
                + 2.0 * (fy_ref[rows, :] + flux_z)
            )
        for level in range(ROUNDS):
            low, high = 1 << level, XC - (1 << level)
            for b in range(batch):
                rows = z_rows(z0 + b)
                side = sides[b]
                sides[b] = (
                    side
                    + pltpu.roll(x_ref[2 * level, rows, :] * side, low, 1)
                    + pltpu.roll(x_ref[2 * level + 1, rows, :] * side, high, 1)
                )
        for b in range(batch):
            rows = z_rows(z0 + b)
            r_ref[rows, :] = x_ref[2 * ROUNDS, rows, :] * sides[b] - fy_ref[rows, :]
    return face_y


def front_kernel(
    t_ref,
    c_ref,
    m_ref,
    x_ref,
    below_ref,
    above_ref,
    south_ref,
    north_ref,
    pay_ref,
    co1_ref,
    side_ref,
    fluxz_ref,
    cure_ref,
    entry_ref,
    k_ref,
    g_ref,
    fy_ref,
    r_ref,
    p_ref,
    sem,
    *,
    groups,
):
    face_y = flow_rhs(
        t_ref,
        c_ref,
        m_ref,
        x_ref,
        (below_ref[0], above_ref[0]),
        (south_ref[0], north_ref[0]),
        (below_ref[1], above_ref[1]),
        (south_ref[1], north_ref[1]),
        (fluxz_ref, cure_ref),
        (k_ref, g_ref, fy_ref, r_ref),
    )
    entry_ref[...] = face_y[YC]
    at_end = lax.axis_index("gy") == groups - 1
    back_ground, edge, ground = reduce_coefficients(
        YC, lambda i: g_ref[y_rows(i), :], lambda i: face_y[i + 1], face_y[0], co1_ref
    )
    ground = ground + jnp.where(at_end, face_y[YC], 0.0)
    side, back_side = reduce_sides(YC, lambda i: r_ref[y_rows(i), :], co1_ref, side_ref)
    for y, row in ((0, 5 * ZC), (YC - 1, 5 * ZC + 4)):
        for i, corner in enumerate((below_ref[0], above_ref[0], below_ref[1], above_ref[1])):
            p_ref[row + i : row + i + 1] = corner[y : y + 1]
    numbers = (back_ground, edge, ground, side, back_side)
    for q, number in enumerate(numbers):
        p_ref[ZC * q : ZC * q + ZC] = number
    spread(p_ref, pay_ref, sem, groups)


def chain(count, read, put):
    def ground_of(j):
        return read(j, 2) + read(j + 1, 0) if j + 1 < count else read(j, 2)

    def side_of(j):
        return read(j, 3) + read(j + 1, 4) if j + 1 < count else read(j, 3)

    half = count // 2
    gain, part = [None] * count, [None] * count
    ground_l, side_l = ground_of(0) + read(0, 1), side_of(0)
    ground_r, side_r = ground_of(count - 1), side_of(count - 1)
    for i in range(half - 1):
        edge = read(i + 1, 1)
        inv = 1.0 / (ground_l + edge)
        gain[i], part[i] = edge * inv, side_l * inv
        ground_l = ground_of(i + 1) + gain[i] * ground_l
        side_l = side_of(i + 1) + gain[i] * side_l
        j = count - 1 - i
        edge = read(j, 1)
        inv = 1.0 / (ground_r + edge)
        gain[j], part[j] = edge * inv, side_r * inv
        ground_r = ground_of(j - 1) + gain[j] * ground_r
        side_r = side_of(j - 1) + gain[j] * side_r
    edge = read(half, 1)
    inv = 1.0 / (ground_l * ground_r + edge * (ground_l + ground_r))
    low = (side_l * (ground_r + edge) + edge * side_r) * inv
    high = (side_r * (ground_l + edge) + edge * side_l) * inv
    put(half - 1, low)
    put(half, high)
    for i in range(half - 2, -1, -1):
        low = part[i] + gain[i] * low
        put(i, low)
        j = count - 1 - i
        high = part[j] + gain[j] * high
        put(j, high)


def first_of_next(own, after, back_ground, edge, back_side, entry):
    return own - (back_ground * own + edge * (own - after) - back_side) / entry


def substitute_y(before, own, co_ref, side_ref, v_ref):
    def place(i, value):
        v_ref[y_rows(i), :] = value

    substitute(YC, before, own, co_ref, side_ref, place)


def block_rows(q):
    return pl.ds(YC * q, YC)


def wide_rows(q):
    return pl.ds(2 * YC + 2 * q, 2)


def middle_kernel(
    all_ref,
    co_y_ref,
    side_y_ref,
    fluxz_ref,
    m_ref,
    co_z_ref,
    y_entry_ref,
    south_ref,
    north_ref,
    p_ref,
    side_z_ref,
    co_wide_ref,
    side_wide_ref,
    s_ref,
    v_ref,
    h_ref,
    *,
    groups_y,
    groups_z,
):
    def read(j, q):
        return all_ref[j, ZC * q : ZC * q + ZC, :]

    s_ref[0] = jnp.zeros((ZC, XC), jnp.float32)

    def put(j, value):
        s_ref[j + 1] = value

    chain(groups_y, read, put)
    me = lax.axis_index("gy")
    before, own = s_ref[me], s_ref[me + 1]
    substitute_y(before, own, co_y_ref, side_y_ref, v_ref)

    def right(i):
        return store_of(m_ref[z_rows(i), :]) * v_ref[z_rows(i), :] - fluxz_ref[z_rows(i), :]

    sides = reduce_sides(ZC, right, co_z_ref, side_z_ref)
    p_ref[24:32, :] = jnp.zeros((8, XC), jnp.float32)
    p_ref[block_rows(0), :] = sides[0]
    p_ref[block_rows(1), :] = sides[1]

    then = jnp.minimum(me + 1, groups_y - 1)
    north = first_of_next(
        own,
        s_ref[then + 1],
        all_ref[then, 0:16, :],
        all_ref[then, 16:32, :],
        all_ref[then, 64:80, :],
        y_entry_ref[...],
    )
    last = jnp.maximum(me - 1, 0)
    beside = (
        (0, before, south_ref, all_ref[last, 5 * ZC + 4 : 5 * ZC + 8, :]),
        (1, north, north_ref, all_ref[then, 5 * ZC : 5 * ZC + 4, :]),
    )
    for side, value, halo_ref, corners in beside:
        rows = pl.ds(2 + side, ZC, stride=2)
        for q in range(2):
            h_ref[q, rows, :] = halo_ref[q]
            h_ref[q, side : side + 1, :] = corners[2 * q : 2 * q + 1]
            h_ref[q, 34 + side : 35 + side, :] = corners[2 * q + 1 : 2 * q + 2]
        h_ref[2, rows, :] = value
    faces = 0.5 * (h_ref[1, 0:34, :] + h_ref[1, 2:36, :])
    h_ref[3, 0:34, :] = faces
    h_ref[4, 0:34, :] = faces * (h_ref[0, 2:36, :] - h_ref[0, 0:34, :])
    capacity = store_by(h_ref[1, 2:34, :])
    h_ref[5, 0:32, :] = capacity
    h_ref[6, 0:32, :] = capacity * h_ref[2, 2:34, :] - (h_ref[4, 2:34, :] - h_ref[4, 0:32, :])
    numbers = reduce_coefficients(
        ZC,
        lambda i: h_ref[5, 2 * i : 2 * i + 2, :],
        lambda i: h_ref[3, 2 * i + 2 : 2 * i + 4, :],
        h_ref[3, 0:2, :],
        co_wide_ref,
    )
    sides = reduce_sides(
        ZC, lambda i: h_ref[6, 2 * i : 2 * i + 2, :], co_wide_ref, side_wide_ref
    )
    at_end = lax.axis_index("gz") == groups_z - 1
    p_ref[wide_rows(0), :] = numbers[0]
    p_ref[wide_rows(1), :] = numbers[1]
    p_ref[wide_rows(2), :] = numbers[2] + jnp.where(at_end, h_ref[3, 32:34, :], 0.0)
    p_ref[wide_rows(3), :] = sides[0]
    p_ref[wide_rows(4), :] = sides[1]


def later_middle_kernel(
    all_ref,
    scale_ref,
    co_y_ref,
    side_y_ref,
    fluxz_ref,
    m_ref,
    co_z_ref,
    p_ref,
    side_z_ref,
    s_ref,
    v_ref,
    *,
    groups_y,
):
    s_ref[0] = jnp.zeros((ZC, XC), jnp.float32)

    def side_of(j):
        side = all_ref[j, ZC : 2 * ZC, :]
        return side + all_ref[j + 1, 2 * ZC : 3 * ZC, :] if j + 1 < groups_y else side

    def put(j, value):
        s_ref[j + 1] = value

    unit_chain(groups_y, lambda j: all_ref[j, 0:ZC, :], side_of, put)
    me = lax.axis_index("gy")
    before, own = s_ref[me] * scale_ref[1], s_ref[me + 1] * scale_ref[0]
    substitute_y(before, own, co_y_ref, side_y_ref, v_ref)

    def right(i):
        return store_of(m_ref[z_rows(i), :]) * v_ref[z_rows(i), :] - fluxz_ref[z_rows(i), :]

    sides = reduce_sides(ZC, right, co_z_ref, side_z_ref)
    p_ref[0:YC] = sides[0]
    p_ref[YC : 2 * YC] = sides[1]


HALF = YC // 2


def node_between(low, high):
    ground = low[2] + high[0]
    return ground, 1.0 / (ground + low[1] + high[1])


def merged_coefficients(low, high):
    ground, inv = node_between(low, high)
    low_inv, high_inv = low[1] * inv, high[1] * inv
    return low[0] + low_inv * ground, low_inv * high[1], high[2] + high_inv * ground


def merged_sides(low, high):
    _, inv = node_between(low, high)
    side = low[3] + high[4]
    return high[3] + high[1] * inv * side, low[4] + low[1] * inv * side


def block_numbers(coef_ref, side_ref, step):
    return [
        [coef_ref[core, block_rows(3 * step + q), :] for q in range(3)]
        + [side_ref[core, block_rows(q), :] for q in range(2)]
        for core in range(2)
    ]


def wide_numbers(side_ref):
    return [[side_ref[core, wide_rows(q), :] for q in range(5)] for core in range(2)]


def my_half(number):
    half = number.shape[0] // 2
    core = lax.rem(lax.axis_index("gz"), 2)
    return jnp.where(core == 0, number[:half], number[half:])


def halves(q):
    return pl.ds(HALF * q, HALF)


def links_kernel(coef_ref, link_ref, low_ref, high_ref):
    for step in range(2):
        low, high = (
            [coef_ref[core, block_rows(3 * step + q), :] for q in range(3)] for core in range(2)
        )
        back_ground, edge, ground = merged_coefficients(low, high)
        link_ref[halves(step), :] = my_half(edge)
        low_ref[halves(step), :] = my_half(back_ground + edge)
        high_ref[halves(step), :] = my_half(ground + edge)


def merge_kernel(
    coef_ref,
    pair_ref,
    link_ref,
    low_ref,
    high_ref,
    from_low_ref,
    from_high_ref,
    pay_ref,
    scale_ref,
    p_ref,
    sem,
    *,
    copies,
):
    p_ref[16:24] = jnp.zeros((8, XC), jnp.float32)
    for step in range(2):
        rows = halves(step)
        own = high_ref[rows, :] + from_high_ref[rows, :]
        root = jnp.sqrt(own)
        own_inv = 1.0 / root
        last_inv = 1.0 / jnp.sqrt(from_low_ref[rows, :] + low_ref[rows, :])
        scale_ref[halves(2 * step), :] = own_inv
        scale_ref[halves(2 * step + 1), :] = last_inv
        p_ref[halves(3 * step), :] = link_ref[rows, :] * (own_inv * last_inv)
        if step == 0:
            scale_ref[halves(4), :] = root
            scale_ref[halves(5), :] = from_high_ref[rows, :]
    low, high = block_numbers(coef_ref, pair_ref, 0)
    side, back_side = merged_sides(low, high)
    p_ref[halves(1), :] = my_half(side) * scale_ref[halves(0), :]
    p_ref[halves(2), :] = my_half(back_side) * scale_ref[halves(1), :]
    low, high = wide_numbers(pair_ref)
    for q, number in enumerate(merged_coefficients(low, high) + merged_sides(low, high)):
        p_ref[16 + q : 17 + q] = my_half(number)
    spread(p_ref, pay_ref, sem, copies)


def later_merge_kernel(coef_ref, more_ref, scale_ref, pay_ref, p_ref, sem, *, copies):
    side, back_side = merged_sides(*block_numbers(coef_ref, more_ref, 1))
    p_ref[halves(0), :] = my_half(side) * scale_ref[halves(2), :]
    p_ref[halves(1), :] = my_half(back_side) * scale_ref[halves(3), :]
    spread(p_ref, pay_ref, sem, copies)


def unit_chain(count, link, side_of, put):
    half = count // 2
    gain, part = [None] * count, [None] * count
    diag_l = diag_r = None
    side_l, side_r = side_of(0), side_of(count - 1)
    for i in range(half - 1):
        j = count - 1 - i
        edge_l, edge_r = link(i + 1), link(j)
        if i == 0:
            gain[i], part[i], gain[j], part[j] = edge_l, side_l, edge_r, side_r
        else:
            inv_l, inv_r = 1.0 / diag_l, 1.0 / diag_r
            gain[i], part[i] = edge_l * inv_l, side_l * inv_l
            gain[j], part[j] = edge_r * inv_r, side_r * inv_r
        diag_l = 1.0 - edge_l * gain[i]
        side_l = side_of(i + 1) + edge_l * part[i]
        diag_r = 1.0 - edge_r * gain[j]
        side_r = side_of(j - 1) + edge_r * part[j]
    edge = link(half)
    if half == 1:
        diag_l = diag_r = jnp.ones_like(edge)
    inv = 1.0 / (diag_l * diag_r - edge * edge)
    low = (side_l * diag_r + edge * side_r) * inv
    high = (side_r * diag_l + edge * side_l) * inv
    put(half - 1, low)
    put(half, high)
    for i in range(half - 2, -1, -1):
        low = part[i] + gain[i] * low
        put(i, low)
        j = count - 1 - i
        high = part[j] + gain[j] * high
        put(j, high)


def chain_kernel(all_ref, scale_ref, out_ref, s_ref, w_ref, *, chips):
    s_ref[0] = jnp.zeros((HALF, XC), jnp.float32)
    w_ref[0] = jnp.zeros((1, XC), jnp.float32)

    def side_of(j):
        side = all_ref[j, halves(1), :]
        return side + all_ref[j + 1, halves(2), :] if j + 1 < chips else side

    def put(j, value):
        s_ref[j + 1] = value

    def put_wide(j, value):
        w_ref[j + 1] = value

    unit_chain(chips, lambda j: all_ref[j, halves(0), :], side_of, put)
    chain(chips, lambda j, q: all_ref[j, 16 + q : 17 + q, :], put_wide)
    me = lax.div(lax.axis_index("gz"), 2)
    then = jnp.minimum(me + 1, chips - 1)
    own = s_ref[me + 1] * scale_ref[halves(0), :]
    inflow = all_ref[then, halves(0), :] * s_ref[then + 1] + all_ref[then, halves(2), :]
    out_ref[8:16] = jnp.zeros((8, XC), jnp.float32)
    out_ref[halves(0), :] = s_ref[me] * scale_ref[halves(1), :]
    out_ref[halves(1), :] = own
    out_ref[halves(2), :] = scale_ref[halves(5), :] * own - scale_ref[halves(4), :] * inflow
    out_ref[12:13] = w_ref[me]
    out_ref[13:14] = w_ref[me + 1]


def later_chain_kernel(all_ref, more_ref, scale_ref, out_ref, s_ref, *, chips):
    s_ref[0] = jnp.zeros((HALF, XC), jnp.float32)

    def side_of(j):
        side = more_ref[j, halves(0), :]
        return side + more_ref[j + 1, halves(1), :] if j + 1 < chips else side

    def put(j, value):
        s_ref[j + 1] = value

    unit_chain(chips, lambda j: all_ref[j, halves(3), :], side_of, put)
    me = lax.div(lax.axis_index("gz"), 2)
    out_ref[halves(0), :] = s_ref[me] * scale_ref[halves(3), :]
    out_ref[halves(1), :] = s_ref[me + 1] * scale_ref[halves(2), :]


def ends_of(low, high, before, last):
    _, inv = node_between(low, high)
    node = (low[3] + high[4] + low[1] * before + high[1] * last) * inv
    upper = lax.rem(lax.axis_index("gz"), 2) == 1
    return jnp.where(upper, node, before), jnp.where(upper, last, node), node


def joined(res_ref, u_ref, count):
    for q in range(count):
        for core in range(2):
            u_ref[q, halves(core), :] = res_ref[core, halves(q), :]


def back_kernel(coef_ref, more_ref, res_ref, co_z_ref, side_z_ref, t_ref, u_ref):
    joined(res_ref, u_ref, 2)
    low, high = block_numbers(coef_ref, more_ref, 1)
    before, own, _ = ends_of(low, high, u_ref[0], u_ref[1])

    def place(i, value):
        t_ref[z_rows(i), :] = value

    substitute(ZC, before, own, co_z_ref, side_z_ref, place)


def turn_kernel(
    coef_ref,
    pair_ref,
    res_ref,
    co_z_ref,
    side_z_ref,
    co_wide_ref,
    side_wide_ref,
    z_entry_ref,
    c_ref,
    m_ref,
    x_ref,
    co_y_ref,
    link_ref,
    low_ref,
    high_ref,
    from_low_ref,
    from_high_ref,
    below_ref,
    above_ref,
    south_ref,
    north_ref,
    pay_ref,
    side_y_ref,
    fluxz_ref,
    cure_ref,
    scale_ref,
    u_ref,
    w_ref,
    t_ref,
    e_ref,
    k_ref,
    g_ref,
    fy_ref,
    r_ref,
    p_ref,
    sem,
    *,
    groups_y,
    groups_z,
):
    joined(res_ref, u_ref, 3)
    low, high = block_numbers(coef_ref, pair_ref, 0)
    last = u_ref[1]
    before, own, node = ends_of(low, high, u_ref[0], last)

    def place(i, value):
        t_ref[z_rows(i), :] = value

    substitute(ZC, before, own, co_z_ref, side_z_ref, place)
    me = lax.axis_index("gz")
    inside = high[0] * node + high[1] * (node - last) - high[4]
    current = jnp.where(lax.rem(me, 2) == 1, u_ref[2], inside)
    above = jnp.where(me == groups_z - 1, 0.0, own - current / z_entry_ref[...])

    for q in range(2):
        for core in range(2):
            w_ref[q, core : core + 1] = res_ref[core, 12 + q : 13 + q, :]
    low, high = wide_numbers(pair_ref)
    before_wide, own_wide, _ = ends_of(low, high, w_ref[0], w_ref[1])

    def place_wide(i, value):
        e_ref[2 * i : 2 * i + 2] = value

    substitute(ZC, before_wide, own_wide, co_wide_ref, side_wide_ref, place_wide)
    row = lax.axis_index("gy")
    south = jnp.where(row == 0, 0.0, e_ref[pl.ds(0, ZC, stride=2), :])
    north = jnp.where(row == groups_y - 1, 0.0, e_ref[pl.ds(1, ZC, stride=2), :])
    flow_rhs(
        t_ref,
        c_ref,
        m_ref,
        x_ref,
        (before, above),
        (south, north),
        (below_ref[2], above_ref[2]),
        (south_ref[2], north_ref[2]),
        (fluxz_ref, cure_ref),
        (k_ref, g_ref, fy_ref, r_ref),
    )
    side, back_side = reduce_sides(YC, lambda i: r_ref[y_rows(i), :], co_y_ref, side_y_ref)
    own_inv = 1.0 / jnp.sqrt(high_ref[...] + from_high_ref[...])
    last_inv = 1.0 / jnp.sqrt(from_low_ref[...] + low_ref[...])
    scale_ref[0] = own_inv
    scale_ref[1] = last_inv
    p_ref[0:ZC] = link_ref[...] * (own_inv * last_inv)
    p_ref[ZC : 2 * ZC] = side * own_inv
    p_ref[2 * ZC : 3 * ZC] = back_side * last_inv
    spread(p_ref, pay_ref, sem, groups_y)


def call(kernel, outs, scratch=(), spread_to=0, **static):
    out_specs = [pl.BlockSpec(memory_space=pltpu.VMEM)] * len(outs)
    shapes = [pltpu.VMEM(shape, jnp.float32) for shape in scratch]
    if spread_to:
        out_specs[0] = pl.BlockSpec(memory_space=pl.ANY)
        shapes.append(pltpu.SemaphoreType.DMA((spread_to,)))
    return pl.pallas_call(
        functools.partial(kernel, **static),
        out_shape=tuple(outs),
        out_specs=tuple(out_specs),
        scratch_shapes=shapes,
        compiler_params=pltpu.CompilerParams(vmem_limit_bytes=12 * 1024 * 1024),
        name=kernel.__name__,
    )


def body(warmth, cure, label):
    groups_z, groups_y = lax.axis_size("gz"), lax.axis_size("gy")
    chips = groups_z // 2
    up = {a: [(i, i + 1) for i in range(n - 1)] for a, n in (("gz", groups_z), ("gy", groups_y))}
    down = {a: [(j, i) for i, j in up[a]] for a in up}
    pairs = [[2 * i, 2 * i + 1] for i in range(chips)]
    same_core = [[2 * i + core for i in range(chips)] for core in range(2)]
    cells = (ROWS, XC)
    block = f32(*cells)

    zlo, zhi, ylo, yhi, t, c, m = pl.pallas_call(
        edges_kernel,
        out_shape=(
            f32(3, YC, XC),
            f32(3, YC, XC),
            f32(3, ZC, XC),
            f32(3, ZC, XC),
            block,
            block,
            jax.ShapeDtypeStruct(cells, jnp.int32),
        ),
        in_specs=[pl.BlockSpec(memory_space=pltpu.HBM)] * 3,
        scratch_shapes=[pltpu.SemaphoreType.DMA((3,))],
        compiler_params=pltpu.CompilerParams(vmem_limit_bytes=12 * 1024 * 1024),
        name="edges_kernel",
    )(*(pltpu.with_memory_space_constraint(a.reshape(cells), pltpu.HBM) for a in (warmth, cure, label)))
    z_halo = (lax.ppermute(zhi, "gz", up["gz"]), lax.ppermute(zlo, "gz", down["gz"]))
    y_halo = (lax.ppermute(yhi, "gy", up["gy"]), lax.ppermute(ylo, "gy", down["gy"]))

    def gather_y(pay):
        return lax.all_to_all(pay, "gy", 0, 0, tiled=True)

    def gather_z(pay):
        return lax.all_to_all(pay, "gz", 0, 0, tiled=True, axis_index_groups=same_core)

    def share(numbers):
        return lax.all_gather(numbers, "gz", axis_index_groups=pairs)

    sizes = dict(groups_y=groups_y, groups_z=groups_z)
    co_y, side_y = f32(3, YC - 1, ZC, XC), f32(YC - 1, ZC, XC)
    co_z, side_z = f32(3, ZC - 1, YC, XC), f32(ZC - 1, YC, XC)
    next_chip = [(i, i + 2) for i in range(groups_z - 2)]
    last_chip = [(j, i) for i, j in next_chip]
    x_shape = f32(2 * ROUNDS + 2, ROWS, XC)
    line = (groups_y + 1, ZC, XC)

    (x1,) = call(x_kernel, [x_shape])(c, m)
    pay, co_y1, side, fluxz, c1, y_entry = call(
        front_kernel,
        [f32(groups_y, 5 * ZC + 8, XC), co_y, side_y, block, block, f32(ZC, XC)],
        [cells] * 4 + [(5 * ZC + 8, XC)],
        spread_to=groups_y,
        groups=groups_y,
    )(t, c, m, x1, *z_halo, *y_halo)
    y_row = f32(ZC, XC)
    x2, co_z1, co_z2, numbers, z_entry, co_y2, link_y, low_y, high_y = call(
        ahead_kernel,
        [x_shape, co_z, co_z, f32(6 * YC, XC), f32(YC, XC), co_y, y_row, y_row, y_row],
        [cells] * 2,
        **sizes,
    )(c, c1, m, *z_halo, *y_halo)
    coef = share(numbers)
    link, low, high = call(links_kernel, [f32(YC, XC)] * 3)(coef)
    from_low = lax.ppermute(high, "gz", next_chip)
    from_high = lax.ppermute(low, "gz", last_chip)
    everyone = gather_y(pay)
    numbers, side, co_wide, side_wide = call(
        middle_kernel,
        [f32(4 * YC, XC), side_z, f32(3, ZC - 1, 2, XC), f32(ZC - 1, 2, XC)],
        [line, cells, (7, 40, XC)],
        **sizes,
    )(everyone, co_y1, side, fluxz, m, co_z1, y_entry, *y_halo)
    pair = share(numbers)
    pay, scale = call(
        merge_kernel,
        [f32(chips, 24, XC), f32(24, XC)],
        [(24, XC)],
        spread_to=chips,
        copies=chips,
    )(coef, pair, link, low, high, from_low, from_high)
    pay, send_low, send_high = lax.optimization_barrier((pay, low_y, high_y))
    column = gather_z(pay)
    from_south = lax.ppermute(send_high, "gy", up["gy"])
    from_north = lax.ppermute(send_low, "gy", down["gy"])
    half_line = (chips + 1, HALF, XC)
    (found,) = call(
        chain_kernel, [f32(16, XC)], [half_line, (chips + 1, 1, XC)], chips=chips
    )(column, scale)
    pay, side, fluxz, c2, scale_y = call(
        turn_kernel,
        [f32(groups_y, 3 * ZC, XC), side_y, block, block, f32(2, ZC, XC)],
        [(3, YC, XC), (2, 2, XC), cells, (2 * ZC, XC)] + [cells] * 4 + [(3 * ZC, XC)],
        spread_to=groups_y,
        **sizes,
    )(
        coef,
        pair,
        share(found),
        co_z1,
        side,
        co_wide,
        side_wide,
        z_entry,
        c1,
        m,
        x2,
        co_y2,
        link_y,
        low_y,
        high_y,
        from_south,
        from_north,
        *z_halo,
        *y_halo,
    )
    numbers, side = call(
        later_middle_kernel, [f32(2 * YC, XC), side_z], [line, cells], groups_y=groups_y
    )(gather_y(pay), scale_y, co_y2, side, fluxz, m, co_z2)
    more = share(numbers)
    (pay,) = call(
        later_merge_kernel, [f32(chips, YC, XC)], [(YC, XC)], spread_to=chips, copies=chips
    )(coef, more, scale)
    (found,) = call(later_chain_kernel, [f32(YC, XC)], [half_line], chips=chips)(
        column, gather_z(pay), scale
    )
    (t2,) = call(back_kernel, [block], [(2, YC, XC)])(coef, more, share(found), co_z2, side)
    return t2.reshape(warmth.shape), c2.reshape(cure.shape)


def solution(mesh):
    return jax.shard_map(
        body,
        mesh=mesh,
        in_specs=(P("gz", "gy", None),) * 3,
        out_specs=(P("gz", "gy", None),) * 2,
        check_vma=False,
    )
```
